128 devices in a mesh: section: 2 (over core), blk: 16 (over y, x), mp: 4 (over z).
Axes of the slice: x: 4, y: 4, z: 4, core: 2. Of those that a mesh axis runs over, the one named last changes fastest.
Arguments:
- patches: bfloat16 [256, 5120], P('section'), may hold values from -6 to 6
- merge_gain: float32 [1280], replicated, may hold values from 0.25 to 1.75
- merge_first: bfloat16 [5120, 5120], P(None, ('blk', 'mp')), may hold values from -0.078125 to 0.078125
- merge_second: bfloat16 [5120, 4096], P(('blk', 'mp')), may hold values from -0.078125 to 0.078125
- text_embeds: bfloat16 [4, 1024, 4096], P(None, 'blk', 'mp'), may hold values from -7 to 14
- positions: int32 [256], replicated, may hold values from 0 to 4095, as said below
- segments: int32 [4096], replicated, may hold values from 0 to 2, never falling along the last dimension, each value on 1 to 2048 neighbouring positions
- norm_gain: float32 [2, 4096], P('section'), may hold values from 0.25 to 1.75
- query_weight: bfloat16 [2, 4096, 4096], P('section', 'blk', 'mp'), may hold values from -1 to 1
- keyval_weight: bfloat16 [2, 4096, 4, 2, 128], P('section', 'blk', 'mp'), may hold values from -1 to 1
- out_weight: bfloat16 [2, 4096, 4096], P('section', 'mp', 'blk'), may hold values from -0.09375 to 0.09375
Outputs:
- hidden: bfloat16 [2, 4, 1024, 4096], P('section', None, 'blk', 'mp')
The draws below stay inside these ranges and needn't reach their ends.
Inputs may be any that keep to these rules, and one draw needn't show every extreme that they name: `positions`: distinct and increasing.
All inputs are finite; a program needn't handle non-finite values.
Results may differ from the reference program's by a relative error of at most 0.015.
Values may be sent and summed in bfloat16 or wider, within the bound.
No kernel may reach another device: no remote copies, remote signals or barrier semaphores. Data moves between devices by JAX's collectives and lax.ppermute only.
A program may use at most 128 MiB of HBM per device.

```python
import math
import jax
import jax.numpy as jnp
import numpy as np
from jax import lax

D = 4096
HEADS = 32
KV_HEADS = 4
HD = 128
PW = 1280
MB = 4
DOCS = 3
MH = 5120
BLOCK_LEN = 1024
SEQ = 4096
VIS = 256
LAYERS = 2
N_MP = 4


def draw_positions(key, part):
    shuffled = jax.random.permutation(jax.random.fold_in(key, 14), SEQ)
    return jnp.sort(shuffled[:VIS]).astype(jnp.int32)


def draw_text_embeds(key, part):
    noise_key = jax.random.fold_in(jax.random.fold_in(key, 13), 0)
    shape = (MB, BLOCK_LEN, D)
    values = jax.random.truncated_normal(noise_key, -6.0, 6.0, shape, jnp.float32)
    return values.astype(jnp.bfloat16)


def draw_query_weight(key, part):
    shape = (LAYERS, D, HEADS, HD)
    base_key = jax.random.fold_in(key, 11)
    values = jax.random.truncated_normal(base_key, -6.0, 6.0, shape, jnp.float32) * D ** (-0.5)
    return values.reshape(LAYERS, D, HEADS * HD).astype(jnp.bfloat16)


def draw_keyval_weight(key, part):
    shape = (LAYERS, D, KV_HEADS, 2, HD)
    base_key = jax.random.fold_in(key, 12)
    values = jax.random.truncated_normal(base_key, -6.0, 6.0, shape, jnp.float32) * D ** (-0.5)
    return values.astype(jnp.bfloat16)


def block_scale(rng, shape, cuts, low, top_value):
    def one(dim, parts):
        draws = jax.random.uniform(jax.random.fold_in(jax.random.fold_in(rng, 6), dim), (parts,), jnp.float32, low / len(cuts), top_value / len(cuts))
        return jnp.repeat(jnp.exp(draws), shape[dim] // parts).reshape((-1,) + (1,) * (len(shape) - dim - 1))

    gain = one(*cuts[0])
    for cut in cuts[1:]:
        gain = gain * one(*cut)
    return gain


def split_up(number_of, total, reach, lean):
    weights = [(1 << 20) // math.isqrt(standing ** lean) + 1 for standing in range(2, number_of + 1)]
    spare, given = total - reach - (number_of - 1), [1] * (number_of - 1)
    while spare > 0:
        candidates = [i for i in range(number_of - 1) if given[i] < reach]
        whole, remaining = sum([weights[i] for i in candidates]), spare
        for i in candidates:
            more = min(reach - given[i], max(1, remaining * weights[i] // whole), spare)
            given[i] = given[i] + more
            spare = spare - more
    return np.array([reach] + given)


def uneven_parts(key, count, total, limit, lean):
    if count == 2:
        one = jax.random.randint(key, (), max(1, total - limit), min(limit, total - 1) + 1)
        return jnp.stack([one, total - one])
    sizes = jnp.asarray(split_up(count, total, limit, lean), jnp.int32)
    pairs = (count - 1) // 2
    source_of, receiver = sizes[1:1 + 2 * pairs:2], sizes[2:2 + 2 * pairs:2]
    margin = jnp.minimum(source_of - 1, limit - receiver)
    moved = jax.random.randint(jax.random.fold_in(key, 1), (pairs,), 0, 1 << 20) % (margin + 1)
    sizes = sizes.at[1:1 + 2 * pairs:2].set(source_of - moved).at[2:2 + 2 * pairs:2].set(receiver + moved)
    return sizes[jax.random.permutation(jax.random.fold_in(key, 2), count)]


def scatter_about(key, shape, spread, most, cuts=(), held_as=jnp.bfloat16):
    result = jax.random.normal(key, shape, jnp.float32) * spread
    if len(cuts) > 0:
        result = block_scale(key, shape, cuts, -0.22, 0.18) * result
    return jnp.clip(result, min=-most, max=most).astype(held_as)


def setup_inputs(seed: int = 0) -> dict:
    arg_keys = jax.random.split(jax.random.key(seed), 12)
    return {
        "patches": scatter_about(arg_keys[0], (VIS, MH), 1.0, 6.0, ((0, 2),)),
        "merge_gain": jnp.clip(1.0 + 0.15 * jax.random.normal(arg_keys[1], (PW,), jnp.float32), 0.25, 1.75),
        "merge_first": scatter_about(arg_keys[2], (MH, MH), MH ** -0.5, 0.078125, ((1, 64),)),
        "merge_second": scatter_about(arg_keys[3], (MH, D), MH ** -0.5, 0.078125, ((0, 64),)),
        "text_embeds": draw_text_embeds(jax.random.fold_in(arg_keys[11], 71), 0),
        "positions": draw_positions(jax.random.fold_in(arg_keys[11], 71), 0),
        "segments": jnp.searchsorted(jnp.cumsum(uneven_parts(arg_keys[6], DOCS, SEQ, SEQ // 2, 1)), jnp.arange(SEQ), side="right").astype(jnp.int32),
        "norm_gain": jnp.clip(1.0 + 0.15 * jax.random.normal(arg_keys[7], (LAYERS, D), jnp.float32), 0.25, 1.75),
        "query_weight": draw_query_weight(jax.random.fold_in(arg_keys[11], 71), 0),
        "keyval_weight": draw_keyval_weight(jax.random.fold_in(arg_keys[11], 71), 0),
        "out_weight": scatter_about(arg_keys[10], (LAYERS, HEADS * HD, D), (HEADS * HD) ** -0.5, 0.09375, ((0, 2), (1, 4), (2, 16))),
    }


epsilon = 1e-06
rope_base = 1000000.0

def rope_tables(where_at, head_size):
    steps_half = jnp.arange(head_size // 2).astype(jnp.float32)
    inverse = jnp.exp(-jnp.log(rope_base) * 2.0 * steps_half / head_size)
    angles = where_at.astype(jnp.float32)[:, None] * inverse[None, :]
    return (jnp.cos(angles), jnp.sin(angles))

def rotate(values, cosine, sine):
    half = values.shape[-1] // 2
    first = values[..., :half]
    second = values[..., half:]
    cosine = cosine[:, None, :]
    sine = sine[:, None, :]
    return jnp.concatenate([first * cosine - second * sine, second * cosine + first * sine], axis=-1)

def merger(patches, merge_gain, merge_first, merge_second):
    count = patches.shape[0]
    width = merge_gain.shape[0]
    pieces = patches.astype(jnp.float32).reshape(count, -1, width)
    centered = pieces - lax.optimization_barrier(jnp.mean(pieces, axis=-1, keepdims=True))
    variance = lax.optimization_barrier(jnp.mean(centered * centered, axis=-1, keepdims=True))
    normed = (centered * lax.rsqrt(variance + epsilon) * merge_gain).reshape(count, -1).astype(jnp.bfloat16)
    inner = jax.nn.gelu(jnp.dot(normed, merge_first, preferred_element_type=jnp.float32), approximate=False).astype(jnp.bfloat16)
    return jnp.dot(inner, merge_second, preferred_element_type=jnp.float32).astype(jnp.bfloat16)

def reference(patches, merge_gain, merge_first, merge_second, text_embeds, positions, segments, norm_gain, query_weight, keyval_weight, out_weight):
    merged = merger(patches, merge_gain, merge_first, merge_second)
    state = text_embeds.reshape(SEQ, D)
    state = state.at[positions].set(merged)
    where_at = jnp.arange(SEQ).astype(jnp.int32)
    cosine, sine = rope_tables(where_at, HD)
    group = HEADS // KV_HEADS
    heads_group = HEADS // N_MP
    scale = 1.0 / HD ** 0.5
    results = []
    for layer_index in range(LAYERS):
        state_f = state.astype(jnp.float32)
        normx = (state_f * lax.rsqrt(lax.optimization_barrier(jnp.mean(state_f * state_f, axis=-1, keepdims=True)) + epsilon) * norm_gain[layer_index]).astype(jnp.bfloat16)
        query = jnp.dot(normx, query_weight[layer_index], preferred_element_type=jnp.float32).reshape(SEQ, HEADS, HD)
        query = rotate(query, cosine, sine).astype(jnp.bfloat16)
        keyval = jnp.dot(normx, keyval_weight[layer_index].reshape(D, -1), preferred_element_type=jnp.float32).reshape(SEQ, KV_HEADS, 2, HD)
        keys = rotate(keyval[:, :, 0, :], cosine, sine).astype(jnp.bfloat16)
        values = keyval[:, :, 1, :].astype(jnp.bfloat16)
        pieces_out = []
        for block_index in range(MB):
            lower = block_index * BLOCK_LEN
            upper = lower + BLOCK_LEN
            query_pos = where_at[lower:upper]
            allowed = (where_at[None, :upper] <= query_pos[:, None]) & (segments[None, :upper] == segments[lower:upper][:, None])
            head_pieces = []
            for kv_index in range(KV_HEADS):
                query_block = query[lower:upper, kv_index * group:(kv_index + 1) * group, :].astype(jnp.float32)
                key_block = keys[:upper, kv_index, :].astype(jnp.float32)
                value_block = values[:upper, kv_index, :].astype(jnp.float32)
                scores = jnp.einsum('qgd,sd->gqs', query_block, key_block) * scale
                scores = jnp.where(allowed[None], scores, -jnp.inf)
                top = lax.optimization_barrier(jnp.max(scores, axis=-1, keepdims=True))
                expo = jnp.exp(scores - top)
                probs = (expo / lax.optimization_barrier(jnp.sum(expo, axis=-1, keepdims=True))).astype(jnp.bfloat16)
                head_pieces.append(jnp.einsum('gqs,sd->qgd', probs.astype(jnp.float32), value_block))
            attended_block = jnp.concatenate(head_pieces, axis=1).reshape(BLOCK_LEN, HEADS * HD)
            pieces_out.append(attended_block.astype(jnp.bfloat16))
        attended = jnp.concatenate(pieces_out, axis=0)
        total = state_f
        for group_index in range(N_MP):
            cols = heads_group * HD
            term = jnp.dot(attended[:, group_index * cols:(group_index + 1) * cols], out_weight[layer_index][group_index * cols:(group_index + 1) * cols], preferred_element_type=jnp.float32).astype(jnp.bfloat16)
            term = lax.optimization_barrier(term)
            total = total + term.astype(jnp.float32)
        state = total.astype(jnp.bfloat16)
        results.append(state.reshape(MB, BLOCK_LEN, D))
    return jnp.stack(results)
```

```python
import jax
import jax.numpy as jnp
from jax import lax
from jax.sharding import PartitionSpec as P

epsilon = 1e-06
rope_base = 1000000.0
lane = 128


def moved(value, axis, by):
    size = lax.axis_size(axis)
    return lax.ppermute(value, axis, [(i, (i + by) % size) for i in range(size)])


def swapped(value):
    return lax.ppermute(value, "section", [(0, 1), (1, 0)])


def rope_tables(where_at, head_size):
    steps_half = jnp.arange(head_size // 2).astype(jnp.float32)
    inverse = jnp.exp(-jnp.log(rope_base) * 2.0 * steps_half / head_size)
    angles = where_at.astype(jnp.float32)[:, None] * inverse[None, :]
    return (jnp.cos(angles), jnp.sin(angles))


def rotate(values, cosine, sine):
    half = values.shape[-1] // 2
    first = values[..., :half]
    second = values[..., half:]
    return jnp.concatenate(
        [first * cosine - second * sine, second * cosine + first * sine], axis=-1
    )


def my_half(value, axis, section_index):
    shape = value.shape
    runs = shape[axis] // (2 * lane)
    split = value.reshape(shape[:axis] + (runs, 2, lane) + shape[axis + 1 :])
    index = [slice(None)] * split.ndim
    index[axis + 1] = 0
    even = split[tuple(index)]
    index[axis + 1] = 1
    odd = split[tuple(index)]
    picked = jnp.where(section_index == 0, even, odd)
    return picked.reshape(shape[:axis] + (runs * lane,) + shape[axis + 1 :])


def scatter_sum(term, model_index):
    size = lax.axis_size("mp")
    width = term.shape[1] // size

    def piece(by):
        return lax.dynamic_slice_in_dim(term, ((model_index + by) % size) * width, width, 1)

    total = piece(0)
    arrived = [moved(piece(by).astype(jnp.bfloat16), "mp", by) for by in (1, 3, 2)]
    for part in arrived:
        total = total + part.astype(jnp.float32)
    return total


def spread(value):
    size = lax.axis_size("blk")
    copies = jnp.broadcast_to(value[None], (size,) + value.shape)
    return lax.all_to_all(copies, "blk", 0, 0, tiled=True)


def local(
    patches,
    merge_gain,
    merge_first,
    merge_second,
    text_embeds,
    positions,
    segments,
    norm_gain,
    query_weight,
    keyval_weight,
    out_weight,
):
    count = patches.shape[0]
    width = merge_gain.shape[0]
    blocks, rows_here, slice_width = text_embeds.shape
    seq_len = segments.shape[0]
    block_len = seq_len // blocks
    section_index = lax.axis_index("section")
    cycle_index = lax.axis_index("blk")
    model_index = lax.axis_index("mp")
    n_mp = lax.axis_size("mp")
    n_blk = lax.axis_size("blk")
    first_core = section_index == 0
    head_size = keyval_weight.shape[4]
    rows = blocks * rows_here
    layers = 2

    query_own = query_weight[0]
    keyval_own = keyval_weight[0].reshape(keyval_weight.shape[1], 2 * head_size)
    out_own = out_weight[0]
    heads_half = query_own.shape[1] // 2
    weight_half = query_own.shape[0] // 2
    low = jnp.concatenate([query_own[:, :heads_half], keyval_own[:, :head_size]], axis=1)
    high = jnp.concatenate([query_own[:, heads_half:], keyval_own[:, head_size:]], axis=1)
    proj_keep = jnp.where(
        first_core,
        jnp.concatenate([low[:weight_half], high[:weight_half]], axis=1),
        jnp.concatenate([high[weight_half:], low[weight_half:]], axis=1),
    )
    proj_send = jnp.where(
        first_core,
        jnp.concatenate([high[weight_half:], low[weight_half:]], axis=1),
        jnp.concatenate([low[:weight_half], high[:weight_half]], axis=1),
    )
    out_half = out_own.shape[0] // 2
    cols_half = out_own.shape[1] // 2
    for_first = out_own[:, :cols_half]
    for_second = jnp.concatenate(
        [out_own[out_half:, cols_half:], out_own[:out_half, cols_half:]], axis=0
    )
    out_keep = jnp.where(first_core, for_first, for_second)
    out_send = jnp.where(first_core, for_second, for_first)
    proj_other = swapped(proj_send)
    out_other = swapped(out_send)
    proj_layers = [
        jnp.where(first_core, proj_keep, proj_other),
        jnp.where(first_core, proj_other, proj_keep),
    ]
    out_layers = [
        jnp.where(first_core, out_keep, out_other),
        jnp.where(first_core, out_other, out_keep),
    ]
    gain_half = norm_gain[0].reshape(-1, 2, lane)
    gain_keep = jnp.where(first_core, gain_half[:, 0], gain_half[:, 1])
    gain_send = jnp.where(first_core, gain_half[:, 1], gain_half[:, 0])
    gain_other = swapped(gain_send)
    gain_layers = [
        jnp.where(first_core, gain_keep, gain_other).reshape(n_mp, -1),
        jnp.where(first_core, gain_other, gain_keep).reshape(n_mp, -1),
    ]
    proj_full = []
    out_full = []
    for layer_index in range(layers):
        proj_full.append(lax.all_gather(proj_layers[layer_index], "blk", axis=0, tiled=True))
        out_full.append(lax.all_gather(out_layers[layer_index], "blk", axis=1, tiled=True))

    pieces = patches.astype(jnp.float32).reshape(count, -1, width)
    centered = pieces - jnp.mean(pieces, axis=-1, keepdims=True)
    variance = jnp.mean(centered * centered, axis=-1, keepdims=True)
    normed = (
        (centered * lax.rsqrt(variance + epsilon) * merge_gain)
        .reshape(count, -1)
        .astype(jnp.bfloat16)
    )
    inner = jax.nn.gelu(
        jnp.dot(normed, merge_first, preferred_element_type=jnp.float32), approximate=False
    ).astype(jnp.bfloat16)
    inner_other = swapped(inner)
    inner_all = jnp.concatenate(
        [
            jnp.where(first_core, inner, inner_other),
            jnp.where(first_core, inner_other, inner),
        ],
        axis=0,
    )
    second_half = my_half(merge_second, 1, section_index)
    partial_merge = jnp.dot(inner_all, second_half, preferred_element_type=jnp.float32)
    tokens = partial_merge.shape[0]
    merged_part = scatter_sum(partial_merge, model_index).astype(jnp.bfloat16)
    merged_terms = lax.all_to_all(
        merged_part.reshape(n_blk, tokens // n_blk, -1), "blk", 0, 0, tiled=True
    )
    merged_mine = jnp.sum(merged_terms.astype(jnp.float32), axis=0).astype(jnp.bfloat16)
    merged = spread(merged_mine).reshape(tokens, -1)

    row_where = (
        jnp.arange(blocks)[:, None] * block_len
        + cycle_index * rows_here
        + jnp.arange(rows_here)[None, :]
    ).reshape(-1)
    key_where = (
        jnp.arange(n_blk)[:, None, None] * rows_here
        + jnp.arange(blocks)[None, :, None] * block_len
        + jnp.arange(rows_here)[None, None, :]
    ).reshape(-1)
    key_segments = segments.reshape(blocks, n_blk, rows_here).transpose(1, 0, 2).reshape(-1)
    row_segments = lax.dynamic_index_in_dim(
        segments.reshape(blocks, n_blk, rows_here), cycle_index, 1, keepdims=False
    ).reshape(-1)
    allowed = (key_where[None, :] <= row_where[:, None]) & (
        key_segments[None, :] == row_segments[:, None]
    )

    is_visual = positions[None, :] == row_where[:, None]
    picked = jnp.dot(
        is_visual.astype(jnp.bfloat16), merged, preferred_element_type=jnp.float32
    ).astype(jnp.bfloat16)
    text_rows = my_half(text_embeds.reshape(rows, slice_width), 1, section_index)
    state = jnp.where(jnp.any(is_visual, axis=1)[:, None], picked, text_rows)

    cosine, sine = rope_tables(row_where, head_size)
    cosine = cosine[:, None, :]
    sine = sine[:, None, :]
    keyval_cosine = jnp.where(first_core, cosine, 1.0)
    keyval_sine = jnp.where(first_core, sine, 0.0)
    scale = 1.0 / head_size**0.5

    results = []
    for layer_index in range(layers):
        weight = proj_full[layer_index]
        gain = gain_layers[layer_index]
        parts = [state] + [moved(state, "mp", by) for by in (1, 3, 2)]
        squares = 0.0
        projected = 0.0
        for part, by in zip(parts, (0, 1, 3, 2)):
            source = (model_index + n_mp - by) % n_mp
            part_f = part.astype(jnp.float32)
            squares = squares + jnp.sum(part_f * part_f, axis=1, keepdims=True)
            scaled = (part_f * lax.dynamic_index_in_dim(gain, source, 0)).astype(jnp.bfloat16)
            depth = part.shape[1]
            projected = projected + jnp.dot(
                scaled,
                lax.dynamic_slice_in_dim(weight, source * depth, depth, 0),
                preferred_element_type=jnp.float32,
            )
        squares = squares + swapped(squares)
        columns = projected.shape[1] // 2
        total = projected[:, :columns] + swapped(projected[:, columns:])
        total = total * lax.rsqrt(squares / (2 * n_mp * slice_width // 2) + epsilon)
        query = total[:, :heads_half].reshape(rows, -1, head_size)
        query = rotate(query, cosine, sine).astype(jnp.bfloat16)
        keyval = total[:, None, heads_half:]
        keyval = rotate(keyval, keyval_cosine, keyval_sine).astype(jnp.bfloat16)[:, 0]
        gathered = spread(keyval).reshape(seq_len, head_size)
        gathered_other = swapped(gathered)
        keys = jnp.where(first_core, gathered, gathered_other)
        values = jnp.where(first_core, gathered_other, gathered)
        scores = jnp.einsum("qgd,sd->gqs", query, keys, preferred_element_type=jnp.float32) * scale
        scores = jnp.where(allowed[None], scores, -jnp.inf)
        top = jnp.max(scores, axis=-1, keepdims=True)
        expo = jnp.exp(scores - top)
        probs = (expo / jnp.sum(expo, axis=-1, keepdims=True)).astype(jnp.bfloat16)
        attended = jnp.einsum("gqs,sd->qgd", probs, values, preferred_element_type=jnp.float32)
        attended = attended.reshape(rows, -1).astype(jnp.bfloat16)
        attended_other = swapped(attended)
        out_here = out_full[layer_index]
        term = jnp.dot(attended, out_here[:out_half], preferred_element_type=jnp.float32)
        term = term + jnp.dot(
            attended_other, out_here[out_half:], preferred_element_type=jnp.float32
        )
        state = (state.astype(jnp.float32) + scatter_sum(term, model_index)).astype(jnp.bfloat16)
        results.append(state)

    keep = jnp.where(first_core, results[0], results[1])
    send = jnp.where(first_core, results[1], results[0])
    other = swapped(send)
    even = jnp.where(first_core, keep, other).reshape(rows, -1, 1, lane)
    odd = jnp.where(first_core, other, keep).reshape(rows, -1, 1, lane)
    return jnp.concatenate([even, odd], axis=2).reshape(1, blocks, rows_here, slice_width)


def solution(mesh):
    return jax.shard_map(
        local,
        mesh=mesh,
        in_specs=(
            P("section", None),
            P(),
            P(None, ("blk", "mp")),
            P(("blk", "mp"), None),
            P(None, "blk", "mp"),
            P(),
            P(),
            P("section", None),
            P("section", "blk", "mp"),
            P("section", "blk", "mp", None, None),
            P("section", "mp", "blk"),
        ),
        out_specs=P("section", None, "blk", "mp"),
        check_vma=False,
    )
```

```python
import functools
import math

import jax
import jax.numpy as jnp
from jax import lax
from jax.experimental import pallas as pl
from jax.experimental.pallas import tpu as pltpu
from jax.sharding import PartitionSpec as P

epsilon = 1e-06
rope_base = 1000000.0
lane = 128


def moved(value, axis, by):
    size = lax.axis_size(axis)
    return lax.ppermute(value, axis, [(i, (i + by) % size) for i in range(size)])


def swapped(value):
    return lax.ppermute(value, "section", [(0, 1), (1, 0)])


def rope_tables(where_at, head_size):
    steps_half = jnp.arange(head_size // 2).astype(jnp.float32)
    inverse = jnp.exp(-jnp.log(rope_base) * 2.0 * steps_half / head_size)
    angles = where_at.astype(jnp.float32)[:, None] * inverse[None, :]
    return (jnp.cos(angles), jnp.sin(angles))


def rotate(values, cosine, sine):
    half = values.shape[-1] // 2
    first = values[..., :half]
    second = values[..., half:]
    return jnp.concatenate(
        [first * cosine - second * sine, second * cosine + first * sine], axis=-1
    )


def my_half(value, axis, section_index):
    shape = value.shape
    runs = shape[axis] // (2 * lane)
    split = value.reshape(shape[:axis] + (runs, 2, lane) + shape[axis + 1 :])
    index = [slice(None)] * split.ndim
    index[axis + 1] = 0
    even = split[tuple(index)]
    index[axis + 1] = 1
    odd = split[tuple(index)]
    picked = jnp.where(section_index == 0, even, odd)
    return picked.reshape(shape[:axis] + (runs * lane,) + shape[axis + 1 :])


def scatter_sum(term, model_index):
    size = lax.axis_size("mp")
    width = term.shape[1] // size

    def piece(by):
        return lax.dynamic_slice_in_dim(term, ((model_index + by) % size) * width, width, 1)

    total = piece(0)
    arrived = [moved(piece(by).astype(jnp.bfloat16), "mp", by) for by in (1, 3, 2)]
    for part in arrived:
        total = total + part.astype(jnp.float32)
    return total


def spread(value):
    size = lax.axis_size("blk")
    copies = jnp.broadcast_to(value[None], (size,) + value.shape)
    return lax.all_to_all(copies, "blk", 0, 0, tiled=True)


def attention_kernel(scalars, query_ref, mine_ref, other_ref, out_ref, *, chunk_runs):
    runs, blocks, run, head_size = mine_ref.shape
    heads = query_ref.shape[1] // head_size
    rows = heads * run
    chunk = chunk_runs * run
    per_block = runs // chunk_runs
    block_len = runs * run
    start_one, start_two, cycle, section = scalars[0], scalars[1], scalars[2], scalars[3]
    factor = 1.0 / head_size**0.5 * math.log2(math.e)

    def stripes(key_ref, value_ref):
        def stripe(block, carry):
            row_from = pl.multiple_of(block * run, run)
            first = block * block_len + cycle * run
            here = query_ref[pl.ds(row_from, run), :]
            stacked = jnp.concatenate(
                [here[:, h * head_size : (h + 1) * head_size] for h in range(heads)], axis=0
            )
            row_at = lax.broadcasted_iota(jnp.int32, (rows, 1), 0) % run + first
            row_start = jnp.where(
                row_at >= start_two, start_two, jnp.where(row_at >= start_one, start_one, 0)
            )
            stripe_start = jnp.where(
                first >= start_two, start_two, jnp.where(first >= start_one, start_one, 0)
            )

            def step(index, state):
                top, total, mixed = state
                in_block = index // per_block
                from_run = (index % per_block) * chunk_runs
                key = key_ref[pl.ds(from_run, chunk_runs), in_block].reshape(chunk, head_size)
                value = value_ref[pl.ds(from_run, chunk_runs), in_block].reshape(chunk, head_size)
                scores = lax.dot_general(
                    stacked, key, (((1,), (1,)), ((), ())), preferred_element_type=jnp.float32
                )
                key_at = lax.broadcasted_iota(jnp.int32, (1, chunk), 1) + index * chunk
                allowed = (key_at <= row_at) & (key_at >= row_start)
                scores = jnp.where(allowed, scores * factor, -1e30)
                new_top = jnp.maximum(top, jnp.max(scores, axis=1, keepdims=True))
                fade = jnp.exp2(top - new_top)
                weights = jnp.exp2(scores - new_top)
                total = total * fade + jnp.sum(weights, axis=1, keepdims=True)
                mixed = mixed * fade + jnp.dot(
                    weights.astype(jnp.bfloat16), value, preferred_element_type=jnp.float32
                )
                return new_top, total, mixed

            state = (
                jnp.full((rows, 1), -1e30, jnp.float32),
                jnp.zeros((rows, 1), jnp.float32),
                jnp.zeros((rows, head_size), jnp.float32),
            )
            _, total, mixed = lax.fori_loop(
                stripe_start // chunk, (first + run - 1) // chunk + 1, step, state
            )
            result = (mixed / total).astype(out_ref.dtype)
            for h in range(heads):
                out_ref[pl.ds(row_from, run), h * head_size : (h + 1) * head_size] = result[
                    h * run : (h + 1) * run
                ]
            return carry

        lax.fori_loop(0, blocks, stripe, 0)

    @pl.when(section == 0)
    def _():
        stripes(mine_ref, other_ref)

    @pl.when(section != 0)
    def _():
        stripes(other_ref, mine_ref)


def attention(scalars, query, mine, other):
    whole = pl.BlockSpec(memory_space=pltpu.VMEM)
    return pl.pallas_call(
        functools.partial(attention_kernel, chunk_runs=mine.shape[0] // 2),
        out_shape=jax.ShapeDtypeStruct(query.shape, query.dtype),
        in_specs=[pl.BlockSpec(memory_space=pltpu.SMEM), whole, whole, whole],
        out_specs=whole,
        cost_estimate=pl.CostEstimate(
            flops=4 * query.size * mine.size // query.shape[1] // 4,
            bytes_accessed=2 * (2 * query.size + 2 * mine.size),
            transcendentals=0,
        ),
        name="attention",
    )(scalars, query, mine, other)


def local(
    patches,
    merge_gain,
    merge_first,
    merge_second,
    text_embeds,
    positions,
    segments,
    norm_gain,
    query_weight,
    keyval_weight,
    out_weight,
):
    count = patches.shape[0]
    width = merge_gain.shape[0]
    blocks, rows_here, slice_width = text_embeds.shape
    seq_len = segments.shape[0]
    block_len = seq_len // blocks
    section_index = lax.axis_index("section")
    cycle_index = lax.axis_index("blk")
    model_index = lax.axis_index("mp")
    n_mp = lax.axis_size("mp")
    n_blk = lax.axis_size("blk")
    first_core = section_index == 0
    head_size = keyval_weight.shape[4]
    rows = blocks * rows_here
    layers = 2

    query_own = query_weight[0]
    keyval_own = keyval_weight[0].reshape(keyval_weight.shape[1], 2 * head_size)
    out_own = out_weight[0]
    heads_half = query_own.shape[1] // 2
    weight_half = query_own.shape[0] // 2
    proj_width = query_own.shape[1] + 2 * head_size

    def packed(core):
        keep_rows = slice(core * weight_half, (core + 1) * weight_half)
        query_rows, keyval_rows = query_own[keep_rows], keyval_own[keep_rows]
        out_rows = out_own[:, keep_rows].T
        parts = []
        for half in (core, 1 - core):
            parts.append(query_rows[:, half * heads_half : (half + 1) * heads_half])
            parts.append(keyval_rows[:, half * head_size : (half + 1) * head_size])
        for half in (core, 1 - core):
            parts.append(out_rows[:, half * heads_half : (half + 1) * heads_half])
        return jnp.concatenate(parts, axis=1)

    for_first, for_second = packed(0), packed(1)
    weight_keep = jnp.where(first_core, for_first, for_second)
    weight_other = swapped(jnp.where(first_core, for_second, for_first))
    weight_layers = [
        jnp.where(first_core, weight_keep, weight_other),
        jnp.where(first_core, weight_other, weight_keep),
    ]
    gain_half = norm_gain[0].reshape(-1, 2, lane)
    gain_keep = jnp.where(first_core, gain_half[:, 0], gain_half[:, 1])
    gain_send = jnp.where(first_core, gain_half[:, 1], gain_half[:, 0])
    gain_other = swapped(gain_send)
    gain_layers = [
        jnp.where(first_core, gain_keep, gain_other).reshape(n_mp, -1),
        jnp.where(first_core, gain_other, gain_keep).reshape(n_mp, -1),
    ]
    weight_full = [
        lax.all_gather(weight_layers[layer_index], "blk", axis=0, tiled=True)
        for layer_index in range(layers)
    ]

    pieces = patches.astype(jnp.float32).reshape(count, -1, width)
    centered = pieces - jnp.mean(pieces, axis=-1, keepdims=True)
    variance = jnp.mean(centered * centered, axis=-1, keepdims=True)
    normed = (
        (centered * lax.rsqrt(variance + epsilon) * merge_gain)
        .reshape(count, -1)
        .astype(jnp.bfloat16)
    )
    inner = jax.nn.gelu(
        jnp.dot(normed, merge_first, preferred_element_type=jnp.float32), approximate=False
    ).astype(jnp.bfloat16)
    inner_other = swapped(inner)
    inner_all = jnp.concatenate(
        [
            jnp.where(first_core, inner, inner_other),
            jnp.where(first_core, inner_other, inner),
        ],
        axis=0,
    )
    second_half = my_half(merge_second, 1, section_index)
    partial_merge = jnp.dot(inner_all, second_half, preferred_element_type=jnp.float32)
    tokens = partial_merge.shape[0]
    merged_part = scatter_sum(partial_merge, model_index).astype(jnp.bfloat16)
    merged_terms = lax.all_to_all(
        merged_part.reshape(n_blk, tokens // n_blk, -1), "blk", 0, 0, tiled=True
    )
    merged_mine = jnp.sum(merged_terms.astype(jnp.float32), axis=0).astype(jnp.bfloat16)
    merged = spread(merged_mine).reshape(tokens, -1)

    row_where = (
        jnp.arange(blocks)[:, None] * block_len
        + cycle_index * rows_here
        + jnp.arange(rows_here)[None, :]
    ).reshape(-1)
    starts = jnp.stack([jnp.sum(segments < 1), jnp.sum(segments < 2)])
    scalars = jnp.concatenate([starts, jnp.stack([cycle_index, section_index])]).astype(jnp.int32)

    is_visual = positions[None, :] == row_where[:, None]
    picked = jnp.dot(
        is_visual.astype(jnp.bfloat16), merged, preferred_element_type=jnp.float32
    ).astype(jnp.bfloat16)
    text_rows = my_half(text_embeds.reshape(rows, slice_width), 1, section_index)
    state = jnp.where(jnp.any(is_visual, axis=1)[:, None], picked, text_rows)

    cosine, sine = rope_tables(row_where, head_size)
    cosine = cosine[:, None, :]
    sine = sine[:, None, :]
    keyval_cosine = jnp.where(first_core, cosine, 1.0)
    keyval_sine = jnp.where(first_core, sine, 0.0)

    results = []
    for layer_index in range(layers):
        weight = weight_full[layer_index]
        gain = gain_layers[layer_index]
        parts = [state] + [moved(state, "mp", by) for by in (1, 3, 2)]
        squares = 0.0
        projected = 0.0
        for part, by in zip(parts, (0, 1, 3, 2)):
            source = (model_index + n_mp - by) % n_mp
            part_f = part.astype(jnp.float32)
            squares = squares + jnp.sum(part_f * part_f, axis=1, keepdims=True)
            scaled = (part_f * lax.dynamic_index_in_dim(gain, source, 0)).astype(jnp.bfloat16)
            depth = part.shape[1]
            projected = projected + jnp.dot(
                scaled,
                lax.dynamic_slice(weight, (source * depth, 0), (depth, proj_width)),
                preferred_element_type=jnp.float32,
            )
        squares = squares + swapped(squares)
        columns = projected.shape[1] // 2
        total = projected[:, :columns] + swapped(projected[:, columns:])
        total = total * lax.rsqrt(squares / (2 * n_mp * slice_width // 2) + epsilon)
        query = total[:, :heads_half].reshape(rows, -1, head_size)
        query = rotate(query, cosine, sine).astype(jnp.bfloat16).reshape(rows, heads_half)
        keyval = total[:, None, heads_half:]
        keyval = rotate(keyval, keyval_cosine, keyval_sine).astype(jnp.bfloat16)[:, 0]
        gathered = spread(keyval).reshape(n_blk, blocks, rows_here, head_size)
        attended = attention(scalars, query, gathered, swapped(gathered))
        attended_other = swapped(attended)
        term = jnp.einsum(
            "pk,nk->pn",
            attended,
            weight[:, proj_width : proj_width + heads_half],
            preferred_element_type=jnp.float32,
        )
        term = term + jnp.einsum(
            "pk,nk->pn",
            attended_other,
            weight[:, proj_width + heads_half :],
            preferred_element_type=jnp.float32,
        )
        state = (state.astype(jnp.float32) + scatter_sum(term, model_index)).astype(jnp.bfloat16)
        results.append(state)

    keep = jnp.where(first_core, results[0], results[1])
    send = jnp.where(first_core, results[1], results[0])
    other = swapped(send)
    even = jnp.where(first_core, keep, other).reshape(rows, -1, 1, lane)
    odd = jnp.where(first_core, other, keep).reshape(rows, -1, 1, lane)
    return jnp.concatenate([even, odd], axis=2).reshape(1, blocks, rows_here, slice_width)


def solution(mesh):
    return jax.shard_map(
        local,
        mesh=mesh,
        in_specs=(
            P("section", None),
            P(),
            P(None, ("blk", "mp")),
            P(("blk", "mp"), None),
            P(None, "blk", "mp"),
            P(),
            P(),
            P("section", None),
            P("section", "blk", "mp"),
            P("section", "blk", "mp", None, None),
            P("section", "mp", "blk"),
        ),
        out_specs=P("section", None, "blk", "mp"),
        check_vma=False,
    )
```

```python
import functools
import math

import jax
import jax.numpy as jnp
from jax import lax
from jax.experimental import pallas as pl
from jax.experimental.pallas import tpu as pltpu
from jax.sharding import PartitionSpec as P

epsilon = 1e-06
rope_base = 1000000.0
lane = 128


def moved(value, axis, by):
    size = lax.axis_size(axis)
    return lax.ppermute(value, axis, [(i, (i + by) % size) for i in range(size)])


def swapped(value):
    return lax.ppermute(value, "section", [(0, 1), (1, 0)])


def rope_tables(where_at, head_size):
    steps_half = jnp.arange(head_size // 2).astype(jnp.float32)
    inverse = jnp.exp(-jnp.log(rope_base) * 2.0 * steps_half / head_size)
    angles = where_at.astype(jnp.float32)[:, None] * inverse[None, :]
    return (jnp.cos(angles), jnp.sin(angles))


def rotate(values, cosine, sine):
    half = values.shape[-1] // 2
    first = values[..., :half]
    second = values[..., half:]
    return jnp.concatenate(
        [first * cosine - second * sine, second * cosine + first * sine], axis=-1
    )


def my_half(value, axis, section_index):
    shape = value.shape
    runs = shape[axis] // (2 * lane)
    split = value.reshape(shape[:axis] + (runs, 2, lane) + shape[axis + 1 :])
    index = [slice(None)] * split.ndim
    index[axis + 1] = 0
    even = split[tuple(index)]
    index[axis + 1] = 1
    odd = split[tuple(index)]
    picked = jnp.where(section_index == 0, even, odd)
    return picked.reshape(shape[:axis] + (runs * lane,) + shape[axis + 1 :])


def spread(value):
    size = lax.axis_size("blk")
    copies = jnp.broadcast_to(value[None], (size,) + value.shape)
    return lax.all_to_all(copies, "blk", 0, 0, tiled=True)


def attention_kernel(scalars, query_ref, mine_ref, other_ref, out_ref, *, chunk_runs):
    runs, blocks, run, head_size = mine_ref.shape
    heads = query_ref.shape[1] // head_size
    rows = heads * run
    chunk = chunk_runs * run
    per_block = runs // chunk_runs
    block_len = runs * run
    start_one, start_two, cycle, section = scalars[0], scalars[1], scalars[2], scalars[3]
    factor = 1.0 / head_size**0.5 * math.log2(math.e)

    def stripes(key_ref, value_ref):
        def stripe(block, carry):
            row_from = pl.multiple_of(block * run, run)
            first = block * block_len + cycle * run
            here = query_ref[pl.ds(row_from, run), :]
            stacked = jnp.concatenate(
                [here[:, h * head_size : (h + 1) * head_size] for h in range(heads)], axis=0
            )
            row_at = lax.broadcasted_iota(jnp.int32, (rows, 1), 0) % run + first
            row_start = jnp.where(
                row_at >= start_two, start_two, jnp.where(row_at >= start_one, start_one, 0)
            )
            stripe_start = jnp.where(
                first >= start_two, start_two, jnp.where(first >= start_one, start_one, 0)
            )

            def step(index, state):
                top, total, mixed = state
                in_block = index // per_block
                from_run = (index % per_block) * chunk_runs
                key = key_ref[pl.ds(from_run, chunk_runs), in_block].reshape(chunk, head_size)
                value = value_ref[pl.ds(from_run, chunk_runs), in_block].reshape(chunk, head_size)
                scores = lax.dot_general(
                    stacked, key, (((1,), (1,)), ((), ())), preferred_element_type=jnp.float32
                )
                key_at = lax.broadcasted_iota(jnp.int32, (1, chunk), 1) + index * chunk
                allowed = (key_at <= row_at) & (key_at >= row_start)
                scores = jnp.where(allowed, scores * factor, -1e30)
                new_top = jnp.maximum(top, jnp.max(scores, axis=1, keepdims=True))
                fade = jnp.exp2(top - new_top)
                weights = jnp.exp2(scores - new_top)
                total = total * fade + jnp.sum(weights, axis=1, keepdims=True)
                mixed = mixed * fade + jnp.dot(
                    weights.astype(jnp.bfloat16), value, preferred_element_type=jnp.float32
                )
                return new_top, total, mixed

            state = (
                jnp.full((rows, 1), -1e30, jnp.float32),
                jnp.zeros((rows, 1), jnp.float32),
                jnp.zeros((rows, head_size), jnp.float32),
            )
            _, total, mixed = lax.fori_loop(
                stripe_start // chunk, (first + run - 1) // chunk + 1, step, state
            )
            result = (mixed / total).astype(out_ref.dtype)
            for h in range(heads):
                out_ref[pl.ds(row_from, run), h * head_size : (h + 1) * head_size] = result[
                    h * run : (h + 1) * run
                ]
            return carry

        lax.fori_loop(0, blocks, stripe, 0)

    @pl.when(section == 0)
    def _():
        stripes(mine_ref, other_ref)

    @pl.when(section != 0)
    def _():
        stripes(other_ref, mine_ref)


def attention(scalars, query, mine, other):
    whole = pl.BlockSpec(memory_space=pltpu.VMEM)
    return pl.pallas_call(
        functools.partial(attention_kernel, chunk_runs=mine.shape[0] // 2),
        out_shape=jax.ShapeDtypeStruct(query.shape, query.dtype),
        in_specs=[pl.BlockSpec(memory_space=pltpu.SMEM), whole, whole, whole],
        out_specs=whole,
        cost_estimate=pl.CostEstimate(
            flops=4 * query.size * mine.size // query.shape[1] // 4,
            bytes_accessed=2 * (2 * query.size + 2 * mine.size),
            transcendentals=0,
        ),
        name="attention",
    )(scalars, query, mine, other)


def merger_kernel(patches_ref, gain_ref, weight_ref, out_ref):
    width = gain_ref.shape[1]
    total = jnp.zeros(out_ref.shape, jnp.float32)
    for at in range(0, patches_ref.shape[1], width):
        piece = patches_ref[:, at : at + width].astype(jnp.float32)
        centered = piece - jnp.mean(piece, axis=1, keepdims=True)
        variance = jnp.mean(centered * centered, axis=1, keepdims=True)
        normed = (centered * lax.rsqrt(variance + epsilon) * gain_ref[...]).astype(jnp.bfloat16)
        total = total + jnp.dot(
            normed, weight_ref[at : at + width, :], preferred_element_type=jnp.float32
        )
    out_ref[...] = (0.5 * total * (1.0 + lax.erf(total * math.sqrt(0.5)))).astype(out_ref.dtype)


def merger_inner(patches, merge_gain, merge_first):
    whole = pl.BlockSpec(memory_space=pltpu.VMEM)
    rows, units = patches.shape[0], merge_first.shape[1]
    return pl.pallas_call(
        merger_kernel,
        out_shape=jax.ShapeDtypeStruct((rows, units), jnp.bfloat16),
        in_specs=[whole, whole, whole],
        out_specs=whole,
        cost_estimate=pl.CostEstimate(
            flops=2 * rows * merge_first.size,
            bytes_accessed=2 * (patches.size + merge_first.size),
            transcendentals=0,
        ),
        name="merger_inner",
    )(patches, merge_gain.reshape(1, -1), merge_first)


def project_in_kernel(
    place, own_ref, from_one, from_two, from_three, gain_ref, weight_ref, kept_ref, sent_ref, rows_ref
):
    step = pl.program_id(0)
    count = pl.num_programs(0)
    pieces, _, depth = gain_ref.shape
    columns = weight_ref.shape[1]
    queries = (count - 1) * columns // 2

    @pl.when(step == 0)
    def _():
        squares = jnp.zeros((own_ref.shape[0], 1), jnp.float32)
        for by, part_ref in enumerate((own_ref, from_one, from_two, from_three)):
            source = (place[0] + pieces - by) % pieces
            part = part_ref[...].astype(jnp.float32)
            squares = squares + jnp.sum(part * part, axis=1, keepdims=True)
            rows_ref[source] = (part * gain_ref[source]).astype(jnp.bfloat16)
        spread_squares = jnp.broadcast_to(squares, (squares.shape[0], lane))
        kept_ref[:, queries + lane :] = spread_squares
        sent_ref[:, queries + lane :] = spread_squares

    result = jnp.dot(rows_ref[0], weight_ref[:depth, :], preferred_element_type=jnp.float32)
    for piece in range(1, pieces):
        result = result + jnp.dot(
            rows_ref[piece],
            weight_ref[piece * depth : (piece + 1) * depth, :],
            preferred_element_type=jnp.float32,
        )

    for block in range((5 - 1) // 2):

        @pl.when(step == block)
        def _():
            kept_ref[:, block * columns : (block + 1) * columns] = result

        @pl.when(step == block + (5 - 1) // 2)
        def _():
            sent_ref[:, block * columns : (block + 1) * columns] = result

    @pl.when(step == count - 1)
    def _():
        kept_ref[:, queries : queries + lane] = result[:, :lane]
        sent_ref[:, queries : queries + lane] = result[:, lane:]


def project_in(place, parts, gain, weight):
    rows, depth = parts[0].shape
    columns = 2 * lane
    skipped = 2 * depth // columns
    steps = weight.shape[1] // columns - skipped
    assert steps == 5
    out = jax.ShapeDtypeStruct((rows, (steps - 1) * columns // 2 + 2 * lane), jnp.float32)
    part_spec = pl.BlockSpec((rows, depth), lambda step, place: (0, 0))
    out_spec = pl.BlockSpec(out.shape, lambda step, place: (0, 0))
    return pl.pallas_call(
        project_in_kernel,
        out_shape=(out, out),
        grid_spec=pltpu.PrefetchScalarGridSpec(
            num_scalar_prefetch=1,
            grid=(steps,),
            in_specs=[part_spec] * 4
            + [
                pl.BlockSpec(gain.shape, lambda step, place: (0, 0, 0)),
                pl.BlockSpec((weight.shape[0], columns), lambda step, place: (0, step + skipped)),
            ],
            out_specs=[out_spec, out_spec],
            scratch_shapes=[pltpu.VMEM((len(parts), rows, depth), jnp.bfloat16)],
        ),
        cost_estimate=pl.CostEstimate(
            flops=2 * rows * weight.shape[0] * steps * columns,
            bytes_accessed=2 * weight.shape[0] * steps * columns + 8 * rows * out.shape[1],
            transcendentals=0,
        ),
        name="project_in",
    )(place.reshape(1), *parts, gain, weight)


def project_out_kernel(place, mine_ref, other_ref, weight_ref, own_ref, one_ref, two_ref, three_ref):
    half = mine_ref.shape[1]
    over_last = (((1,), (1,)), ((), ()))
    result = lax.dot_general(
        mine_ref[...], weight_ref[:, :half], over_last, preferred_element_type=jnp.float32
    ) + lax.dot_general(
        other_ref[...], weight_ref[:, half:], over_last, preferred_element_type=jnp.float32
    )
    for by, out_ref in enumerate((own_ref, one_ref, two_ref, three_ref)):

        @pl.when(pl.program_id(0) == by)
        def _():
            out_ref[...] = result.astype(out_ref.dtype)


def project_out(place, mine, other, weight):
    rows, half = mine.shape
    pieces = lax.axis_size("mp")
    depth = weight.shape[0] // pieces
    shape = (rows, depth)
    part_spec = pl.BlockSpec((rows, half), lambda step, place: (0, 0))
    out_spec = pl.BlockSpec(shape, lambda step, place: (0, 0))
    return pl.pallas_call(
        project_out_kernel,
        out_shape=[jax.ShapeDtypeStruct(shape, jnp.float32)]
        + [jax.ShapeDtypeStruct(shape, jnp.bfloat16)] * (pieces - 1),
        grid_spec=pltpu.PrefetchScalarGridSpec(
            num_scalar_prefetch=1,
            grid=(pieces,),
            in_specs=[
                part_spec,
                part_spec,
                pl.BlockSpec(
                    (depth, 2 * half), lambda step, place: ((place[0] + step) % pieces, 0)
                ),
            ],
            out_specs=[out_spec] * pieces,
        ),
        cost_estimate=pl.CostEstimate(
            flops=4 * rows * half * weight.shape[0],
            bytes_accessed=4 * half * weight.shape[0] + 2 * rows * weight.shape[0],
            transcendentals=0,
        ),
        name="project_out",
    )(place.reshape(1), mine, other, weight)


def local(
    patches,
    merge_gain,
    merge_first,
    merge_second,
    text_embeds,
    positions,
    segments,
    norm_gain,
    query_weight,
    keyval_weight,
    out_weight,
):
    count = patches.shape[0]
    width = merge_gain.shape[0]
    blocks, rows_here, slice_width = text_embeds.shape
    seq_len = segments.shape[0]
    block_len = seq_len // blocks
    section_index = lax.axis_index("section")
    cycle_index = lax.axis_index("blk")
    model_index = lax.axis_index("mp")
    n_mp = lax.axis_size("mp")
    n_blk = lax.axis_size("blk")
    first_core = section_index == 0
    head_size = keyval_weight.shape[4]
    rows = blocks * rows_here
    layers = 2

    query_own = query_weight[0]
    keyval_own = keyval_weight[0].reshape(keyval_weight.shape[1], 2 * head_size)
    out_own = out_weight[0]
    heads_half = query_own.shape[1] // 2
    weight_half = query_own.shape[0] // 2

    def packed(core):
        keep_rows = slice(core * weight_half, (core + 1) * weight_half)
        query_rows, keyval_rows = query_own[keep_rows], keyval_own[keep_rows]
        out_rows = out_own[:, keep_rows].T
        halves = (core, 1 - core)
        parts = [out_rows[:, half * heads_half : (half + 1) * heads_half] for half in halves]
        parts += [query_rows[:, half * heads_half : (half + 1) * heads_half] for half in halves]
        parts += [keyval_rows[:, half * head_size : (half + 1) * head_size] for half in halves]
        return jnp.concatenate(parts, axis=1)

    for_first, for_second = packed(0), packed(1)
    weight_keep = jnp.where(first_core, for_first, for_second)
    weight_other = swapped(jnp.where(first_core, for_second, for_first))
    weight_layers = [
        jnp.where(first_core, weight_keep, weight_other),
        jnp.where(first_core, weight_other, weight_keep),
    ]
    gain_half = norm_gain[0].reshape(-1, 2, lane)
    gain_keep = jnp.where(first_core, gain_half[:, 0], gain_half[:, 1])
    gain_send = jnp.where(first_core, gain_half[:, 1], gain_half[:, 0])
    gain_other = swapped(gain_send)
    gain_layers = [
        jnp.where(first_core, gain_keep, gain_other).reshape(n_mp, 1, -1),
        jnp.where(first_core, gain_other, gain_keep).reshape(n_mp, 1, -1),
    ]
    weight_full = [
        lax.all_gather(weight_layers[layer_index], "blk", axis=0, tiled=True)
        for layer_index in range(layers)
    ]

    inner = merger_inner(patches, merge_gain, merge_first)
    inner_other = swapped(inner)
    inner_all = jnp.concatenate(
        [
            jnp.where(first_core, inner, inner_other),
            jnp.where(first_core, inner_other, inner),
        ],
        axis=0,
    )
    second_half = my_half(merge_second, 1, section_index)
    partial_merge = jnp.dot(inner_all, second_half, preferred_element_type=jnp.float32)
    tokens = partial_merge.shape[0]
    share = tokens // n_blk
    merged_terms = lax.all_to_all(
        partial_merge.astype(jnp.bfloat16)
        .reshape(n_blk, share, n_mp, -1)
        .transpose(0, 2, 1, 3)
        .reshape(n_blk * n_mp, share, -1),
        ("blk", "mp"),
        0,
        0,
        tiled=True,
    )
    merged_mine = jnp.sum(merged_terms.astype(jnp.float32), axis=0).astype(jnp.bfloat16)
    merged = spread(merged_mine).reshape(tokens, -1)

    row_where = (
        jnp.arange(blocks)[:, None] * block_len
        + cycle_index * rows_here
        + jnp.arange(rows_here)[None, :]
    ).reshape(-1)
    starts = jnp.stack([jnp.sum(segments < 1), jnp.sum(segments < 2)])
    scalars = jnp.concatenate([starts, jnp.stack([cycle_index, section_index])]).astype(jnp.int32)

    is_visual = positions[None, :] == row_where[:, None]
    picked = jnp.dot(
        is_visual.astype(jnp.bfloat16), merged, preferred_element_type=jnp.float32
    ).astype(jnp.bfloat16)
    text_rows = my_half(text_embeds.reshape(rows, slice_width), 1, section_index)
    state = jnp.where(jnp.any(is_visual, axis=1)[:, None], picked, text_rows)

    cosine, sine = rope_tables(row_where, head_size)
    cosine = cosine[:, None, :]
    sine = sine[:, None, :]
    keyval_cosine = jnp.where(first_core, cosine, 1.0)
    keyval_sine = jnp.where(first_core, sine, 0.0)

    results = []
    for layer_index in range(layers):
        weight = weight_full[layer_index]
        parts = [state] + [moved(state, "mp", by) for by in (1, 2, 3)]
        kept, sent = project_in(model_index, parts, gain_layers[layer_index], weight)
        total = kept + swapped(sent)
        squares = total[:, heads_half + head_size :][:, :1]
        total = total[:, : heads_half + head_size] * lax.rsqrt(
            squares / (n_mp * slice_width) + epsilon
        )
        query = total[:, :heads_half].reshape(rows, -1, head_size)
        query = rotate(query, cosine, sine).astype(jnp.bfloat16).reshape(rows, heads_half)
        keyval = total[:, None, heads_half:]
        keyval = rotate(keyval, keyval_cosine, keyval_sine).astype(jnp.bfloat16)[:, 0]
        gathered = spread(keyval).reshape(n_blk, blocks, rows_here, head_size)
        attended = attention(scalars, query, gathered, swapped(gathered))
        attended_other = swapped(attended)
        total, *terms = project_out(model_index, attended, attended_other, weight)
        arrived = [moved(terms[by - 1], "mp", by) for by in (2, 1, 3)]
        total = state.astype(jnp.float32) + total
        for part in arrived:
            total = total + part.astype(jnp.float32)
        state = total.astype(jnp.bfloat16)
        results.append(state)

    keep = jnp.where(first_core, results[0], results[1])
    send = jnp.where(first_core, results[1], results[0])
    other = swapped(send)
    even = jnp.where(first_core, keep, other).reshape(rows, -1, 1, lane)
    odd = jnp.where(first_core, other, keep).reshape(rows, -1, 1, lane)
    return jnp.concatenate([even, odd], axis=2).reshape(1, blocks, rows_here, slice_width)


def solution(mesh):
    return jax.shard_map(
        local,
        mesh=mesh,
        in_specs=(
            P("section", None),
            P(),
            P(None, ("blk", "mp")),
            P(("blk", "mp"), None),
            P(None, "blk", "mp"),
            P(),
            P(),
            P("section", None),
            P("section", "blk", "mp"),
            P("section", "blk", "mp", None, None),
            P("section", "mp", "blk"),
        ),
        out_specs=P("section", None, "blk", "mp"),
        check_vma=False,
    )
```

```python
import functools
import math

import jax
import jax.numpy as jnp
from jax import lax
from jax.experimental import pallas as pl
from jax.experimental.pallas import tpu as pltpu
from jax.sharding import PartitionSpec as P

epsilon = 1e-06
rope_base = 1000000.0
lane = 128


def moved(value, axis, by):
    size = lax.axis_size(axis)
    return lax.ppermute(value, axis, [(i, (i + by) % size) for i in range(size)])


def swapped(value):
    return lax.ppermute(value, "section", [(0, 1), (1, 0)])


def ringed(value, stride, by):
    size = lax.axis_size("blk")
    side = 4
    span = stride * side
    pairs = [
        (i, i // span * span + (i % span + by * stride) % span) for i in range(size)
    ]
    return lax.ppermute(value, "blk", pairs)


def rope_tables(where_at, head_size):
    steps_half = jnp.arange(head_size // 2).astype(jnp.float32)
    inverse = jnp.exp(-jnp.log(rope_base) * 2.0 * steps_half / head_size)
    angles = where_at.astype(jnp.float32)[:, None] * inverse[None, :]
    return (jnp.cos(angles), jnp.sin(angles))


def rotate(values, cosine, sine):
    half = values.shape[-1] // 2
    first = values[..., :half]
    second = values[..., half:]
    return jnp.concatenate(
        [first * cosine - second * sine, second * cosine + first * sine], axis=-1
    )


def my_half(value, axis, section_index):
    shape = value.shape
    runs = shape[axis] // (2 * lane)
    split = value.reshape(shape[:axis] + (runs, 2, lane) + shape[axis + 1 :])
    index = [slice(None)] * split.ndim
    index[axis + 1] = 0
    even = split[tuple(index)]
    index[axis + 1] = 1
    odd = split[tuple(index)]
    picked = jnp.where(section_index == 0, even, odd)
    return picked.reshape(shape[:axis] + (runs * lane,) + shape[axis + 1 :])


def spread(value):
    size = lax.axis_size("blk")
    copies = jnp.broadcast_to(value[None], (size,) + value.shape)
    return lax.all_to_all(copies, "blk", 0, 0, tiled=True)


def attention_kernel(scalars, query_ref, mine_ref, other_ref, out_ref, *, chunk_runs):
    runs, blocks, run, head_size = mine_ref.shape
    heads = query_ref.shape[1] // head_size
    rows = heads * run
    chunk = chunk_runs * run
    per_block = runs // chunk_runs
    block_len = runs * run
    start_one, start_two, cycle, section = scalars[0], scalars[1], scalars[2], scalars[3]
    factor = 1.0 / head_size**0.5 * math.log2(math.e)

    def stripes(key_ref, value_ref):
        def stripe(block, carry):
            row_from = pl.multiple_of(block * run, run)
            first = block * block_len + cycle * run
            here = query_ref[pl.ds(row_from, run), :]
            stacked = jnp.concatenate(
                [here[:, h * head_size : (h + 1) * head_size] for h in range(heads)], axis=0
            )
            row_at = lax.broadcasted_iota(jnp.int32, (rows, 1), 0) % run + first
            row_start = jnp.where(
                row_at >= start_two, start_two, jnp.where(row_at >= start_one, start_one, 0)
            )
            stripe_start = jnp.where(
                first >= start_two, start_two, jnp.where(first >= start_one, start_one, 0)
            )

            def step(index, state):
                top, total, mixed = state
                in_block = index // per_block
                from_run = (index % per_block) * chunk_runs
                key = key_ref[pl.ds(from_run, chunk_runs), in_block].reshape(chunk, head_size)
                value = value_ref[pl.ds(from_run, chunk_runs), in_block].reshape(chunk, head_size)
                scores = lax.dot_general(
                    stacked, key, (((1,), (1,)), ((), ())), preferred_element_type=jnp.float32
                )
                key_at = lax.broadcasted_iota(jnp.int32, (1, chunk), 1) + index * chunk
                allowed = (key_at <= row_at) & (key_at >= row_start)
                scores = jnp.where(allowed, scores * factor, -1e30)
                new_top = jnp.maximum(top, jnp.max(scores, axis=1, keepdims=True))
                fade = jnp.exp2(top - new_top)
                weights = jnp.exp2(scores - new_top)
                total = total * fade + jnp.sum(weights, axis=1, keepdims=True)
                mixed = mixed * fade + jnp.dot(
                    weights.astype(jnp.bfloat16), value, preferred_element_type=jnp.float32
                )
                return new_top, total, mixed

            state = (
                jnp.full((rows, 1), -1e30, jnp.float32),
                jnp.zeros((rows, 1), jnp.float32),
                jnp.zeros((rows, head_size), jnp.float32),
            )
            _, total, mixed = lax.fori_loop(
                stripe_start // chunk, (first + run - 1) // chunk + 1, step, state
            )
            result = (mixed / total).astype(out_ref.dtype)
            for h in range(heads):
                out_ref[pl.ds(row_from, run), h * head_size : (h + 1) * head_size] = result[
                    h * run : (h + 1) * run
                ]
            return carry

        lax.fori_loop(0, blocks, stripe, 0)

    @pl.when(section == 0)
    def _():
        stripes(mine_ref, other_ref)

    @pl.when(section != 0)
    def _():
        stripes(other_ref, mine_ref)


def attention(scalars, query, mine, other):
    whole = pl.BlockSpec(memory_space=pltpu.VMEM)
    return pl.pallas_call(
        functools.partial(attention_kernel, chunk_runs=mine.shape[0] // 2),
        out_shape=jax.ShapeDtypeStruct(query.shape, query.dtype),
        in_specs=[pl.BlockSpec(memory_space=pltpu.SMEM), whole, whole, whole],
        out_specs=whole,
        cost_estimate=pl.CostEstimate(
            flops=4 * query.size * mine.size // query.shape[1] // 4,
            bytes_accessed=2 * (2 * query.size + 2 * mine.size),
            transcendentals=0,
        ),
        name="attention",
    )(scalars, query, mine, other)


def merger_kernel(patches_ref, gain_ref, weight_ref, out_ref):
    width = gain_ref.shape[1]
    total = jnp.zeros(out_ref.shape, jnp.float32)
    for at in range(0, patches_ref.shape[1], width):
        piece = patches_ref[:, at : at + width].astype(jnp.float32)
        centered = piece - jnp.mean(piece, axis=1, keepdims=True)
        variance = jnp.mean(centered * centered, axis=1, keepdims=True)
        normed = (centered * lax.rsqrt(variance + epsilon) * gain_ref[...]).astype(jnp.bfloat16)
        total = total + jnp.dot(
            normed, weight_ref[at : at + width, :], preferred_element_type=jnp.float32
        )
    out_ref[...] = (0.5 * total * (1.0 + lax.erf(total * math.sqrt(0.5)))).astype(out_ref.dtype)


def merger_inner(patches, merge_gain, merge_first):
    whole = pl.BlockSpec(memory_space=pltpu.VMEM)
    rows, units = patches.shape[0], merge_first.shape[1]
    return pl.pallas_call(
        merger_kernel,
        out_shape=jax.ShapeDtypeStruct((rows, units), jnp.bfloat16),
        in_specs=[whole, whole, whole],
        out_specs=whole,
        cost_estimate=pl.CostEstimate(
            flops=2 * rows * merge_first.size,
            bytes_accessed=2 * (patches.size + merge_first.size),
            transcendentals=0,
        ),
        name="merger_inner",
    )(patches, merge_gain.reshape(1, -1), merge_first)


def merger_outer_kernel(place, mine_ref, other_ref, weight_ref, out_ref):
    section = place[0]
    pieces, share, depth = out_ref.shape
    tokens = mine_ref.shape[0]
    runs = weight_ref.shape[1] // (2 * lane)
    slices = runs * lane // depth
    weight = jnp.concatenate(
        [
            weight_ref[:, pl.ds(pl.multiple_of((2 * run + section) * lane, lane), lane)]
            for run in range(runs)
        ],
        axis=1,
    )
    for inner_ref, core in ((mine_ref, section), (other_ref, 1 - section)):
        result = jnp.dot(inner_ref[...], weight, preferred_element_type=jnp.float32)
        result = result.astype(out_ref.dtype)
        for owner in range(tokens // share):
            for piece in range(slices):
                out_ref[(core * (tokens // share) + owner) * slices + piece] = result[
                    owner * share : (owner + 1) * share, piece * depth : (piece + 1) * depth
                ]


def merger_outer(place, mine, other, merge_second, n_blk, n_mp):
    whole = pl.BlockSpec(memory_space=pltpu.VMEM)
    share = 2 * mine.shape[0] // n_blk
    depth = merge_second.shape[1] // 2 // n_mp
    return pl.pallas_call(
        merger_outer_kernel,
        out_shape=jax.ShapeDtypeStruct((n_blk * n_mp, share, depth), jnp.bfloat16),
        in_specs=[pl.BlockSpec(memory_space=pltpu.SMEM), whole, whole, whole],
        out_specs=whole,
        name="merger_outer",
    )(place, mine, other, merge_second)


def project_in_kernel(
    place,
    own_ref,
    from_one,
    from_two,
    from_three,
    gain_ref,
    weight_hbm,
    kept_ref,
    sent_ref,
    rows_ref,
    weight_ref,
    sums_ref,
    semaphores,
):
    pieces, _, depth = gain_ref.shape
    width = weight_ref.shape[1]
    queries = width // 2 - lane
    copies = []
    for piece in range(pieces):
        span = (pl.ds(piece * depth, depth), pl.ds(0, width))
        copies.append(
            pltpu.make_async_copy(
                weight_hbm.at[span], weight_ref.at[span], semaphores.at[piece]
            )
        )
        copies[-1].start()
    squares = jnp.zeros((own_ref.shape[0], 1), jnp.float32)
    for by, part_ref in enumerate((own_ref, from_one, from_two, from_three)):
        source = (place[2] + pieces - by) % pieces
        part = part_ref[...].astype(jnp.float32)
        squares = squares + jnp.sum(part * part, axis=1, keepdims=True)
        rows_ref[source] = (part * gain_ref[source]).astype(jnp.bfloat16)
    squares = jnp.broadcast_to(squares, (squares.shape[0], lane))
    kept_ref[:, queries + lane :] = squares
    sent_ref[:, queries + lane :] = squares
    for piece in range(pieces):
        copies[piece].wait()
        result = jnp.dot(
            rows_ref[piece],
            weight_ref[piece * depth : (piece + 1) * depth, :],
            preferred_element_type=jnp.float32,
        )
        if piece > 0:
            result = result + sums_ref[...]
        if piece < pieces - 1:
            sums_ref[...] = result
    kept_ref[:, :queries] = result[:, :queries]
    sent_ref[:, :queries] = result[:, queries : 2 * queries]
    kept_ref[:, queries : queries + lane] = result[:, 2 * queries : 2 * queries + lane]
    sent_ref[:, queries : queries + lane] = result[:, 2 * queries + lane :]


def project_in(place, parts, gain, weight):
    rows, depth = parts[0].shape
    width = 2 * (depth + lane)
    out = jax.ShapeDtypeStruct((rows, width // 2 + lane), jnp.float32)
    whole = pl.BlockSpec(memory_space=pltpu.VMEM)
    return pl.pallas_call(
        project_in_kernel,
        out_shape=(out, out),
        in_specs=[pl.BlockSpec(memory_space=pltpu.SMEM)]
        + [whole] * 5
        + [pl.BlockSpec(memory_space=pl.ANY)],
        out_specs=(whole, whole),
        scratch_shapes=[
            pltpu.VMEM((len(parts), rows, depth), jnp.bfloat16),
            pltpu.VMEM((weight.shape[0], width), jnp.bfloat16),
            pltpu.VMEM((rows, width), jnp.float32),
            pltpu.SemaphoreType.DMA((len(parts),)),
        ],
        cost_estimate=pl.CostEstimate(
            flops=2 * rows * weight.shape[0] * width,
            bytes_accessed=2 * weight.shape[0] * width + 8 * rows * out.shape[1],
            transcendentals=0,
        ),
        compiler_params=pltpu.CompilerParams(vmem_limit_bytes=24 << 20),
        name="project_in",
    )(place, *parts, gain, weight)


def project_out_kernel(
    place, mine_ref, other_ref, weight_hbm, own_ref, one_ref, two_ref, three_ref, weight_ref, semaphores
):
    half = mine_ref.shape[1]
    depth = own_ref.shape[1]
    over_last = (((1,), (1,)), ((), ()))
    outs = (own_ref, one_ref, two_ref, three_ref)
    copies = []
    for by in range(len(outs)):
        source = (place[2] + by) % len(outs)
        copies.append(
            pltpu.make_async_copy(
                weight_hbm.at[
                    pl.ds(source * depth, depth), pl.ds(weight_hbm.shape[1] - 2 * half, 2 * half)
                ],
                weight_ref.at[by],
                semaphores.at[by],
            )
        )
        copies[-1].start()
    for by, out_ref in enumerate(outs):
        copies[by].wait()
        result = lax.dot_general(
            mine_ref[...], weight_ref[by, :, :half], over_last, preferred_element_type=jnp.float32
        ) + lax.dot_general(
            other_ref[...], weight_ref[by, :, half:], over_last, preferred_element_type=jnp.float32
        )
        out_ref[...] = result.astype(out_ref.dtype)


def project_out(place, mine, other, weight):
    rows, half = mine.shape
    pieces = lax.axis_size("mp")
    depth = weight.shape[0] // pieces
    shape = jax.ShapeDtypeStruct((rows, depth), jnp.bfloat16)
    whole = pl.BlockSpec(memory_space=pltpu.VMEM)
    return pl.pallas_call(
        project_out_kernel,
        out_shape=[shape] * pieces,
        in_specs=[
            pl.BlockSpec(memory_space=pltpu.SMEM),
            whole,
            whole,
            pl.BlockSpec(memory_space=pl.ANY),
        ],
        out_specs=[whole] * pieces,
        scratch_shapes=[
            pltpu.VMEM((pieces, depth, 2 * half), jnp.bfloat16),
            pltpu.SemaphoreType.DMA((pieces,)),
        ],
        cost_estimate=pl.CostEstimate(
            flops=4 * rows * half * weight.shape[0],
            bytes_accessed=4 * half * weight.shape[0] + 2 * rows * weight.shape[0],
            transcendentals=0,
        ),
        compiler_params=pltpu.CompilerParams(vmem_limit_bytes=24 << 20),
        name="project_out",
    )(place, mine, other, weight)


def project_out_ring_kernel(place, mine_ref, other_ref, *refs):
    weights, outs = refs[:4], refs[4:]
    side = len(weights)
    half = mine_ref.shape[1]
    over_last = (((1,), (1,)), ((), ()))
    row, column = place[1] // side, place[1] % side
    for back, weight_ref in enumerate(weights):
        weight = weight_ref[...].reshape(-1, 2 * half)
        result = lax.dot_general(
            mine_ref[...], weight[:, :half], over_last, preferred_element_type=jnp.float32
        ) + lax.dot_general(
            other_ref[...], weight[:, half:], over_last, preferred_element_type=jnp.float32
        )
        result = result.astype(jnp.bfloat16)
        ahead = (row + 2 * side - back - place[2]) % side
        for by, out_ref in enumerate(outs):

            @pl.when(ahead == by)
            def _():
                for run in range(side):
                    at = pl.multiple_of(((column + side - run) % side) * lane, lane)
                    out_ref[:, pl.ds(at, lane)] = result[:, run * lane : (run + 1) * lane]


def project_out_ring(place, mine, other, weights):
    rows, half = mine.shape
    depth = weights[0].shape[0] * weights[0].shape[1]
    shape = jax.ShapeDtypeStruct((rows, depth), jnp.bfloat16)
    whole = pl.BlockSpec(memory_space=pltpu.VMEM)
    total = depth * len(weights)
    return pl.pallas_call(
        project_out_ring_kernel,
        out_shape=[shape] * len(weights),
        in_specs=[pl.BlockSpec(memory_space=pltpu.SMEM)] + [whole] * (2 + len(weights)),
        out_specs=[whole] * len(weights),
        cost_estimate=pl.CostEstimate(
            flops=4 * rows * half * total,
            bytes_accessed=4 * half * total + 2 * rows * total,
            transcendentals=0,
        ),
        compiler_params=pltpu.CompilerParams(vmem_limit_bytes=24 << 20),
        name="project_out_ring",
    )(place, mine, other, *weights)


def local(
    patches,
    merge_gain,
    merge_first,
    merge_second,
    text_embeds,
    positions,
    segments,
    norm_gain,
    query_weight,
    keyval_weight,
    out_weight,
):
    count = patches.shape[0]
    width = merge_gain.shape[0]
    blocks, rows_here, slice_width = text_embeds.shape
    seq_len = segments.shape[0]
    block_len = seq_len // blocks
    section_index = lax.axis_index("section")
    cycle_index = lax.axis_index("blk")
    model_index = lax.axis_index("mp")
    n_mp = lax.axis_size("mp")
    n_blk = lax.axis_size("blk")
    first_core = section_index == 0
    head_size = keyval_weight.shape[4]
    rows = blocks * rows_here
    layers = 2

    query_own = query_weight[0]
    keyval_own = keyval_weight[0].reshape(keyval_weight.shape[1], 2 * head_size)
    out_own = out_weight[0]
    heads_half = query_own.shape[1] // 2
    weight_half = query_own.shape[0] // 2

    def packed(core):
        keep_rows = slice(core * weight_half, (core + 1) * weight_half)
        query_rows, keyval_rows = query_own[keep_rows], keyval_own[keep_rows]
        out_rows = out_own[:, keep_rows].T
        halves = (core, 1 - core)
        parts = [query_rows[:, half * heads_half : (half + 1) * heads_half] for half in halves]
        parts += [keyval_rows[:, half * head_size : (half + 1) * head_size] for half in halves]
        parts += [out_rows[:, half * heads_half : (half + 1) * heads_half] for half in halves]
        return jnp.concatenate(parts, axis=1)

    for_first, for_second = packed(0), packed(1)
    weight_keep = jnp.where(first_core, for_first, for_second)
    weight_other = swapped(jnp.where(first_core, for_second, for_first))
    proj_width = 2 * (heads_half + head_size)
    proj_first = jnp.where(first_core, weight_keep[:, :proj_width], weight_other[:, :proj_width])
    out_first = jnp.where(first_core, weight_keep[:, proj_width:], weight_other[:, proj_width:])
    weight_second = jnp.where(first_core, weight_other, weight_keep)
    gain_half = norm_gain[0].reshape(-1, 2, lane)
    gain_keep = jnp.where(first_core, gain_half[:, 0], gain_half[:, 1])
    gain_send = jnp.where(first_core, gain_half[:, 1], gain_half[:, 0])
    gain_other = swapped(gain_send)
    gain_layers = [
        jnp.where(first_core, gain_keep, gain_other).reshape(n_mp, 1, -1),
        jnp.where(first_core, gain_other, gain_keep).reshape(n_mp, 1, -1),
    ]
    proj_full = lax.all_gather(proj_first, "blk", axis=0, tiled=True)
    second_full = lax.all_gather(weight_second, "blk", axis=0, tiled=True)
    out_near = jnp.stack([out_first] + [ringed(out_first, 1, by) for by in (1, 2, 3)])

    inner = merger_inner(patches, merge_gain, merge_first)
    place = jnp.stack([section_index, cycle_index, model_index]).astype(jnp.int32)
    merged_pieces = merger_outer(place, inner, swapped(inner), merge_second, n_blk, n_mp)
    merged_terms = lax.all_to_all(merged_pieces, ("blk", "mp"), 0, 0, tiled=True)

    row_where = (
        jnp.arange(blocks)[:, None] * block_len
        + cycle_index * rows_here
        + jnp.arange(rows_here)[None, :]
    ).reshape(-1)
    starts = jnp.stack([jnp.sum(segments < 1), jnp.sum(segments < 2)])
    scalars = jnp.concatenate([starts, jnp.stack([cycle_index, section_index])]).astype(jnp.int32)
    is_visual = (positions[None, :] == row_where[:, None]).astype(jnp.bfloat16)
    has_visual = jnp.max(is_visual, axis=1, keepdims=True)
    text_rows = my_half(text_embeds.reshape(rows, slice_width), 1, section_index)
    cosine, sine = rope_tables(row_where, head_size)
    merged_terms, scalars, is_visual, has_visual, text_rows, cosine, sine, out_near = (
        lax.optimization_barrier(
            (merged_terms, scalars, is_visual, has_visual, text_rows, cosine, sine, out_near)
        )
    )
    out_far = [out_near] + [ringed(out_near, n_blk // 4, by) for by in (1, 2, 3)]
    merged_mine = jnp.sum(merged_terms.astype(jnp.float32), axis=0).astype(jnp.bfloat16)
    merged = spread(merged_mine).reshape(n_blk * merged_mine.shape[0], -1)
    picked = jnp.dot(is_visual, merged, preferred_element_type=jnp.float32).astype(jnp.bfloat16)
    state = jnp.where(has_visual > 0, picked, text_rows)

    cosine = cosine[:, None, :]
    sine = sine[:, None, :]
    keyval_cosine = jnp.where(first_core, cosine, 1.0)
    keyval_sine = jnp.where(first_core, sine, 0.0)

    results = []
    for layer_index in range(layers):
        parts = [state] + [moved(state, "mp", by) for by in (1, 2, 3)]
        weight = proj_full if layer_index == 0 else second_full
        kept, sent = project_in(place, parts, gain_layers[layer_index], weight)
        total = kept + swapped(sent)
        squares = total[:, heads_half + head_size :][:, :1]
        total = total[:, : heads_half + head_size] * lax.rsqrt(
            squares / (n_mp * slice_width) + epsilon
        )
        query = total[:, :heads_half].reshape(rows, -1, head_size)
        query = rotate(query, cosine, sine).astype(jnp.bfloat16).reshape(rows, heads_half)
        keyval = total[:, None, heads_half:]
        keyval = rotate(keyval, keyval_cosine, keyval_sine).astype(jnp.bfloat16)[:, 0]
        gathered = spread(keyval).reshape(n_blk, blocks, rows_here, head_size)
        attended = attention(scalars, query, gathered, swapped(gathered))
        attended_other = swapped(attended)
        if layer_index == 0:
            own, *terms = project_out_ring(place, attended, attended_other, out_far)
        else:
            own, *terms = project_out(place, attended, attended_other, second_full)
        arrived = [moved(terms[by - 1], "mp", by) for by in (2, 1, 3)]
        total = state.astype(jnp.float32) + own.astype(jnp.float32)
        for part in arrived:
            total = total + part.astype(jnp.float32)
        state = total.astype(jnp.bfloat16)
        results.append(state)

    keep = jnp.where(first_core, results[0], results[1])
    send = jnp.where(first_core, results[1], results[0])
    other = swapped(send)
    even = jnp.where(first_core, keep, other).reshape(rows, -1, 1, lane)
    odd = jnp.where(first_core, other, keep).reshape(rows, -1, 1, lane)
    return jnp.concatenate([even, odd], axis=2).reshape(1, blocks, rows_here, slice_width)


def solution(mesh):
    return jax.shard_map(
        local,
        mesh=mesh,
        in_specs=(
            P("section", None),
            P(),
            P(None, ("blk", "mp")),
            P(("blk", "mp"), None),
            P(None, "blk", "mp"),
            P(),
            P(),
            P("section", None),
            P("section", "blk", "mp"),
            P("section", "blk", "mp", None, None),
            P("section", "mp", "blk"),
        ),
        out_specs=P("section", None, "blk", "mp"),
        check_vma=False,
    )
```

```python
import functools
import math

import jax
import jax.numpy as jnp
from jax import lax
from jax.experimental import pallas as pl
from jax.experimental.pallas import tpu as pltpu
from jax.sharding import PartitionSpec as P

epsilon = 1e-06
rope_base = 1000000.0
lane = 128


def moved(value, axis, by):
    size = lax.axis_size(axis)
    return lax.ppermute(value, axis, [(i, (i + by) % size) for i in range(size)])


def swapped(value):
    return lax.ppermute(value, "section", [(0, 1), (1, 0)])


def rope_tables(where_at, head_size):
    steps_half = jnp.arange(head_size // 2).astype(jnp.float32)
    inverse = jnp.exp(-jnp.log(rope_base) * 2.0 * steps_half / head_size)
    angles = where_at.astype(jnp.float32)[:, None] * inverse[None, :]
    return (jnp.cos(angles), jnp.sin(angles))


def rotate(values, cosine, sine):
    half = values.shape[-1] // 2
    first = values[..., :half]
    second = values[..., half:]
    return jnp.concatenate(
        [first * cosine - second * sine, second * cosine + first * sine], axis=-1
    )


def my_half(value, axis, section_index):
    shape = value.shape
    runs = shape[axis] // (2 * lane)
    split = value.reshape(shape[:axis] + (runs, 2, lane) + shape[axis + 1 :])
    index = [slice(None)] * split.ndim
    index[axis + 1] = 0
    even = split[tuple(index)]
    index[axis + 1] = 1
    odd = split[tuple(index)]
    picked = jnp.where(section_index == 0, even, odd)
    return picked.reshape(shape[:axis] + (runs * lane,) + shape[axis + 1 :])


def spread(value):
    size = lax.axis_size("blk")
    copies = jnp.broadcast_to(value[None], (size,) + value.shape)
    return lax.all_to_all(copies, "blk", 0, 0, tiled=True)


def attention_kernel(scalars, query_ref, mine_ref, other_ref, out_ref, *, chunk_runs):
    runs, blocks, run, head_size = mine_ref.shape
    heads = query_ref.shape[1] // head_size
    rows = heads * run
    chunk = chunk_runs * run
    per_block = runs // chunk_runs
    block_len = runs * run
    start_one, start_two, cycle, section = scalars[0], scalars[1], scalars[2], scalars[3]
    factor = 1.0 / head_size**0.5 * math.log2(math.e)

    def stripes(key_ref, value_ref):
        def stripe(block, carry):
            row_from = pl.multiple_of(block * run, run)
            first = block * block_len + cycle * run
            here = query_ref[pl.ds(row_from, run), :]
            stacked = jnp.concatenate(
                [here[:, h * head_size : (h + 1) * head_size] for h in range(heads)], axis=0
            )
            row_at = lax.broadcasted_iota(jnp.int32, (rows, 1), 0) % run + first
            row_start = jnp.where(
                row_at >= start_two, start_two, jnp.where(row_at >= start_one, start_one, 0)
            )
            stripe_start = jnp.where(
                first >= start_two, start_two, jnp.where(first >= start_one, start_one, 0)
            )

            def step(index, state):
                top, total, mixed = state
                in_block = index // per_block
                from_run = (index % per_block) * chunk_runs
                key = key_ref[pl.ds(from_run, chunk_runs), in_block].reshape(chunk, head_size)
                value = value_ref[pl.ds(from_run, chunk_runs), in_block].reshape(chunk, head_size)
                scores = lax.dot_general(
                    stacked, key, (((1,), (1,)), ((), ())), preferred_element_type=jnp.float32
                )
                key_at = lax.broadcasted_iota(jnp.int32, (1, chunk), 1) + index * chunk
                allowed = (key_at <= row_at) & (key_at >= row_start)
                scores = jnp.where(allowed, scores * factor, -1e30)
                new_top = jnp.maximum(top, jnp.max(scores, axis=1, keepdims=True))
                fade = jnp.exp2(top - new_top)
                weights = jnp.exp2(scores - new_top)
                total = total * fade + jnp.sum(weights, axis=1, keepdims=True)
                mixed = mixed * fade + jnp.dot(
                    weights.astype(jnp.bfloat16), value, preferred_element_type=jnp.float32
                )
                return new_top, total, mixed

            state = (
                jnp.full((rows, 1), -1e30, jnp.float32),
                jnp.zeros((rows, 1), jnp.float32),
                jnp.zeros((rows, head_size), jnp.float32),
            )
            _, total, mixed = lax.fori_loop(
                stripe_start // chunk, (first + run - 1) // chunk + 1, step, state
            )
            result = (mixed / total).astype(out_ref.dtype)
            for h in range(heads):
                out_ref[pl.ds(row_from, run), h * head_size : (h + 1) * head_size] = result[
                    h * run : (h + 1) * run
                ]
            return carry

        lax.fori_loop(0, blocks, stripe, 0)

    @pl.when(section == 0)
    def _():
        stripes(mine_ref, other_ref)

    @pl.when(section != 0)
    def _():
        stripes(other_ref, mine_ref)


def attention(scalars, query, mine, other):
    whole = pl.BlockSpec(memory_space=pltpu.VMEM)
    return pl.pallas_call(
        functools.partial(attention_kernel, chunk_runs=mine.shape[0] // 2),
        out_shape=jax.ShapeDtypeStruct(query.shape, query.dtype),
        in_specs=[pl.BlockSpec(memory_space=pltpu.SMEM), whole, whole, whole],
        out_specs=whole,
        cost_estimate=pl.CostEstimate(
            flops=4 * query.size * mine.size // query.shape[1] // 4,
            bytes_accessed=2 * (2 * query.size + 2 * mine.size),
            transcendentals=0,
        ),
        name="attention",
    )(scalars, query, mine, other)


def merger_kernel(patches_ref, gain_ref, weight_ref, out_ref):
    width = gain_ref.shape[1]
    total = jnp.zeros(out_ref.shape, jnp.float32)
    for at in range(0, patches_ref.shape[1], width):
        piece = patches_ref[:, at : at + width].astype(jnp.float32)
        centered = piece - jnp.mean(piece, axis=1, keepdims=True)
        variance = jnp.mean(centered * centered, axis=1, keepdims=True)
        normed = (centered * lax.rsqrt(variance + epsilon) * gain_ref[...]).astype(jnp.bfloat16)
        total = total + jnp.dot(
            normed, weight_ref[at : at + width, :], preferred_element_type=jnp.float32
        )
    out_ref[...] = (0.5 * total * (1.0 + lax.erf(total * math.sqrt(0.5)))).astype(out_ref.dtype)


def merger_inner(patches, merge_gain, merge_first):
    whole = pl.BlockSpec(memory_space=pltpu.VMEM)
    rows, units = patches.shape[0], merge_first.shape[1]
    return pl.pallas_call(
        merger_kernel,
        out_shape=jax.ShapeDtypeStruct((rows, units), jnp.bfloat16),
        in_specs=[whole, whole, whole],
        out_specs=whole,
        cost_estimate=pl.CostEstimate(
            flops=2 * rows * merge_first.size,
            bytes_accessed=2 * (patches.size + merge_first.size),
            transcendentals=0,
        ),
        name="merger_inner",
    )(patches, merge_gain.reshape(1, -1), merge_first)


def merger_outer_kernel(place, mine_ref, other_ref, weight_ref, out_ref):
    section = place[0]
    pieces, share, depth = out_ref.shape
    tokens = mine_ref.shape[0]
    runs = weight_ref.shape[1] // (2 * lane)
    slices = runs * lane // depth
    weight = jnp.concatenate(
        [
            weight_ref[:, pl.ds(pl.multiple_of((2 * run + section) * lane, lane), lane)]
            for run in range(runs)
        ],
        axis=1,
    )
    for inner_ref, core in ((mine_ref, section), (other_ref, 1 - section)):
        result = jnp.dot(inner_ref[...], weight, preferred_element_type=jnp.float32)
        result = result.astype(out_ref.dtype)
        for owner in range(tokens // share):
            for piece in range(slices):
                out_ref[(core * (tokens // share) + owner) * slices + piece] = result[
                    owner * share : (owner + 1) * share, piece * depth : (piece + 1) * depth
                ]


def merger_outer(place, mine, other, merge_second, n_blk, n_mp):
    whole = pl.BlockSpec(memory_space=pltpu.VMEM)
    share = 2 * mine.shape[0] // n_blk
    depth = merge_second.shape[1] // 2 // n_mp
    return pl.pallas_call(
        merger_outer_kernel,
        out_shape=jax.ShapeDtypeStruct((n_blk * n_mp, share, depth), jnp.bfloat16),
        in_specs=[pl.BlockSpec(memory_space=pltpu.SMEM), whole, whole, whole],
        out_specs=whole,
        name="merger_outer",
    )(place, mine, other, merge_second)


def project_in_kernel(
    place,
    own_ref,
    from_one,
    from_two,
    from_three,
    gain_ref,
    weight_hbm,
    kept_ref,
    sent_ref,
    rows_ref,
    weight_ref,
    sums_ref,
    semaphores,
):
    pieces, _, depth = gain_ref.shape
    half = weight_ref.shape[1] // 2
    copies = []
    for piece in range(pieces):
        span = (pl.ds(piece * depth, depth), pl.ds(0, 2 * half))
        copies.append(
            pltpu.make_async_copy(
                weight_hbm.at[span], weight_ref.at[span], semaphores.at[piece]
            )
        )
        copies[-1].start()
    squares = jnp.zeros((own_ref.shape[0], 1), jnp.float32)
    for by, part_ref in enumerate((own_ref, from_one, from_two, from_three)):
        source = (place[2] + pieces - by) % pieces
        part = part_ref[...].astype(jnp.float32)
        if kept_ref.shape[1] > half:
            squares = squares + jnp.sum(part * part, axis=1, keepdims=True)
        rows_ref[source] = (part * gain_ref[source]).astype(jnp.bfloat16)
    if kept_ref.shape[1] > half:
        squares = jnp.broadcast_to(squares, (squares.shape[0], lane))
        kept_ref[:, half:] = squares
        sent_ref[:, half:] = squares
    for piece in range(pieces):
        copies[piece].wait()
        result = jnp.dot(
            rows_ref[piece],
            weight_ref[piece * depth : (piece + 1) * depth, :],
            preferred_element_type=jnp.float32,
        )
        if piece > 0:
            result = result + sums_ref[...]
        if piece < pieces - 1:
            sums_ref[...] = result
    kept_ref[:, :half] = result[:, :half]
    sent_ref[:, :half] = result[:, half:]


def project_in(place, parts, gain, weight, width, with_squares):
    rows, depth = parts[0].shape
    spare = lane if with_squares else 0
    out = jax.ShapeDtypeStruct((rows, width // 2 + spare), jnp.float32)
    whole = pl.BlockSpec(memory_space=pltpu.VMEM)
    return pl.pallas_call(
        project_in_kernel,
        out_shape=(out, out),
        in_specs=[pl.BlockSpec(memory_space=pltpu.SMEM)]
        + [whole] * 5
        + [pl.BlockSpec(memory_space=pl.ANY)],
        out_specs=(whole, whole),
        scratch_shapes=[
            pltpu.VMEM((len(parts), rows, depth), jnp.bfloat16),
            pltpu.VMEM((weight.shape[0], width), jnp.bfloat16),
            pltpu.VMEM((rows, width), jnp.float32),
            pltpu.SemaphoreType.DMA((len(parts),)),
        ],
        cost_estimate=pl.CostEstimate(
            flops=2 * rows * weight.shape[0] * width,
            bytes_accessed=2 * weight.shape[0] * width + 8 * rows * out.shape[1],
            transcendentals=0,
        ),
        compiler_params=pltpu.CompilerParams(vmem_limit_bytes=24 << 20),
        name="project_kv" if with_squares else "project_q",
    )(place, *parts, gain, weight)


def project_out_kernel(
    place, mine_ref, other_ref, weight_hbm, own_ref, one_ref, two_ref, three_ref, weight_ref, semaphores
):
    half = mine_ref.shape[1]
    depth = own_ref.shape[1]
    over_last = (((1,), (1,)), ((), ()))
    outs = (own_ref, one_ref, two_ref, three_ref)
    copies = []
    for by in range(len(outs)):
        source = (place[2] + by) % len(outs)
        copies.append(
            pltpu.make_async_copy(
                weight_hbm.at[
                    pl.ds(source * depth, depth), pl.ds(weight_hbm.shape[1] - 2 * half, 2 * half)
                ],
                weight_ref.at[by],
                semaphores.at[by],
            )
        )
        copies[-1].start()
    for by, out_ref in enumerate(outs):
        copies[by].wait()
        result = lax.dot_general(
            mine_ref[...], weight_ref[by, :, :half], over_last, preferred_element_type=jnp.float32
        ) + lax.dot_general(
            other_ref[...], weight_ref[by, :, half:], over_last, preferred_element_type=jnp.float32
        )
        out_ref[...] = result.astype(out_ref.dtype)


def project_out(place, mine, other, weight):
    rows, half = mine.shape
    pieces = lax.axis_size("mp")
    depth = weight.shape[0] // pieces
    shape = jax.ShapeDtypeStruct((rows, depth), jnp.bfloat16)
    whole = pl.BlockSpec(memory_space=pltpu.VMEM)
    return pl.pallas_call(
        project_out_kernel,
        out_shape=[shape] * pieces,
        in_specs=[
            pl.BlockSpec(memory_space=pltpu.SMEM),
            whole,
            whole,
            pl.BlockSpec(memory_space=pl.ANY),
        ],
        out_specs=[whole] * pieces,
        scratch_shapes=[
            pltpu.VMEM((pieces, depth, 2 * half), jnp.bfloat16),
            pltpu.SemaphoreType.DMA((pieces,)),
        ],
        cost_estimate=pl.CostEstimate(
            flops=4 * rows * half * weight.shape[0],
            bytes_accessed=4 * half * weight.shape[0] + 2 * rows * weight.shape[0],
            transcendentals=0,
        ),
        compiler_params=pltpu.CompilerParams(vmem_limit_bytes=24 << 20),
        name="project_out",
    )(place, mine, other, weight)


def local(
    patches,
    merge_gain,
    merge_first,
    merge_second,
    text_embeds,
    positions,
    segments,
    norm_gain,
    query_weight,
    keyval_weight,
    out_weight,
):
    count = patches.shape[0]
    width = merge_gain.shape[0]
    blocks, rows_here, slice_width = text_embeds.shape
    seq_len = segments.shape[0]
    block_len = seq_len // blocks
    section_index = lax.axis_index("section")
    cycle_index = lax.axis_index("blk")
    model_index = lax.axis_index("mp")
    n_mp = lax.axis_size("mp")
    n_blk = lax.axis_size("blk")
    first_core = section_index == 0
    head_size = keyval_weight.shape[4]
    rows = blocks * rows_here
    layers = 2

    query_own = query_weight[0]
    keyval_own = keyval_weight[0].reshape(keyval_weight.shape[1], 2 * head_size)
    out_own = out_weight[0]
    heads_half = query_own.shape[1] // 2
    weight_half = query_own.shape[0] // 2

    def packed(core):
        keep_rows = slice(core * weight_half, (core + 1) * weight_half)
        query_rows, keyval_rows = query_own[keep_rows], keyval_own[keep_rows]
        out_rows = out_own[:, keep_rows].T
        halves = (core, 1 - core)
        parts = [keyval_rows[:, half * head_size : (half + 1) * head_size] for half in halves]
        parts += [query_rows[:, half * heads_half : (half + 1) * heads_half] for half in halves]
        parts += [out_rows[:, half * heads_half : (half + 1) * heads_half] for half in halves]
        return jnp.concatenate(parts, axis=1)

    for_first, for_second = packed(0), packed(1)
    weight_keep = jnp.where(first_core, for_first, for_second)
    weight_other = swapped(jnp.where(first_core, for_second, for_first))
    keyval_width = 2 * head_size
    keyval_shards, weight_full = [], []
    for home in range(layers):
        mine = jnp.where(section_index == home, weight_keep, weight_other)
        keyval_shards.append(mine[:, :keyval_width])
        weight_full.append(lax.all_gather(mine[:, keyval_width:], "blk", axis=0, tiled=True))
    gain_half = norm_gain[0].reshape(-1, 2, lane)
    gain_keep = jnp.where(first_core, gain_half[:, 0], gain_half[:, 1])
    gain_send = jnp.where(first_core, gain_half[:, 1], gain_half[:, 0])
    gain_other = swapped(gain_send)
    gain_layers = [
        jnp.where(first_core, gain_keep, gain_other).reshape(n_mp, 1, -1),
        jnp.where(first_core, gain_other, gain_keep).reshape(n_mp, 1, -1),
    ]
    keyval_weight_full = spread(keyval_shards[0])

    inner = merger_inner(patches, merge_gain, merge_first)
    place = jnp.stack([section_index, cycle_index, model_index]).astype(jnp.int32)
    merged_pieces = merger_outer(place, inner, swapped(inner), merge_second, n_blk, n_mp)
    merged_pieces, keyval_weight_full = lax.optimization_barrier(
        (merged_pieces, keyval_weight_full)
    )
    merged_terms = lax.all_to_all(merged_pieces, ("blk", "mp"), 0, 0, tiled=True)

    row_where = (
        jnp.arange(blocks)[:, None] * block_len
        + cycle_index * rows_here
        + jnp.arange(rows_here)[None, :]
    ).reshape(-1)
    starts = jnp.stack([jnp.sum(segments < 1), jnp.sum(segments < 2)])
    scalars = jnp.concatenate([starts, jnp.stack([cycle_index, section_index])]).astype(jnp.int32)
    is_visual = (positions[None, :] == row_where[:, None]).astype(jnp.bfloat16)
    has_visual = jnp.max(is_visual, axis=1, keepdims=True)
    text_rows = my_half(text_embeds.reshape(rows, slice_width), 1, section_index)
    cosine, sine = rope_tables(row_where, head_size)
    merged_terms, scalars, is_visual, has_visual, text_rows, cosine, sine = (
        lax.optimization_barrier(
            (merged_terms, scalars, is_visual, has_visual, text_rows, cosine, sine)
        )
    )
    merged_mine = jnp.sum(merged_terms.astype(jnp.float32), axis=0).astype(jnp.bfloat16)
    merged = spread(merged_mine).reshape(n_blk * merged_mine.shape[0], -1)
    picked = jnp.dot(is_visual, merged, preferred_element_type=jnp.float32).astype(jnp.bfloat16)
    state = jnp.where(has_visual > 0, picked, text_rows)

    keyval_cosine = jnp.where(first_core, cosine, 1.0)
    keyval_sine = jnp.where(first_core, sine, 0.0)

    results = []
    for layer_index in range(layers):
        parts = [state] + [moved(state, "mp", by) for by in (1, 2, 3)]
        gain = gain_layers[layer_index]
        weight = weight_full[layer_index]
        kept, sent = project_in(
            place, parts, gain, keyval_weight_full.reshape(-1, keyval_width), keyval_width, True
        )
        total = kept + swapped(sent)
        shrink = lax.rsqrt(total[:, head_size : head_size + 1] / (n_mp * slice_width) + epsilon)
        keyval = rotate(total[:, :head_size] * shrink, keyval_cosine, keyval_sine).astype(jnp.bfloat16)
        keyval, parts = lax.optimization_barrier((keyval, parts))
        kept, sent = project_in(place, parts, gain, weight, 2 * heads_half, False)
        query = ((kept + swapped(sent)) * shrink).reshape(rows, -1, head_size)
        query = rotate(query, cosine[:, None, :], sine[:, None, :])
        query = query.astype(jnp.bfloat16).reshape(rows, heads_half)
        gathered = spread(keyval).reshape(n_blk, blocks, rows_here, head_size)
        attended = attention(scalars, query, gathered, swapped(gathered))
        if layer_index + 1 < layers:
            attended, shard = lax.optimization_barrier((attended, keyval_shards[layer_index + 1]))
            keyval_weight_full = spread(shard)
        attended_other = swapped(attended)
        own, *terms = project_out(place, attended, attended_other, weight)
        arrived = [moved(terms[by - 1], "mp", by) for by in (2, 1, 3)]
        total = state.astype(jnp.float32) + own.astype(jnp.float32)
        for part in arrived:
            total = total + part.astype(jnp.float32)
        state = total.astype(jnp.bfloat16)
        results.append(state)

    keep = jnp.where(first_core, results[0], results[1])
    send = jnp.where(first_core, results[1], results[0])
    other = swapped(send)
    even = jnp.where(first_core, keep, other).reshape(rows, -1, 1, lane)
    odd = jnp.where(first_core, other, keep).reshape(rows, -1, 1, lane)
    return jnp.concatenate([even, odd], axis=2).reshape(1, blocks, rows_here, slice_width)


def solution(mesh):
    return jax.shard_map(
        local,
        mesh=mesh,
        in_specs=(
            P("section", None),
            P(),
            P(None, ("blk", "mp")),
            P(("blk", "mp"), None),
            P(None, "blk", "mp"),
            P(),
            P(),
            P("section", None),
            P("section", "blk", "mp"),
            P("section", "blk", "mp", None, None),
            P("section", "mp", "blk"),
        ),
        out_specs=P("section", None, "blk", "mp"),
        check_vma=False,
    )
```

```python
import functools
import math

import jax
import jax.numpy as jnp
from jax import lax
from jax.experimental import pallas as pl
from jax.experimental.pallas import tpu as pltpu
from jax.sharding import PartitionSpec as P

epsilon = 1e-06
rope_base = 1000000.0
lane = 128


def moved(value, axis, by):
    size = lax.axis_size(axis)
    return lax.ppermute(value, axis, [(i, (i + by) % size) for i in range(size)])


def swapped(value):
    return lax.ppermute(value, "section", [(0, 1), (1, 0)])


def rope_tables(where_at, head_size):
    steps_half = jnp.arange(head_size // 2).astype(jnp.float32)
    inverse = jnp.exp(-jnp.log(rope_base) * 2.0 * steps_half / head_size)
    angles = where_at.astype(jnp.float32)[:, None] * inverse[None, :]
    return (jnp.cos(angles), jnp.sin(angles))


def rotate(values, cosine, sine):
    half = values.shape[-1] // 2
    first = values[..., :half]
    second = values[..., half:]
    return jnp.concatenate(
        [first * cosine - second * sine, second * cosine + first * sine], axis=-1
    )


def my_half(value, axis, section_index):
    shape = value.shape
    runs = shape[axis] // (2 * lane)
    split = value.reshape(shape[:axis] + (runs, 2, lane) + shape[axis + 1 :])
    index = [slice(None)] * split.ndim
    index[axis + 1] = 0
    even = split[tuple(index)]
    index[axis + 1] = 1
    odd = split[tuple(index)]
    picked = jnp.where(section_index == 0, even, odd)
    return picked.reshape(shape[:axis] + (runs * lane,) + shape[axis + 1 :])


def spread(value):
    size = lax.axis_size("blk")
    copies = jnp.broadcast_to(value[None], (size,) + value.shape)
    return lax.all_to_all(copies, "blk", 0, 0, tiled=True)


def attention_kernel(scalars, query_ref, mine_ref, other_ref, out_ref, *, chunk_runs):
    runs, blocks, run, head_size = mine_ref.shape
    heads = query_ref.shape[1] // head_size
    rows = heads * run
    chunk = chunk_runs * run
    per_block = runs // chunk_runs
    block_len = runs * run
    start_one, start_two, cycle, section = scalars[0], scalars[1], scalars[2], scalars[3]
    factor = 1.0 / head_size**0.5 * math.log2(math.e)

    def stripes(key_ref, value_ref):
        def stripe(block, carry):
            row_from = pl.multiple_of(block * run, run)
            first = block * block_len + cycle * run
            here = query_ref[pl.ds(row_from, run), :]
            stacked = jnp.concatenate(
                [here[:, h * head_size : (h + 1) * head_size] for h in range(heads)], axis=0
            )
            row_at = lax.broadcasted_iota(jnp.int32, (rows, 1), 0) % run + first
            row_start = jnp.where(
                row_at >= start_two, start_two, jnp.where(row_at >= start_one, start_one, 0)
            )
            stripe_start = jnp.where(
                first >= start_two, start_two, jnp.where(first >= start_one, start_one, 0)
            )

            def step(index, state):
                top, total, mixed = state
                in_block = index // per_block
                from_run = (index % per_block) * chunk_runs
                key = key_ref[pl.ds(from_run, chunk_runs), in_block].reshape(chunk, head_size)
                value = value_ref[pl.ds(from_run, chunk_runs), in_block].reshape(chunk, head_size)
                scores = lax.dot_general(
                    stacked, key, (((1,), (1,)), ((), ())), preferred_element_type=jnp.float32
                )
                key_at = lax.broadcasted_iota(jnp.int32, (1, chunk), 1) + index * chunk
                allowed = (key_at <= row_at) & (key_at >= row_start)
                scores = jnp.where(allowed, scores * factor, -1e30)
                new_top = jnp.maximum(top, jnp.max(scores, axis=1, keepdims=True))
                fade = jnp.exp2(top - new_top)
                weights = jnp.exp2(scores - new_top)
                total = total * fade + jnp.sum(weights, axis=1, keepdims=True)
                mixed = mixed * fade + jnp.dot(
                    weights.astype(jnp.bfloat16), value, preferred_element_type=jnp.float32
                )
                return new_top, total, mixed

            state = (
                jnp.full((rows, 1), -1e30, jnp.float32),
                jnp.zeros((rows, 1), jnp.float32),
                jnp.zeros((rows, head_size), jnp.float32),
            )
            _, total, mixed = lax.fori_loop(
                stripe_start // chunk, (first + run - 1) // chunk + 1, step, state
            )
            result = (mixed / total).astype(out_ref.dtype)
            for h in range(heads):
                out_ref[pl.ds(row_from, run), h * head_size : (h + 1) * head_size] = result[
                    h * run : (h + 1) * run
                ]
            return carry

        lax.fori_loop(0, blocks, stripe, 0)

    @pl.when(section == 0)
    def _():
        stripes(mine_ref, other_ref)

    @pl.when(section != 0)
    def _():
        stripes(other_ref, mine_ref)


def attention(scalars, query, mine, other):
    whole = pl.BlockSpec(memory_space=pltpu.VMEM)
    return pl.pallas_call(
        functools.partial(attention_kernel, chunk_runs=mine.shape[0] // 2),
        out_shape=jax.ShapeDtypeStruct(query.shape, query.dtype),
        in_specs=[pl.BlockSpec(memory_space=pltpu.SMEM), whole, whole, whole],
        out_specs=whole,
        cost_estimate=pl.CostEstimate(
            flops=4 * query.size * mine.size // query.shape[1] // 4,
            bytes_accessed=2 * (2 * query.size + 2 * mine.size),
            transcendentals=0,
        ),
        name="attention",
    )(scalars, query, mine, other)


def merger_kernel(patches_ref, gain_ref, weight_ref, out_ref):
    width = gain_ref.shape[1]
    total = jnp.zeros(out_ref.shape, jnp.float32)
    for at in range(0, patches_ref.shape[1], width):
        piece = patches_ref[:, at : at + width].astype(jnp.float32)
        centered = piece - jnp.mean(piece, axis=1, keepdims=True)
        variance = jnp.mean(centered * centered, axis=1, keepdims=True)
        normed = (centered * lax.rsqrt(variance + epsilon) * gain_ref[...]).astype(jnp.bfloat16)
        total = total + jnp.dot(
            normed, weight_ref[at : at + width, :], preferred_element_type=jnp.float32
        )
    out_ref[...] = (0.5 * total * (1.0 + lax.erf(total * math.sqrt(0.5)))).astype(out_ref.dtype)


def merger_inner(patches, merge_gain, merge_first):
    whole = pl.BlockSpec(memory_space=pltpu.VMEM)
    rows, units = patches.shape[0], merge_first.shape[1]
    return pl.pallas_call(
        merger_kernel,
        out_shape=jax.ShapeDtypeStruct((rows, units), jnp.bfloat16),
        in_specs=[whole, whole, whole],
        out_specs=whole,
        cost_estimate=pl.CostEstimate(
            flops=2 * rows * merge_first.size,
            bytes_accessed=2 * (patches.size + merge_first.size),
            transcendentals=0,
        ),
        name="merger_inner",
    )(patches, merge_gain.reshape(1, -1), merge_first)


def merger_outer_kernel(place, mine_ref, other_ref, weight_ref, out_ref):
    section = place[0]
    pieces, share, depth = out_ref.shape
    tokens = mine_ref.shape[0]
    runs = weight_ref.shape[1] // (2 * lane)
    slices = runs * lane // depth
    weight = jnp.concatenate(
        [
            weight_ref[:, pl.ds(pl.multiple_of((2 * run + section) * lane, lane), lane)]
            for run in range(runs)
        ],
        axis=1,
    )
    for inner_ref, core in ((mine_ref, section), (other_ref, 1 - section)):
        result = jnp.dot(inner_ref[...], weight, preferred_element_type=jnp.float32)
        result = result.astype(out_ref.dtype)
        for owner in range(tokens // share):
            for piece in range(slices):
                out_ref[(core * (tokens // share) + owner) * slices + piece] = result[
                    owner * share : (owner + 1) * share, piece * depth : (piece + 1) * depth
                ]


def merger_outer(place, mine, other, merge_second, n_blk, n_mp):
    whole = pl.BlockSpec(memory_space=pltpu.VMEM)
    share = 2 * mine.shape[0] // n_blk
    depth = merge_second.shape[1] // 2 // n_mp
    return pl.pallas_call(
        merger_outer_kernel,
        out_shape=jax.ShapeDtypeStruct((n_blk * n_mp, share, depth), jnp.bfloat16),
        in_specs=[pl.BlockSpec(memory_space=pltpu.SMEM), whole, whole, whole],
        out_specs=whole,
        name="merger_outer",
    )(place, mine, other, merge_second)


def project_in_kernel(
    place,
    own_ref,
    from_one,
    from_two,
    from_three,
    gain_ref,
    weight_hbm,
    kept_ref,
    sent_ref,
    rows_ref,
    weight_ref,
    sums_ref,
    semaphores,
    *,
    at,
):
    pieces, _, depth = gain_ref.shape
    half = weight_ref.shape[1] // 2
    copies = []
    for piece in range(pieces):
        deep = pl.ds(piece * depth, depth)
        copies.append(
            pltpu.make_async_copy(
                weight_hbm.at[deep, pl.ds(at, 2 * half)], weight_ref.at[deep], semaphores.at[piece]
            )
        )
        copies[-1].start()
    squares = jnp.zeros((own_ref.shape[0], 1), jnp.float32)
    for by, part_ref in enumerate((own_ref, from_one, from_two, from_three)):
        source = (place[2] + pieces - by) % pieces
        part = part_ref[...].astype(jnp.float32)
        if kept_ref.shape[1] > half:
            squares = squares + jnp.sum(part * part, axis=1, keepdims=True)
        rows_ref[source] = (part * gain_ref[source]).astype(jnp.bfloat16)
    if kept_ref.shape[1] > half:
        squares = jnp.broadcast_to(squares, (squares.shape[0], lane))
        kept_ref[:, half:] = squares
        sent_ref[:, half:] = squares
    for piece in range(pieces):
        copies[piece].wait()
        result = jnp.dot(
            rows_ref[piece],
            weight_ref[piece * depth : (piece + 1) * depth, :],
            preferred_element_type=jnp.float32,
        )
        if piece > 0:
            result = result + sums_ref[...]
        if piece < pieces - 1:
            sums_ref[...] = result
    kept_ref[:, :half] = result[:, :half]
    sent_ref[:, :half] = result[:, half:]


def project_in(place, parts, gain, weight, at, width, with_squares):
    rows, depth = parts[0].shape
    spare = lane if with_squares else 0
    out = jax.ShapeDtypeStruct((rows, width // 2 + spare), jnp.float32)
    whole = pl.BlockSpec(memory_space=pltpu.VMEM)
    return pl.pallas_call(
        functools.partial(project_in_kernel, at=at),
        out_shape=(out, out),
        in_specs=[pl.BlockSpec(memory_space=pltpu.SMEM)]
        + [whole] * 5
        + [pl.BlockSpec(memory_space=pltpu.HBM)],
        out_specs=(whole, whole),
        scratch_shapes=[
            pltpu.VMEM((len(parts), rows, depth), jnp.bfloat16),
            pltpu.VMEM((weight.shape[0], width), jnp.bfloat16),
            pltpu.VMEM((rows, width), jnp.float32),
            pltpu.SemaphoreType.DMA((len(parts),)),
        ],
        cost_estimate=pl.CostEstimate(
            flops=2 * rows * weight.shape[0] * width,
            bytes_accessed=2 * weight.shape[0] * width + 8 * rows * out.shape[1],
            transcendentals=0,
        ),
        compiler_params=pltpu.CompilerParams(vmem_limit_bytes=24 << 20),
        name="project_kv" if with_squares else "project_q",
    )(place, *parts, gain, weight)


def project_out_kernel(
    place, mine_ref, other_ref, weight_hbm, own_ref, one_ref, two_ref, three_ref, weight_ref, semaphores
):
    half = mine_ref.shape[1]
    depth = own_ref.shape[1]
    over_last = (((1,), (1,)), ((), ()))
    outs = (own_ref, one_ref, two_ref, three_ref)
    copies = []
    for by in range(len(outs)):
        source = (place[2] + by) % len(outs)
        copies.append(
            pltpu.make_async_copy(
                weight_hbm.at[
                    pl.ds(source * depth, depth), pl.ds(weight_hbm.shape[1] - 2 * half, 2 * half)
                ],
                weight_ref.at[by],
                semaphores.at[by],
            )
        )
        copies[-1].start()
    for by, out_ref in enumerate(outs):
        copies[by].wait()
        result = lax.dot_general(
            mine_ref[...], weight_ref[by, :, :half], over_last, preferred_element_type=jnp.float32
        ) + lax.dot_general(
            other_ref[...], weight_ref[by, :, half:], over_last, preferred_element_type=jnp.float32
        )
        out_ref[...] = result.astype(out_ref.dtype)


def project_out(place, mine, other, weight):
    rows, half = mine.shape
    pieces = lax.axis_size("mp")
    depth = weight.shape[0] // pieces
    shape = jax.ShapeDtypeStruct((rows, depth), jnp.bfloat16)
    whole = pl.BlockSpec(memory_space=pltpu.VMEM)
    return pl.pallas_call(
        project_out_kernel,
        out_shape=[shape] * pieces,
        in_specs=[
            pl.BlockSpec(memory_space=pltpu.SMEM),
            whole,
            whole,
            pl.BlockSpec(memory_space=pltpu.HBM),
        ],
        out_specs=[whole] * pieces,
        scratch_shapes=[
            pltpu.VMEM((pieces, depth, 2 * half), jnp.bfloat16),
            pltpu.SemaphoreType.DMA((pieces,)),
        ],
        cost_estimate=pl.CostEstimate(
            flops=4 * rows * half * weight.shape[0],
            bytes_accessed=4 * half * weight.shape[0] + 2 * rows * weight.shape[0],
            transcendentals=0,
        ),
        compiler_params=pltpu.CompilerParams(vmem_limit_bytes=24 << 20),
        name="project_out",
    )(place, mine, other, weight)


def joined_kernel(place, first_ref, first_other_ref, second_ref, second_other_ref, out_ref):
    runs = first_ref.shape[1] // lane

    def write(even_ref, odd_ref):
        for run in range(runs):
            here = slice(run * lane, (run + 1) * lane)
            out_ref[:, 2 * run * lane : (2 * run + 1) * lane] = even_ref[:, here]
            out_ref[:, (2 * run + 1) * lane : (2 * run + 2) * lane] = odd_ref[:, here]

    @pl.when(place[0] == 0)
    def _():
        write(first_ref, first_other_ref)

    @pl.when(place[0] != 0)
    def _():
        write(second_other_ref, second_ref)


def joined(place, first, first_other, second, second_other):
    whole = pl.BlockSpec(memory_space=pltpu.VMEM)
    return pl.pallas_call(
        joined_kernel,
        out_shape=jax.ShapeDtypeStruct((first.shape[0], 2 * first.shape[1]), first.dtype),
        in_specs=[pl.BlockSpec(memory_space=pltpu.SMEM)] + [whole] * 4,
        out_specs=whole,
        name="joined",
    )(place, first, first_other, second, second_other)


def local(
    patches,
    merge_gain,
    merge_first,
    merge_second,
    text_embeds,
    positions,
    segments,
    norm_gain,
    query_weight,
    keyval_weight,
    out_weight,
):
    count = patches.shape[0]
    width = merge_gain.shape[0]
    blocks, rows_here, slice_width = text_embeds.shape
    seq_len = segments.shape[0]
    block_len = seq_len // blocks
    section_index = lax.axis_index("section")
    cycle_index = lax.axis_index("blk")
    model_index = lax.axis_index("mp")
    n_mp = lax.axis_size("mp")
    n_blk = lax.axis_size("blk")
    first_core = section_index == 0
    head_size = keyval_weight.shape[4]
    rows = blocks * rows_here
    layers = 2

    query_own = query_weight[0]
    keyval_own = keyval_weight[0].reshape(keyval_weight.shape[1], 2 * head_size)
    out_own = out_weight[0]
    heads_half = query_own.shape[1] // 2
    weight_half = query_own.shape[0] // 2

    def packed(core):
        keep_rows = slice(core * weight_half, (core + 1) * weight_half)
        query_rows, keyval_rows = query_own[keep_rows], keyval_own[keep_rows]
        out_rows = out_own[:, keep_rows].T
        halves = (core, 1 - core)
        parts = [keyval_rows[:, half * head_size : (half + 1) * head_size] for half in halves]
        parts += [query_rows[:, half * heads_half : (half + 1) * heads_half] for half in halves]
        parts += [out_rows[:, half * heads_half : (half + 1) * heads_half] for half in halves]
        return jnp.concatenate(parts, axis=1)

    for_first, for_second = packed(0), packed(1)
    weight_keep = jnp.where(first_core, for_first, for_second)
    weight_other = swapped(jnp.where(first_core, for_second, for_first))
    keyval_width = 2 * head_size
    keyval_shards, weight_full = [], []
    for home in range(layers):
        mine = jnp.where(section_index == home, weight_keep, weight_other)
        keyval_shards.append(mine[:, :keyval_width])
        sent_off = mine if home == 0 else mine[:, keyval_width:]
        weight_full.append(lax.all_gather(sent_off, "blk", axis=0, tiled=True))
    gain_half = norm_gain[0].reshape(-1, 2, lane)
    gain_keep = jnp.where(first_core, gain_half[:, 0], gain_half[:, 1])
    gain_send = jnp.where(first_core, gain_half[:, 1], gain_half[:, 0])
    gain_other = swapped(gain_send)
    gain_layers = [
        jnp.where(first_core, gain_keep, gain_other).reshape(n_mp, 1, -1),
        jnp.where(first_core, gain_other, gain_keep).reshape(n_mp, 1, -1),
    ]

    inner = merger_inner(patches, merge_gain, merge_first)
    place = jnp.stack([section_index, cycle_index, model_index]).astype(jnp.int32)
    merged_pieces = merger_outer(place, inner, swapped(inner), merge_second, n_blk, n_mp)
    merged_terms = lax.all_to_all(merged_pieces, ("blk", "mp"), 0, 0, tiled=True)

    row_where = (
        jnp.arange(blocks)[:, None] * block_len
        + cycle_index * rows_here
        + jnp.arange(rows_here)[None, :]
    ).reshape(-1)
    starts = jnp.stack([jnp.sum(segments < 1), jnp.sum(segments < 2)])
    scalars = jnp.concatenate([starts, jnp.stack([cycle_index, section_index])]).astype(jnp.int32)
    is_visual = (positions[None, :] == row_where[:, None]).astype(jnp.bfloat16)
    has_visual = jnp.max(is_visual, axis=1, keepdims=True)
    text_rows = my_half(text_embeds.reshape(rows, slice_width), 1, section_index)
    cosine, sine = rope_tables(row_where, head_size)
    merged_terms, scalars, is_visual, has_visual, text_rows, cosine, sine = (
        lax.optimization_barrier(
            (merged_terms, scalars, is_visual, has_visual, text_rows, cosine, sine)
        )
    )
    merged_mine = jnp.sum(merged_terms.astype(jnp.float32), axis=0).astype(jnp.bfloat16)
    merged = spread(merged_mine).reshape(n_blk * merged_mine.shape[0], -1)
    picked = jnp.dot(is_visual, merged, preferred_element_type=jnp.float32).astype(jnp.bfloat16)
    state = jnp.where(has_visual > 0, picked, text_rows)

    keyval_cosine = jnp.where(first_core, cosine, 1.0)
    keyval_sine = jnp.where(first_core, sine, 0.0)

    results = []
    for layer_index in range(layers):
        parts = [state] + [moved(state, "mp", by) for by in (1, 2, 3)]
        gain = gain_layers[layer_index]
        weight = weight_full[layer_index]
        if layer_index == 0:
            keyval_from, query_at = weight, keyval_width
        else:
            keyval_from, query_at = keyval_weight_full.reshape(-1, keyval_width), 0
        kept, sent = project_in(place, parts, gain, keyval_from, 0, keyval_width, True)
        total = kept + swapped(sent)
        shrink = lax.rsqrt(total[:, head_size : head_size + 1] / (n_mp * slice_width) + epsilon)
        keyval = rotate(total[:, :head_size] * shrink, keyval_cosine, keyval_sine).astype(jnp.bfloat16)
        keyval, parts = lax.optimization_barrier((keyval, parts))
        kept, sent = project_in(place, parts, gain, weight, query_at, 2 * heads_half, False)
        query = ((kept + swapped(sent)) * shrink).reshape(rows, -1, head_size)
        query = rotate(query, cosine[:, None, :], sine[:, None, :])
        query = query.astype(jnp.bfloat16).reshape(rows, heads_half)
        gathered = spread(keyval).reshape(n_blk, blocks, rows_here, head_size)
        attended = attention(scalars, query, gathered, swapped(gathered))
        attended_other = swapped(attended)
        own, *terms = project_out(place, attended, attended_other, weight)
        if layer_index + 1 < layers:
            own, shard = lax.optimization_barrier((own, keyval_shards[layer_index + 1]))
            keyval_weight_full = spread(shard)
        arrived = [moved(terms[by - 1], "mp", by) for by in (2, 1, 3)]
        total = state.astype(jnp.float32) + own.astype(jnp.float32)
        for part in arrived:
            total = total + part.astype(jnp.float32)
        state = total.astype(jnp.bfloat16)
        results.append(state)

    first_other = swapped(results[0])
    second_other = swapped(results[1])
    hidden = joined(place, results[0], first_other, results[1], second_other)
    return hidden.reshape(1, blocks, rows_here, slice_width)


def solution(mesh):
    return jax.shard_map(
        local,
        mesh=mesh,
        in_specs=(
            P("section", None),
            P(),
            P(None, ("blk", "mp")),
            P(("blk", "mp"), None),
            P(None, "blk", "mp"),
            P(),
            P(),
            P("section", None),
            P("section", "blk", "mp"),
            P("section", "blk", "mp", None, None),
            P("section", "mp", "blk"),
        ),
        out_specs=P("section", None, "blk", "mp"),
        check_vma=False,
    )
```

```python
import functools
import math

import jax
import jax.numpy as jnp
from jax import lax
from jax.experimental import pallas as pl
from jax.experimental.pallas import tpu as pltpu
from jax.sharding import PartitionSpec as P

epsilon = 1e-06
rope_base = 1000000.0
lane = 128


def moved(value, axis, by):
    size = lax.axis_size(axis)
    return lax.ppermute(value, axis, [(i, (i + by) % size) for i in range(size)])


def swapped(value):
    return lax.ppermute(value, "section", [(0, 1), (1, 0)])


def rope_tables(where_at, head_size):
    steps_half = jnp.arange(head_size // 2).astype(jnp.float32)
    inverse = jnp.exp(-jnp.log(rope_base) * 2.0 * steps_half / head_size)
    angles = where_at.astype(jnp.float32)[:, None] * inverse[None, :]
    return (jnp.cos(angles), jnp.sin(angles))


def rotate(values, cosine, sine):
    half = values.shape[-1] // 2
    first = values[..., :half]
    second = values[..., half:]
    return jnp.concatenate(
        [first * cosine - second * sine, second * cosine + first * sine], axis=-1
    )


def my_half(value, axis, section_index):
    shape = value.shape
    runs = shape[axis] // (2 * lane)
    split = value.reshape(shape[:axis] + (runs, 2, lane) + shape[axis + 1 :])
    index = [slice(None)] * split.ndim
    index[axis + 1] = 0
    even = split[tuple(index)]
    index[axis + 1] = 1
    odd = split[tuple(index)]
    picked = jnp.where(section_index == 0, even, odd)
    return picked.reshape(shape[:axis] + (runs * lane,) + shape[axis + 1 :])


def spread(value):
    size = lax.axis_size("blk")
    copies = jnp.broadcast_to(value[None], (size,) + value.shape)
    return lax.all_to_all(copies, "blk", 0, 0, tiled=True)


def attention_kernel(scalars, query_ref, mine_ref, other_ref, out_ref, *, chunk_runs):
    runs, blocks, run, head_size = mine_ref.shape
    heads = query_ref.shape[1] // head_size
    rows = heads * run
    chunk = chunk_runs * run
    per_block = runs // chunk_runs
    block_len = runs * run
    start_one, start_two, cycle, section = scalars[0], scalars[1], scalars[2], scalars[3]
    factor = 1.0 / head_size**0.5 * math.log2(math.e)

    def stripes(key_ref, value_ref):
        def stripe(block, carry):
            row_from = pl.multiple_of(block * run, run)
            first = block * block_len + cycle * run
            here = query_ref[pl.ds(row_from, run), :]
            stacked = jnp.concatenate(
                [here[:, h * head_size : (h + 1) * head_size] for h in range(heads)], axis=0
            )
            row_at = lax.broadcasted_iota(jnp.int32, (rows, 1), 0) % run + first
            row_start = jnp.where(
                row_at >= start_two, start_two, jnp.where(row_at >= start_one, start_one, 0)
            )
            stripe_start = jnp.where(
                first >= start_two, start_two, jnp.where(first >= start_one, start_one, 0)
            )

            def step(index, state):
                top, total, mixed = state
                in_block = index // per_block
                from_run = (index % per_block) * chunk_runs
                key = key_ref[pl.ds(from_run, chunk_runs), in_block].reshape(chunk, head_size)
                value = value_ref[pl.ds(from_run, chunk_runs), in_block].reshape(chunk, head_size)
                scores = lax.dot_general(
                    stacked, key, (((1,), (1,)), ((), ())), preferred_element_type=jnp.float32
                )
                key_at = lax.broadcasted_iota(jnp.int32, (1, chunk), 1) + index * chunk
                allowed = (key_at <= row_at) & (key_at >= row_start)
                scores = jnp.where(allowed, scores * factor, -1e30)
                new_top = jnp.maximum(top, jnp.max(scores, axis=1, keepdims=True))
                fade = jnp.exp2(top - new_top)
                weights = jnp.exp2(scores - new_top)
                total = total * fade + jnp.sum(weights, axis=1, keepdims=True)
                mixed = mixed * fade + jnp.dot(
                    weights.astype(jnp.bfloat16), value, preferred_element_type=jnp.float32
                )
                return new_top, total, mixed

            state = (
                jnp.full((rows, 1), -1e30, jnp.float32),
                jnp.zeros((rows, 1), jnp.float32),
                jnp.zeros((rows, head_size), jnp.float32),
            )
            _, total, mixed = lax.fori_loop(
                stripe_start // chunk, (first + run - 1) // chunk + 1, step, state
            )
            result = (mixed / total).astype(out_ref.dtype)
            for h in range(heads):
                out_ref[pl.ds(row_from, run), h * head_size : (h + 1) * head_size] = result[
                    h * run : (h + 1) * run
                ]
            return carry

        lax.fori_loop(0, blocks, stripe, 0)

    @pl.when(section == 0)
    def _():
        stripes(mine_ref, other_ref)

    @pl.when(section != 0)
    def _():
        stripes(other_ref, mine_ref)


def attention(scalars, query, mine, other):
    whole = pl.BlockSpec(memory_space=pltpu.VMEM)
    return pl.pallas_call(
        functools.partial(attention_kernel, chunk_runs=mine.shape[0]),
        out_shape=jax.ShapeDtypeStruct(query.shape, query.dtype),
        in_specs=[pl.BlockSpec(memory_space=pltpu.SMEM), whole, whole, whole],
        out_specs=whole,
        cost_estimate=pl.CostEstimate(
            flops=4 * query.size * mine.size // query.shape[1] // 4,
            bytes_accessed=2 * (2 * query.size + 2 * mine.size),
            transcendentals=0,
        ),
        name="attention",
    )(scalars, query, mine, other)


def merger_kernel(patches_ref, gain_ref, weight_ref, out_ref):
    width = gain_ref.shape[1]
    total = jnp.zeros(out_ref.shape, jnp.float32)
    for at in range(0, patches_ref.shape[1], width):
        piece = patches_ref[:, at : at + width].astype(jnp.float32)
        centered = piece - jnp.mean(piece, axis=1, keepdims=True)
        variance = jnp.mean(centered * centered, axis=1, keepdims=True)
        normed = (centered * lax.rsqrt(variance + epsilon) * gain_ref[...]).astype(jnp.bfloat16)
        total = total + jnp.dot(
            normed, weight_ref[at : at + width, :], preferred_element_type=jnp.float32
        )
    out_ref[...] = (0.5 * total * (1.0 + lax.erf(total * math.sqrt(0.5)))).astype(out_ref.dtype)


def merger_inner(patches, merge_gain, merge_first):
    whole = pl.BlockSpec(memory_space=pltpu.VMEM)
    rows, units = patches.shape[0], merge_first.shape[1]
    return pl.pallas_call(
        merger_kernel,
        out_shape=jax.ShapeDtypeStruct((rows, units), jnp.bfloat16),
        in_specs=[whole, whole, whole],
        out_specs=whole,
        cost_estimate=pl.CostEstimate(
            flops=2 * rows * merge_first.size,
            bytes_accessed=2 * (patches.size + merge_first.size),
            transcendentals=0,
        ),
        name="merger_inner",
    )(patches, merge_gain.reshape(1, -1), merge_first)


def merger_outer_kernel(place, mine_ref, other_ref, weight_ref, out_ref):
    section = place[0]
    pieces, share, depth = out_ref.shape
    tokens = mine_ref.shape[0]
    runs = weight_ref.shape[1] // (2 * lane)
    slices = runs * lane // depth
    weight = jnp.concatenate(
        [
            weight_ref[:, pl.ds(pl.multiple_of((2 * run + section) * lane, lane), lane)]
            for run in range(runs)
        ],
        axis=1,
    )
    for inner_ref, core in ((mine_ref, section), (other_ref, 1 - section)):
        result = jnp.dot(inner_ref[...], weight, preferred_element_type=jnp.float32)
        result = result.astype(out_ref.dtype)
        for owner in range(tokens // share):
            for piece in range(slices):
                out_ref[(core * (tokens // share) + owner) * slices + piece] = result[
                    owner * share : (owner + 1) * share, piece * depth : (piece + 1) * depth
                ]


def merger_outer(place, mine, other, merge_second, n_blk, n_mp):
    whole = pl.BlockSpec(memory_space=pltpu.VMEM)
    share = 2 * mine.shape[0] // n_blk
    depth = merge_second.shape[1] // 2 // n_mp
    return pl.pallas_call(
        merger_outer_kernel,
        out_shape=jax.ShapeDtypeStruct((n_blk * n_mp, share, depth), jnp.bfloat16),
        in_specs=[pl.BlockSpec(memory_space=pltpu.SMEM), whole, whole, whole],
        out_specs=whole,
        name="merger_outer",
    )(place, mine, other, merge_second)


def project_in_kernel(
    place,
    own_ref,
    from_one,
    from_two,
    from_three,
    gain_ref,
    weight_hbm,
    kept_ref,
    sent_ref,
    rows_ref,
    weight_ref,
    sums_ref,
    semaphores,
    *,
    at,
):
    pieces, _, depth = gain_ref.shape
    half = weight_ref.shape[1] // 2
    copies = []
    for piece in range(pieces):
        deep = pl.ds(piece * depth, depth)
        copies.append(
            pltpu.make_async_copy(
                weight_hbm.at[deep, pl.ds(at, 2 * half)], weight_ref.at[deep], semaphores.at[piece]
            )
        )
        copies[-1].start()
    squares = jnp.zeros((own_ref.shape[0], 1), jnp.float32)
    for by, part_ref in enumerate((own_ref, from_one, from_two, from_three)):
        source = (place[2] + pieces - by) % pieces
        part = part_ref[...].astype(jnp.float32)
        if kept_ref.shape[1] > half:
            squares = squares + jnp.sum(part * part, axis=1, keepdims=True)
        rows_ref[source] = (part * gain_ref[source]).astype(jnp.bfloat16)
    if kept_ref.shape[1] > half:
        squares = jnp.broadcast_to(squares, (squares.shape[0], lane))
        kept_ref[:, half:] = squares
        sent_ref[:, half:] = squares
    for piece in range(pieces):
        copies[piece].wait()
        result = jnp.dot(
            rows_ref[piece],
            weight_ref[piece * depth : (piece + 1) * depth, :],
            preferred_element_type=jnp.float32,
        )
        if piece > 0:
            result = result + sums_ref[...]
        if piece < pieces - 1:
            sums_ref[...] = result
    kept_ref[:, :half] = result[:, :half]
    sent_ref[:, :half] = result[:, half:]


def project_in(place, parts, gain, weight, at, width, with_squares):
    rows, depth = parts[0].shape
    spare = lane if with_squares else 0
    out = jax.ShapeDtypeStruct((rows, width // 2 + spare), jnp.float32)
    whole = pl.BlockSpec(memory_space=pltpu.VMEM)
    return pl.pallas_call(
        functools.partial(project_in_kernel, at=at),
        out_shape=(out, out),
        in_specs=[pl.BlockSpec(memory_space=pltpu.SMEM)]
        + [whole] * 5
        + [pl.BlockSpec(memory_space=pltpu.HBM)],
        out_specs=(whole, whole),
        scratch_shapes=[
            pltpu.VMEM((len(parts), rows, depth), jnp.bfloat16),
            pltpu.VMEM((weight.shape[0], width), jnp.bfloat16),
            pltpu.VMEM((rows, width), jnp.float32),
            pltpu.SemaphoreType.DMA((len(parts),)),
        ],
        cost_estimate=pl.CostEstimate(
            flops=2 * rows * weight.shape[0] * width,
            bytes_accessed=2 * weight.shape[0] * width + 8 * rows * out.shape[1],
            transcendentals=0,
        ),
        compiler_params=pltpu.CompilerParams(vmem_limit_bytes=48 << 20),
        name="project_kv" if with_squares else "project_q",
    )(place, *parts, gain, weight)


def project_out_kernel(
    place, mine_ref, other_ref, weight_hbm, own_ref, one_ref, two_ref, three_ref, weight_ref, semaphores
):
    half = mine_ref.shape[1]
    depth = own_ref.shape[1]
    over_last = (((1,), (1,)), ((), ()))
    outs = (own_ref, one_ref, two_ref, three_ref)
    copies = []
    for by in range(len(outs)):
        source = (place[2] + by) % len(outs)
        copies.append(
            pltpu.make_async_copy(
                weight_hbm.at[
                    pl.ds(source * depth, depth), pl.ds(weight_hbm.shape[1] - 2 * half, 2 * half)
                ],
                weight_ref.at[by],
                semaphores.at[by],
            )
        )
        copies[-1].start()
    for by, out_ref in enumerate(outs):
        copies[by].wait()
        result = lax.dot_general(
            mine_ref[...], weight_ref[by, :, :half], over_last, preferred_element_type=jnp.float32
        ) + lax.dot_general(
            other_ref[...], weight_ref[by, :, half:], over_last, preferred_element_type=jnp.float32
        )
        out_ref[...] = result.astype(out_ref.dtype)


def project_out(place, mine, other, weight):
    rows, half = mine.shape
    pieces = lax.axis_size("mp")
    depth = weight.shape[0] // pieces
    shape = jax.ShapeDtypeStruct((rows, depth), jnp.bfloat16)
    whole = pl.BlockSpec(memory_space=pltpu.VMEM)
    return pl.pallas_call(
        project_out_kernel,
        out_shape=[shape] * pieces,
        in_specs=[
            pl.BlockSpec(memory_space=pltpu.SMEM),
            whole,
            whole,
            pl.BlockSpec(memory_space=pltpu.HBM),
        ],
        out_specs=[whole] * pieces,
        scratch_shapes=[
            pltpu.VMEM((pieces, depth, 2 * half), jnp.bfloat16),
            pltpu.SemaphoreType.DMA((pieces,)),
        ],
        cost_estimate=pl.CostEstimate(
            flops=4 * rows * half * weight.shape[0],
            bytes_accessed=4 * half * weight.shape[0] + 2 * rows * weight.shape[0],
            transcendentals=0,
        ),
        compiler_params=pltpu.CompilerParams(vmem_limit_bytes=48 << 20),
        name="project_out",
    )(place, mine, other, weight)


def joined_kernel(place, first_ref, first_other_ref, second_ref, second_other_ref, out_ref):
    runs = first_ref.shape[1] // lane

    def write(even_ref, odd_ref):
        for run in range(runs):
            here = slice(run * lane, (run + 1) * lane)
            out_ref[:, 2 * run * lane : (2 * run + 1) * lane] = even_ref[:, here]
            out_ref[:, (2 * run + 1) * lane : (2 * run + 2) * lane] = odd_ref[:, here]

    @pl.when(place[0] == 0)
    def _():
        write(first_ref, first_other_ref)

    @pl.when(place[0] != 0)
    def _():
        write(second_other_ref, second_ref)


def joined(place, first, first_other, second, second_other):
    whole = pl.BlockSpec(memory_space=pltpu.VMEM)
    return pl.pallas_call(
        joined_kernel,
        out_shape=jax.ShapeDtypeStruct((first.shape[0], 2 * first.shape[1]), first.dtype),
        in_specs=[pl.BlockSpec(memory_space=pltpu.SMEM)] + [whole] * 4,
        out_specs=whole,
        name="joined",
    )(place, first, first_other, second, second_other)


def local(
    patches,
    merge_gain,
    merge_first,
    merge_second,
    text_embeds,
    positions,
    segments,
    norm_gain,
    query_weight,
    keyval_weight,
    out_weight,
):
    count = patches.shape[0]
    width = merge_gain.shape[0]
    blocks, rows_here, slice_width = text_embeds.shape
    seq_len = segments.shape[0]
    block_len = seq_len // blocks
    section_index = lax.axis_index("section")
    cycle_index = lax.axis_index("blk")
    model_index = lax.axis_index("mp")
    n_mp = lax.axis_size("mp")
    n_blk = lax.axis_size("blk")
    first_core = section_index == 0
    head_size = keyval_weight.shape[4]
    rows = blocks * rows_here
    layers = 2

    query_own = query_weight[0]
    keyval_own = keyval_weight[0].reshape(keyval_weight.shape[1], 2 * head_size)
    out_own = out_weight[0]
    heads_half = query_own.shape[1] // 2
    weight_half = query_own.shape[0] // 2

    def packed(core):
        keep_rows = slice(core * weight_half, (core + 1) * weight_half)
        query_rows, keyval_rows = query_own[keep_rows], keyval_own[keep_rows]
        out_rows = out_own[:, keep_rows].T
        halves = (core, 1 - core)
        parts = [keyval_rows[:, half * head_size : (half + 1) * head_size] for half in halves]
        parts += [query_rows[:, half * heads_half : (half + 1) * heads_half] for half in halves]
        parts += [out_rows[:, half * heads_half : (half + 1) * heads_half] for half in halves]
        return jnp.concatenate(parts, axis=1)

    for_first, for_second = packed(0), packed(1)
    weight_keep = jnp.where(first_core, for_first, for_second)
    weight_other = swapped(jnp.where(first_core, for_second, for_first))
    keyval_width = 2 * head_size
    keyval_shards, weight_full = [], []
    for home in range(layers):
        mine = jnp.where(section_index == home, weight_keep, weight_other)
        keyval_shards.append(mine[:, :keyval_width])
        sent_off = mine if home == 0 else mine[:, keyval_width:]
        weight_full.append(lax.all_gather(sent_off, "blk", axis=0, tiled=True))
    gain_half = norm_gain[0].reshape(-1, 2, lane)
    gain_keep = jnp.where(first_core, gain_half[:, 0], gain_half[:, 1])
    gain_send = jnp.where(first_core, gain_half[:, 1], gain_half[:, 0])
    gain_other = swapped(gain_send)
    gain_layers = [
        jnp.where(first_core, gain_keep, gain_other).reshape(n_mp, 1, -1),
        jnp.where(first_core, gain_other, gain_keep).reshape(n_mp, 1, -1),
    ]

    inner = merger_inner(patches, merge_gain, merge_first)
    place = jnp.stack([section_index, cycle_index, model_index]).astype(jnp.int32)
    merged_pieces = merger_outer(place, inner, swapped(inner), merge_second, n_blk, n_mp)
    merged_terms = lax.all_to_all(merged_pieces, ("blk", "mp"), 0, 0, tiled=True)

    row_where = (
        jnp.arange(blocks)[:, None] * block_len
        + cycle_index * rows_here
        + jnp.arange(rows_here)[None, :]
    ).reshape(-1)
    starts = jnp.stack([jnp.sum(segments < 1), jnp.sum(segments < 2)])
    scalars = jnp.concatenate([starts, jnp.stack([cycle_index, section_index])]).astype(jnp.int32)
    is_visual = (positions[None, :] == row_where[:, None]).astype(jnp.bfloat16)
    has_visual = jnp.max(is_visual, axis=1, keepdims=True)
    text_rows = my_half(text_embeds.reshape(rows, slice_width), 1, section_index)
    cosine, sine = rope_tables(row_where, head_size)
    merged_terms, scalars, is_visual, has_visual, text_rows, cosine, sine = (
        lax.optimization_barrier(
            (merged_terms, scalars, is_visual, has_visual, text_rows, cosine, sine)
        )
    )
    merged_mine = jnp.sum(merged_terms.astype(jnp.float32), axis=0).astype(jnp.bfloat16)
    merged = spread(merged_mine).reshape(n_blk * merged_mine.shape[0], -1)
    picked = jnp.dot(is_visual, merged, preferred_element_type=jnp.float32).astype(jnp.bfloat16)
    state = jnp.where(has_visual > 0, picked, text_rows)

    keyval_cosine = jnp.where(first_core, cosine, 1.0)
    keyval_sine = jnp.where(first_core, sine, 0.0)

    results = []
    for layer_index in range(layers):
        parts = [state] + [moved(state, "mp", by) for by in (1, 2, 3)]
        gain = gain_layers[layer_index]
        weight = weight_full[layer_index]
        if layer_index == 0:
            keyval_from, query_at = weight, keyval_width
        else:
            keyval_from, query_at = keyval_weight_full.reshape(-1, keyval_width), 0
        kept, sent = project_in(place, parts, gain, keyval_from, 0, keyval_width, True)
        total = kept + swapped(sent)
        shrink = lax.rsqrt(total[:, head_size : head_size + 1] / (n_mp * slice_width) + epsilon)
        keyval = rotate(total[:, :head_size] * shrink, keyval_cosine, keyval_sine).astype(jnp.bfloat16)
        keyval, parts = lax.optimization_barrier((keyval, parts))
        kept, sent = project_in(place, parts, gain, weight, query_at, 2 * heads_half, False)
        query = ((kept + swapped(sent)) * shrink).reshape(rows, -1, head_size)
        query = rotate(query, cosine[:, None, :], sine[:, None, :])
        query = query.astype(jnp.bfloat16).reshape(rows, heads_half)
        gathered = spread(keyval).reshape(n_blk, blocks, rows_here, head_size)
        attended = attention(scalars, query, gathered, swapped(gathered))
        attended_other = swapped(attended)
        own, *terms = project_out(place, attended, attended_other, weight)
        if layer_index + 1 < layers:
            own, shard = lax.optimization_barrier((own, keyval_shards[layer_index + 1]))
            keyval_weight_full = spread(shard)
        arrived = [moved(terms[by - 1], "mp", by) for by in (2, 1, 3)]
        total = state.astype(jnp.float32) + own.astype(jnp.float32)
        for part in arrived:
            total = total + part.astype(jnp.float32)
        state = total.astype(jnp.bfloat16)
        results.append(state)

    first_other = swapped(results[0])
    second_other = swapped(results[1])
    hidden = joined(place, results[0], first_other, results[1], second_other)
    return hidden.reshape(1, blocks, rows_here, slice_width)


def solution(mesh):
    return jax.shard_map(
        local,
        mesh=mesh,
        in_specs=(
            P("section", None),
            P(),
            P(None, ("blk", "mp")),
            P(("blk", "mp"), None),
            P(None, "blk", "mp"),
            P(),
            P(),
            P("section", None),
            P("section", "blk", "mp"),
            P("section", "blk", "mp", None, None),
            P("section", "mp", "blk"),
        ),
        out_specs=P("section", None, "blk", "mp"),
        check_vma=False,
    )
```

```python
import functools
import math

import jax
import jax.numpy as jnp
from jax import lax
from jax.experimental import pallas as pl
from jax.experimental.pallas import tpu as pltpu
from jax.sharding import PartitionSpec as P

epsilon = 1e-06
rope_base = 1000000.0
lane = 128


def moved(value, axis, by):
    size = lax.axis_size(axis)
    return lax.ppermute(value, axis, [(i, (i + by) % size) for i in range(size)])


def swapped(value):
    return lax.ppermute(value, "section", [(0, 1), (1, 0)])


def rope_tables(where_at, head_size):
    steps_half = jnp.arange(head_size // 2).astype(jnp.float32)
    inverse = jnp.exp(-jnp.log(rope_base) * 2.0 * steps_half / head_size)
    angles = where_at.astype(jnp.float32)[:, None] * inverse[None, :]
    return (jnp.cos(angles), jnp.sin(angles))


def rotate(values, cosine, sine):
    half = values.shape[-1] // 2
    first = values[..., :half]
    second = values[..., half:]
    return jnp.concatenate(
        [first * cosine - second * sine, second * cosine + first * sine], axis=-1
    )


def my_half(value, axis, section_index):
    shape = value.shape
    runs = shape[axis] // (2 * lane)
    split = value.reshape(shape[:axis] + (runs, 2, lane) + shape[axis + 1 :])
    index = [slice(None)] * split.ndim
    index[axis + 1] = 0
    even = split[tuple(index)]
    index[axis + 1] = 1
    odd = split[tuple(index)]
    picked = jnp.where(section_index == 0, even, odd)
    return picked.reshape(shape[:axis] + (runs * lane,) + shape[axis + 1 :])


def spread(value):
    size = lax.axis_size("blk")
    copies = jnp.broadcast_to(value[None], (size,) + value.shape)
    return lax.all_to_all(copies, "blk", 0, 0, tiled=True)


def attention_kernel(scalars, query_ref, mine_ref, other_ref, out_ref, *, chunk_runs):
    runs, blocks, run, head_size = mine_ref.shape
    heads = query_ref.shape[1] // head_size
    rows = heads * run
    chunk = chunk_runs * run
    per_block = runs // chunk_runs
    block_len = runs * run
    start_one, start_two, cycle, section = scalars[0], scalars[1], scalars[2], scalars[3]
    factor = 1.0 / head_size**0.5 * math.log2(math.e)

    def stripes(key_ref, value_ref):
        def stripe(block, carry):
            row_from = pl.multiple_of(block * run, run)
            first = block * block_len + cycle * run
            here = query_ref[pl.ds(row_from, run), :]
            stacked = jnp.concatenate(
                [here[:, h * head_size : (h + 1) * head_size] for h in range(heads)], axis=0
            )
            row_at = lax.broadcasted_iota(jnp.int32, (rows, 1), 0) % run + first
            row_start = jnp.where(
                row_at >= start_two, start_two, jnp.where(row_at >= start_one, start_one, 0)
            )
            stripe_start = jnp.where(
                first >= start_two, start_two, jnp.where(first >= start_one, start_one, 0)
            )

            def step(index, state):
                top, total, mixed = state
                in_block = index // per_block
                from_run = (index % per_block) * chunk_runs
                key = key_ref[pl.ds(from_run, chunk_runs), in_block].reshape(chunk, head_size)
                value = value_ref[pl.ds(from_run, chunk_runs), in_block].reshape(chunk, head_size)
                scores = lax.dot_general(
                    stacked, key, (((1,), (1,)), ((), ())), preferred_element_type=jnp.float32
                )
                key_at = lax.broadcasted_iota(jnp.int32, (1, chunk), 1) + index * chunk
                allowed = (key_at <= row_at) & (key_at >= row_start)
                scores = jnp.where(allowed, scores * factor, -1e30)
                new_top = jnp.maximum(top, jnp.max(scores, axis=1, keepdims=True))
                fade = jnp.exp2(top - new_top)
                weights = jnp.exp2(scores - new_top)
                total = total * fade + jnp.sum(weights, axis=1, keepdims=True)
                mixed = mixed * fade + jnp.dot(
                    weights.astype(jnp.bfloat16), value, preferred_element_type=jnp.float32
                )
                return new_top, total, mixed

            state = (
                jnp.full((rows, 1), -1e30, jnp.float32),
                jnp.zeros((rows, 1), jnp.float32),
                jnp.zeros((rows, head_size), jnp.float32),
            )
            _, total, mixed = lax.fori_loop(
                stripe_start // chunk, (first + run - 1) // chunk + 1, step, state
            )
            result = (mixed / total).astype(out_ref.dtype)
            for h in range(heads):
                out_ref[pl.ds(row_from, run), h * head_size : (h + 1) * head_size] = result[
                    h * run : (h + 1) * run
                ]
            return carry

        lax.fori_loop(0, blocks, stripe, 0)

    @pl.when(section == 0)
    def _():
        stripes(mine_ref, other_ref)

    @pl.when(section != 0)
    def _():
        stripes(other_ref, mine_ref)


def attention(scalars, query, mine, other):
    whole = pl.BlockSpec(memory_space=pltpu.VMEM)
    return pl.pallas_call(
        functools.partial(attention_kernel, chunk_runs=mine.shape[0]),
        out_shape=jax.ShapeDtypeStruct(query.shape, query.dtype),
        in_specs=[pl.BlockSpec(memory_space=pltpu.SMEM), whole, whole, whole],
        out_specs=whole,
        cost_estimate=pl.CostEstimate(
            flops=4 * query.size * mine.size // query.shape[1] // 4,
            bytes_accessed=2 * (2 * query.size + 2 * mine.size),
            transcendentals=0,
        ),
        name="attention",
    )(scalars, query, mine, other)


def merger_kernel(patches_ref, gain_ref, weight_ref, out_ref):
    width = gain_ref.shape[1]
    total = jnp.zeros(out_ref.shape, jnp.float32)
    for at in range(0, patches_ref.shape[1], width):
        piece = patches_ref[:, at : at + width].astype(jnp.float32)
        centered = piece - jnp.mean(piece, axis=1, keepdims=True)
        variance = jnp.mean(centered * centered, axis=1, keepdims=True)
        normed = (centered * lax.rsqrt(variance + epsilon) * gain_ref[...]).astype(jnp.bfloat16)
        total = total + jnp.dot(
            normed, weight_ref[at : at + width, :], preferred_element_type=jnp.float32
        )
    out_ref[...] = (0.5 * total * (1.0 + lax.erf(total * math.sqrt(0.5)))).astype(out_ref.dtype)


def merger_inner(patches, merge_gain, merge_first):
    whole = pl.BlockSpec(memory_space=pltpu.VMEM)
    rows, units = patches.shape[0], merge_first.shape[1]
    return pl.pallas_call(
        merger_kernel,
        out_shape=jax.ShapeDtypeStruct((rows, units), jnp.bfloat16),
        in_specs=[whole, whole, whole],
        out_specs=whole,
        cost_estimate=pl.CostEstimate(
            flops=2 * rows * merge_first.size,
            bytes_accessed=2 * (patches.size + merge_first.size),
            transcendentals=0,
        ),
        name="merger_inner",
    )(patches, merge_gain.reshape(1, -1), merge_first)


def merger_outer_kernel(place, mine_ref, other_ref, weight_ref, out_ref):
    section = place[0]
    pieces, share, depth = out_ref.shape
    tokens = mine_ref.shape[0]
    runs = weight_ref.shape[1] // (2 * lane)
    slices = runs * lane // depth
    weight = jnp.concatenate(
        [
            weight_ref[:, pl.ds(pl.multiple_of((2 * run + section) * lane, lane), lane)]
            for run in range(runs)
        ],
        axis=1,
    )
    for inner_ref, core in ((mine_ref, section), (other_ref, 1 - section)):
        result = jnp.dot(inner_ref[...], weight, preferred_element_type=jnp.float32)
        result = result.astype(out_ref.dtype)
        for owner in range(tokens // share):
            for piece in range(slices):
                out_ref[(core * (tokens // share) + owner) * slices + piece] = result[
                    owner * share : (owner + 1) * share, piece * depth : (piece + 1) * depth
                ]


def merger_outer(place, mine, other, merge_second, n_blk, n_mp):
    whole = pl.BlockSpec(memory_space=pltpu.VMEM)
    share = 2 * mine.shape[0] // n_blk
    depth = merge_second.shape[1] // 2 // n_mp
    return pl.pallas_call(
        merger_outer_kernel,
        out_shape=jax.ShapeDtypeStruct((n_blk * n_mp, share, depth), jnp.bfloat16),
        in_specs=[pl.BlockSpec(memory_space=pltpu.SMEM), whole, whole, whole],
        out_specs=whole,
        name="merger_outer",
    )(place, mine, other, merge_second)


def project_in_kernel(
    place,
    own_ref,
    from_one,
    from_two,
    from_three,
    gain_ref,
    weight_hbm,
    kept_ref,
    sent_ref,
    rows_ref,
    weight_ref,
    sums_ref,
    semaphores,
    *,
    at,
):
    pieces, _, depth = gain_ref.shape
    half = weight_ref.shape[1] // 2
    copies = []
    for piece in range(pieces):
        deep = pl.ds(piece * depth, depth)
        copies.append(
            pltpu.make_async_copy(
                weight_hbm.at[deep, pl.ds(at, 2 * half)], weight_ref.at[deep], semaphores.at[piece]
            )
        )
        copies[-1].start()
    squares = jnp.zeros((own_ref.shape[0], 1), jnp.float32)
    for by, part_ref in enumerate((own_ref, from_one, from_two, from_three)):
        source = (place[2] + pieces - by) % pieces
        part = part_ref[...].astype(jnp.float32)
        if kept_ref.shape[1] > half:
            squares = squares + jnp.sum(part * part, axis=1, keepdims=True)
        rows_ref[source] = (part * gain_ref[source]).astype(jnp.bfloat16)
    if kept_ref.shape[1] > half:
        squares = jnp.broadcast_to(squares, (squares.shape[0], lane))
        kept_ref[:, half:] = squares
        sent_ref[:, half:] = squares
    for piece in range(pieces):
        copies[piece].wait()
        result = jnp.dot(
            rows_ref[piece],
            weight_ref[piece * depth : (piece + 1) * depth, :],
            preferred_element_type=jnp.float32,
        )
        if piece > 0:
            result = result + sums_ref[...]
        if piece < pieces - 1:
            sums_ref[...] = result
    kept_ref[:, :half] = result[:, :half]
    sent_ref[:, :half] = result[:, half:]


def project_in(place, parts, gain, weight, at, width, with_squares):
    rows, depth = parts[0].shape
    spare = lane if with_squares else 0
    out = jax.ShapeDtypeStruct((rows, width // 2 + spare), jnp.float32)
    whole = pl.BlockSpec(memory_space=pltpu.VMEM)
    return pl.pallas_call(
        functools.partial(project_in_kernel, at=at),
        out_shape=(out, out),
        in_specs=[pl.BlockSpec(memory_space=pltpu.SMEM)]
        + [whole] * 5
        + [pl.BlockSpec(memory_space=pltpu.HBM)],
        out_specs=(whole, whole),
        scratch_shapes=[
            pltpu.VMEM((len(parts), rows, depth), jnp.bfloat16),
            pltpu.VMEM((weight.shape[0], width), jnp.bfloat16),
            pltpu.VMEM((rows, width), jnp.float32),
            pltpu.SemaphoreType.DMA((len(parts),)),
        ],
        cost_estimate=pl.CostEstimate(
            flops=2 * rows * weight.shape[0] * width,
            bytes_accessed=2 * weight.shape[0] * width + 8 * rows * out.shape[1],
            transcendentals=0,
        ),
        compiler_params=pltpu.CompilerParams(vmem_limit_bytes=48 << 20),
        name="project_kv" if with_squares else "project_q",
    )(place, *parts, gain, weight)


def keyval_rotate_kernel(kept_ref, arrived_ref, cosine_ref, sine_ref, out_ref, shrink_ref, *, features):
    total = kept_ref[...] + arrived_ref[...]
    shrink = lax.rsqrt(total[:, lane:] / features + epsilon)
    shrink_ref[...] = shrink
    values = total[:, :lane] * shrink
    turned = pltpu.roll(values, lane // 2, 1)
    result = (values * cosine_ref[...] + turned * sine_ref[...]).astype(out_ref.dtype)
    for copy in range(out_ref.shape[0]):
        out_ref[copy] = result


def keyval_rotate(kept, arrived, cosine, sine, copies, features):
    whole = pl.BlockSpec(memory_space=pltpu.VMEM)
    rows = kept.shape[0]
    return pl.pallas_call(
        functools.partial(keyval_rotate_kernel, features=features),
        out_shape=(
            jax.ShapeDtypeStruct((copies, rows, lane), jnp.bfloat16),
            jax.ShapeDtypeStruct((rows, lane), jnp.float32),
        ),
        in_specs=[whole] * 4,
        out_specs=(whole, whole),
        name="keyval_rotate",
    )(kept, arrived, cosine, sine)


def project_out_kernel(
    place, mine_ref, other_ref, weight_hbm, own_ref, one_ref, two_ref, three_ref, weight_ref, semaphores
):
    half = mine_ref.shape[1]
    depth = own_ref.shape[1]
    over_last = (((1,), (1,)), ((), ()))
    outs = (own_ref, one_ref, two_ref, three_ref)
    copies = []
    for by in range(len(outs)):
        source = (place[2] + by) % len(outs)
        copies.append(
            pltpu.make_async_copy(
                weight_hbm.at[
                    pl.ds(source * depth, depth), pl.ds(weight_hbm.shape[1] - 2 * half, 2 * half)
                ],
                weight_ref.at[by],
                semaphores.at[by],
            )
        )
        copies[-1].start()
    for by, out_ref in enumerate(outs):
        copies[by].wait()
        result = lax.dot_general(
            mine_ref[...], weight_ref[by, :, :half], over_last, preferred_element_type=jnp.float32
        ) + lax.dot_general(
            other_ref[...], weight_ref[by, :, half:], over_last, preferred_element_type=jnp.float32
        )
        out_ref[...] = result.astype(out_ref.dtype)


def project_out(place, mine, other, weight):
    rows, half = mine.shape
    pieces = lax.axis_size("mp")
    depth = weight.shape[0] // pieces
    shape = jax.ShapeDtypeStruct((rows, depth), jnp.bfloat16)
    whole = pl.BlockSpec(memory_space=pltpu.VMEM)
    return pl.pallas_call(
        project_out_kernel,
        out_shape=[shape] * pieces,
        in_specs=[
            pl.BlockSpec(memory_space=pltpu.SMEM),
            whole,
            whole,
            pl.BlockSpec(memory_space=pltpu.HBM),
        ],
        out_specs=[whole] * pieces,
        scratch_shapes=[
            pltpu.VMEM((pieces, depth, 2 * half), jnp.bfloat16),
            pltpu.SemaphoreType.DMA((pieces,)),
        ],
        cost_estimate=pl.CostEstimate(
            flops=4 * rows * half * weight.shape[0],
            bytes_accessed=4 * half * weight.shape[0] + 2 * rows * weight.shape[0],
            transcendentals=0,
        ),
        compiler_params=pltpu.CompilerParams(vmem_limit_bytes=48 << 20),
        name="project_out",
    )(place, mine, other, weight)


def joined_kernel(place, first_ref, first_other_ref, second_ref, second_other_ref, out_ref):
    runs = first_ref.shape[1] // lane

    def write(even_ref, odd_ref):
        for run in range(runs):
            here = slice(run * lane, (run + 1) * lane)
            out_ref[:, 2 * run * lane : (2 * run + 1) * lane] = even_ref[:, here]
            out_ref[:, (2 * run + 1) * lane : (2 * run + 2) * lane] = odd_ref[:, here]

    @pl.when(place[0] == 0)
    def _():
        write(first_ref, first_other_ref)

    @pl.when(place[0] != 0)
    def _():
        write(second_other_ref, second_ref)


def joined(place, first, first_other, second, second_other):
    whole = pl.BlockSpec(memory_space=pltpu.VMEM)
    return pl.pallas_call(
        joined_kernel,
        out_shape=jax.ShapeDtypeStruct((first.shape[0], 2 * first.shape[1]), first.dtype),
        in_specs=[pl.BlockSpec(memory_space=pltpu.SMEM)] + [whole] * 4,
        out_specs=whole,
        name="joined",
    )(place, first, first_other, second, second_other)


def local(
    patches,
    merge_gain,
    merge_first,
    merge_second,
    text_embeds,
    positions,
    segments,
    norm_gain,
    query_weight,
    keyval_weight,
    out_weight,
):
    count = patches.shape[0]
    width = merge_gain.shape[0]
    blocks, rows_here, slice_width = text_embeds.shape
    seq_len = segments.shape[0]
    block_len = seq_len // blocks
    section_index = lax.axis_index("section")
    cycle_index = lax.axis_index("blk")
    model_index = lax.axis_index("mp")
    n_mp = lax.axis_size("mp")
    n_blk = lax.axis_size("blk")
    first_core = section_index == 0
    head_size = keyval_weight.shape[4]
    rows = blocks * rows_here
    layers = 2

    query_own = query_weight[0]
    keyval_own = keyval_weight[0].reshape(keyval_weight.shape[1], 2 * head_size)
    out_own = out_weight[0]
    heads_half = query_own.shape[1] // 2
    weight_half = query_own.shape[0] // 2

    def packed(core):
        keep_rows = slice(core * weight_half, (core + 1) * weight_half)
        query_rows, keyval_rows = query_own[keep_rows], keyval_own[keep_rows]
        out_rows = out_own[:, keep_rows].T
        halves = (core, 1 - core)
        parts = [keyval_rows[:, half * head_size : (half + 1) * head_size] for half in halves]
        parts += [query_rows[:, half * heads_half : (half + 1) * heads_half] for half in halves]
        parts += [out_rows[:, half * heads_half : (half + 1) * heads_half] for half in halves]
        return jnp.concatenate(parts, axis=1)

    for_first, for_second = packed(0), packed(1)
    weight_keep = jnp.where(first_core, for_first, for_second)
    weight_other = swapped(jnp.where(first_core, for_second, for_first))
    keyval_width = 2 * head_size
    weight_full = []
    for home in range(layers):
        mine = jnp.where(section_index == home, weight_keep, weight_other)
        weight_full.append(lax.all_gather(mine, "blk", axis=0, tiled=True))
    gain_half = norm_gain[0].reshape(-1, 2, lane)
    gain_keep = jnp.where(first_core, gain_half[:, 0], gain_half[:, 1])
    gain_send = jnp.where(first_core, gain_half[:, 1], gain_half[:, 0])
    gain_other = swapped(gain_send)
    gain_layers = [
        jnp.where(first_core, gain_keep, gain_other).reshape(n_mp, 1, -1),
        jnp.where(first_core, gain_other, gain_keep).reshape(n_mp, 1, -1),
    ]

    inner = merger_inner(patches, merge_gain, merge_first)
    place = jnp.stack([section_index, cycle_index, model_index]).astype(jnp.int32)
    merged_pieces = merger_outer(place, inner, swapped(inner), merge_second, n_blk, n_mp)
    merged_terms = lax.all_to_all(merged_pieces, ("blk", "mp"), 0, 0, tiled=True)

    row_where = (
        jnp.arange(blocks)[:, None] * block_len
        + cycle_index * rows_here
        + jnp.arange(rows_here)[None, :]
    ).reshape(-1)
    starts = jnp.stack([jnp.sum(segments < 1), jnp.sum(segments < 2)])
    scalars = jnp.concatenate([starts, jnp.stack([cycle_index, section_index])]).astype(jnp.int32)
    is_visual = (positions[None, :] == row_where[:, None]).astype(jnp.bfloat16)
    has_visual = jnp.max(is_visual, axis=1, keepdims=True)
    text_rows = my_half(text_embeds.reshape(rows, slice_width), 1, section_index)
    cosine, sine = rope_tables(row_where, head_size)
    keyval_cosine = jnp.where(first_core, jnp.concatenate([cosine, cosine], axis=1), 1.0)
    keyval_sine = jnp.where(first_core, jnp.concatenate([-sine, sine], axis=1), 0.0)
    early = (scalars, is_visual, has_visual, text_rows, cosine, sine, keyval_cosine, keyval_sine)
    merged_terms, early = lax.optimization_barrier((merged_terms, early))
    scalars, is_visual, has_visual, text_rows, cosine, sine, keyval_cosine, keyval_sine = early
    merged_mine = jnp.sum(merged_terms.astype(jnp.float32), axis=0).astype(jnp.bfloat16)
    merged = spread(merged_mine).reshape(n_blk * merged_mine.shape[0], -1)
    picked = jnp.dot(is_visual, merged, preferred_element_type=jnp.float32).astype(jnp.bfloat16)
    state = jnp.where(has_visual > 0, picked, text_rows)


    results = []
    for layer_index in range(layers):
        parts = [state] + [moved(state, "mp", by) for by in (1, 2, 3)]
        gain = gain_layers[layer_index]
        weight = weight_full[layer_index]
        kept, sent = project_in(place, parts, gain, weight, 0, keyval_width, True)
        keyval_copies, shrink = keyval_rotate(
            kept, swapped(sent), keyval_cosine, keyval_sine, n_blk, n_mp * slice_width
        )
        keyval_copies, parts = lax.optimization_barrier((keyval_copies, parts))
        kept, sent = project_in(place, parts, gain, weight, keyval_width, 2 * heads_half, False)
        query = (kept + swapped(sent)).reshape(rows, -1, head_size) * shrink[:, None, :]
        query = rotate(query, cosine[:, None, :], sine[:, None, :])
        query = query.astype(jnp.bfloat16).reshape(rows, heads_half)
        gathered = lax.all_to_all(keyval_copies, "blk", 0, 0, tiled=True)
        gathered = gathered.reshape(n_blk, blocks, rows_here, head_size)
        attended = attention(scalars, query, gathered, swapped(gathered))
        attended_other = swapped(attended)
        own, *terms = project_out(place, attended, attended_other, weight)
        arrived = [moved(terms[by - 1], "mp", by) for by in (2, 1, 3)]
        total = state.astype(jnp.float32) + own.astype(jnp.float32)
        for part in arrived:
            total = total + part.astype(jnp.float32)
        state = total.astype(jnp.bfloat16)
        results.append(state)

    first_other = swapped(results[0])
    second_other = swapped(results[1])
    hidden = joined(place, results[0], first_other, results[1], second_other)
    return hidden.reshape(1, blocks, rows_here, slice_width)


def solution(mesh):
    return jax.shard_map(
        local,
        mesh=mesh,
        in_specs=(
            P("section", None),
            P(),
            P(None, ("blk", "mp")),
            P(("blk", "mp"), None),
            P(None, "blk", "mp"),
            P(),
            P(),
            P("section", None),
            P("section", "blk", "mp"),
            P("section", "blk", "mp", None, None),
            P("section", "mp", "blk"),
        ),
        out_specs=P("section", None, "blk", "mp"),
        check_vma=False,
    )
```

```python
import functools
import math

import jax
import jax.numpy as jnp
from jax import lax
from jax.experimental import pallas as pl
from jax.experimental.pallas import tpu as pltpu
from jax.sharding import PartitionSpec as P

epsilon = 1e-06
rope_base = 1000000.0
lane = 128


def moved(value, axis, by):
    size = lax.axis_size(axis)
    return lax.ppermute(value, axis, [(i, (i + by) % size) for i in range(size)])


def swapped(value):
    return lax.ppermute(value, "section", [(0, 1), (1, 0)])


def rope_tables(where_at, head_size):
    steps_half = jnp.arange(head_size // 2).astype(jnp.float32)
    inverse = jnp.exp(-jnp.log(rope_base) * 2.0 * steps_half / head_size)
    angles = where_at.astype(jnp.float32)[:, None] * inverse[None, :]
    return (jnp.cos(angles), jnp.sin(angles))


def rotate(values, cosine, sine):
    half = values.shape[-1] // 2
    first = values[..., :half]
    second = values[..., half:]
    return jnp.concatenate(
        [first * cosine - second * sine, second * cosine + first * sine], axis=-1
    )


def my_half(value, axis, section_index):
    shape = value.shape
    runs = shape[axis] // (2 * lane)
    split = value.reshape(shape[:axis] + (runs, 2, lane) + shape[axis + 1 :])
    index = [slice(None)] * split.ndim
    index[axis + 1] = 0
    even = split[tuple(index)]
    index[axis + 1] = 1
    odd = split[tuple(index)]
    picked = jnp.where(section_index == 0, even, odd)
    return picked.reshape(shape[:axis] + (runs * lane,) + shape[axis + 1 :])


def spread(value):
    size = lax.axis_size("blk")
    copies = jnp.broadcast_to(value[None], (size,) + value.shape)
    return lax.all_to_all(copies, "blk", 0, 0, tiled=True)


def attention_kernel(scalars, query_ref, mine_ref, other_ref, out_ref, *, chunk_runs):
    runs, blocks, run, head_size = mine_ref.shape
    heads = query_ref.shape[1] // head_size
    rows = heads * run
    chunk = chunk_runs * run
    per_block = runs // chunk_runs
    block_len = runs * run
    start_one, start_two, cycle, section = scalars[0], scalars[1], scalars[2], scalars[3]
    factor = 1.0 / head_size**0.5 * math.log2(math.e)

    def stripes(key_ref, value_ref):
        def stripe(block, carry):
            row_from = pl.multiple_of(block * run, run)
            first = block * block_len + cycle * run
            here = query_ref[pl.ds(row_from, run), :]
            stacked = jnp.concatenate(
                [here[:, h * head_size : (h + 1) * head_size] for h in range(heads)], axis=0
            )
            row_at = lax.broadcasted_iota(jnp.int32, (rows, 1), 0) % run + first
            row_start = jnp.where(
                row_at >= start_two, start_two, jnp.where(row_at >= start_one, start_one, 0)
            )
            stripe_start = jnp.where(
                first >= start_two, start_two, jnp.where(first >= start_one, start_one, 0)
            )

            def step(index, state):
                top, total, mixed = state
                in_block = index // per_block
                from_run = (index % per_block) * chunk_runs
                key = key_ref[pl.ds(from_run, chunk_runs), in_block].reshape(chunk, head_size)
                value = value_ref[pl.ds(from_run, chunk_runs), in_block].reshape(chunk, head_size)
                scores = lax.dot_general(
                    stacked, key, (((1,), (1,)), ((), ())), preferred_element_type=jnp.float32
                )
                key_at = lax.broadcasted_iota(jnp.int32, (1, chunk), 1) + index * chunk
                allowed = (key_at <= row_at) & (key_at >= row_start)
                scores = jnp.where(allowed, scores * factor, -1e30)
                new_top = jnp.maximum(top, jnp.max(scores, axis=1, keepdims=True))
                fade = jnp.exp2(top - new_top)
                weights = jnp.exp2(scores - new_top)
                total = total * fade + jnp.sum(weights, axis=1, keepdims=True)
                mixed = mixed * fade + jnp.dot(
                    weights.astype(jnp.bfloat16), value, preferred_element_type=jnp.float32
                )
                return new_top, total, mixed

            state = (
                jnp.full((rows, 1), -1e30, jnp.float32),
                jnp.zeros((rows, 1), jnp.float32),
                jnp.zeros((rows, head_size), jnp.float32),
            )
            _, total, mixed = lax.fori_loop(
                stripe_start // chunk, (first + run - 1) // chunk + 1, step, state
            )
            result = (mixed / total).astype(out_ref.dtype)
            for h in range(heads):
                out_ref[pl.ds(row_from, run), h * head_size : (h + 1) * head_size] = result[
                    h * run : (h + 1) * run
                ]
            return carry

        lax.fori_loop(0, blocks, stripe, 0)

    @pl.when(section == 0)
    def _():
        stripes(mine_ref, other_ref)

    @pl.when(section != 0)
    def _():
        stripes(other_ref, mine_ref)


def attention(scalars, query, mine, other):
    whole = pl.BlockSpec(memory_space=pltpu.VMEM)
    return pl.pallas_call(
        functools.partial(attention_kernel, chunk_runs=mine.shape[0]),
        out_shape=jax.ShapeDtypeStruct(query.shape, query.dtype),
        in_specs=[pl.BlockSpec(memory_space=pltpu.SMEM), whole, whole, whole],
        out_specs=whole,
        cost_estimate=pl.CostEstimate(
            flops=4 * query.size * mine.size // query.shape[1] // 4,
            bytes_accessed=2 * (2 * query.size + 2 * mine.size),
            transcendentals=0,
        ),
        name="attention",
    )(scalars, query, mine, other)


def merger_kernel(patches_ref, gain_ref, weight_ref, out_ref):
    width = gain_ref.shape[1]
    total = jnp.zeros(out_ref.shape, jnp.float32)
    for at in range(0, patches_ref.shape[1], width):
        piece = patches_ref[:, at : at + width].astype(jnp.float32)
        centered = piece - jnp.mean(piece, axis=1, keepdims=True)
        variance = jnp.mean(centered * centered, axis=1, keepdims=True)
        normed = (centered * lax.rsqrt(variance + epsilon) * gain_ref[...]).astype(jnp.bfloat16)
        total = total + jnp.dot(
            normed, weight_ref[at : at + width, :], preferred_element_type=jnp.float32
        )
    out_ref[...] = (0.5 * total * (1.0 + lax.erf(total * math.sqrt(0.5)))).astype(out_ref.dtype)


def merger_inner(patches, merge_gain, merge_first):
    whole = pl.BlockSpec(memory_space=pltpu.VMEM)
    rows, units = patches.shape[0], merge_first.shape[1]
    return pl.pallas_call(
        merger_kernel,
        out_shape=jax.ShapeDtypeStruct((rows, units), jnp.bfloat16),
        in_specs=[whole, whole, whole],
        out_specs=whole,
        cost_estimate=pl.CostEstimate(
            flops=2 * rows * merge_first.size,
            bytes_accessed=2 * (patches.size + merge_first.size),
            transcendentals=0,
        ),
        name="merger_inner",
    )(patches, merge_gain.reshape(1, -1), merge_first)


def merger_outer_kernel(place, mine_ref, other_ref, weight_ref, *out_refs):
    section = place[0]
    tokens = mine_ref.shape[0]
    runs = out_refs[0].shape[1] // lane
    for by, out_ref in enumerate(out_refs):
        piece = (place[2] + by) % len(out_refs)
        weight = jnp.concatenate(
            [
                weight_ref[
                    :, pl.ds(pl.multiple_of((2 * (piece * runs + run) + section) * lane, lane), lane)
                ]
                for run in range(runs)
            ],
            axis=1,
        )
        for inner_ref, core in ((mine_ref, section), (other_ref, 1 - section)):
            result = jnp.dot(inner_ref[...], weight, preferred_element_type=jnp.float32)
            at = pl.multiple_of(core * tokens, tokens)
            out_ref[pl.ds(at, tokens), :] = result.astype(out_ref.dtype)


def merger_outer(place, mine, other, merge_second, n_mp):
    whole = pl.BlockSpec(memory_space=pltpu.VMEM)
    shape = jax.ShapeDtypeStruct(
        (2 * mine.shape[0], merge_second.shape[1] // 2 // n_mp), jnp.bfloat16
    )
    return pl.pallas_call(
        merger_outer_kernel,
        out_shape=[shape] * n_mp,
        in_specs=[pl.BlockSpec(memory_space=pltpu.SMEM), whole, whole, whole],
        out_specs=[whole] * n_mp,
        name="merger_outer",
    )(place, mine, other, merge_second)


def project_in_kernel(
    place,
    own_ref,
    from_one,
    from_two,
    from_three,
    gain_ref,
    weight_hbm,
    kept_ref,
    sent_ref,
    rows_ref,
    weight_ref,
    sums_ref,
    semaphores,
    *,
    at,
):
    pieces, _, depth = gain_ref.shape
    half = weight_ref.shape[1] // 2
    copies = []
    for piece in range(pieces):
        deep = pl.ds(piece * depth, depth)
        copies.append(
            pltpu.make_async_copy(
                weight_hbm.at[deep, pl.ds(at, 2 * half)], weight_ref.at[deep], semaphores.at[piece]
            )
        )
        copies[-1].start()
    squares = jnp.zeros((own_ref.shape[0], 1), jnp.float32)
    for by, part_ref in enumerate((own_ref, from_one, from_two, from_three)):
        source = (place[2] + pieces - by) % pieces
        part = part_ref[...].astype(jnp.float32)
        if kept_ref.shape[1] > half:
            squares = squares + jnp.sum(part * part, axis=1, keepdims=True)
        rows_ref[source] = (part * gain_ref[source]).astype(jnp.bfloat16)
    if kept_ref.shape[1] > half:
        squares = jnp.broadcast_to(squares, (squares.shape[0], lane))
        kept_ref[:, half:] = squares
        sent_ref[:, half:] = squares
    for piece in range(pieces):
        copies[piece].wait()
        result = jnp.dot(
            rows_ref[piece],
            weight_ref[piece * depth : (piece + 1) * depth, :],
            preferred_element_type=jnp.float32,
        )
        if piece > 0:
            result = result + sums_ref[...]
        if piece < pieces - 1:
            sums_ref[...] = result
    kept_ref[:, :half] = result[:, :half]
    sent_ref[:, :half] = result[:, half:]


def project_in(place, parts, gain, weight, at, width, with_squares):
    rows, depth = parts[0].shape
    spare = lane if with_squares else 0
    out = jax.ShapeDtypeStruct((rows, width // 2 + spare), jnp.float32)
    whole = pl.BlockSpec(memory_space=pltpu.VMEM)
    return pl.pallas_call(
        functools.partial(project_in_kernel, at=at),
        out_shape=(out, out),
        in_specs=[pl.BlockSpec(memory_space=pltpu.SMEM)]
        + [whole] * 5
        + [pl.BlockSpec(memory_space=pltpu.HBM)],
        out_specs=(whole, whole),
        scratch_shapes=[
            pltpu.VMEM((len(parts), rows, depth), jnp.bfloat16),
            pltpu.VMEM((weight.shape[0], width), jnp.bfloat16),
            pltpu.VMEM((rows, width), jnp.float32),
            pltpu.SemaphoreType.DMA((len(parts),)),
        ],
        cost_estimate=pl.CostEstimate(
            flops=2 * rows * weight.shape[0] * width,
            bytes_accessed=2 * weight.shape[0] * width + 8 * rows * out.shape[1],
            transcendentals=0,
        ),
        compiler_params=pltpu.CompilerParams(vmem_limit_bytes=48 << 20),
        name="project_kv" if with_squares else "project_q",
    )(place, *parts, gain, weight)


def project_out_kernel(
    place, mine_ref, other_ref, weight_hbm, own_ref, one_ref, two_ref, three_ref, weight_ref, semaphores
):
    half = mine_ref.shape[1]
    depth = own_ref.shape[1]
    over_last = (((1,), (1,)), ((), ()))
    outs = (own_ref, one_ref, two_ref, three_ref)
    copies = []
    for by in range(len(outs)):
        source = (place[2] + by) % len(outs)
        copies.append(
            pltpu.make_async_copy(
                weight_hbm.at[
                    pl.ds(source * depth, depth), pl.ds(weight_hbm.shape[1] - 2 * half, 2 * half)
                ],
                weight_ref.at[by],
                semaphores.at[by],
            )
        )
        copies[-1].start()
    for by, out_ref in enumerate(outs):
        copies[by].wait()
        result = lax.dot_general(
            mine_ref[...], weight_ref[by, :, :half], over_last, preferred_element_type=jnp.float32
        ) + lax.dot_general(
            other_ref[...], weight_ref[by, :, half:], over_last, preferred_element_type=jnp.float32
        )
        out_ref[...] = result.astype(out_ref.dtype)


def project_out(place, mine, other, weight):
    rows, half = mine.shape
    pieces = lax.axis_size("mp")
    depth = weight.shape[0] // pieces
    shape = jax.ShapeDtypeStruct((rows, depth), jnp.bfloat16)
    whole = pl.BlockSpec(memory_space=pltpu.VMEM)
    return pl.pallas_call(
        project_out_kernel,
        out_shape=[shape] * pieces,
        in_specs=[
            pl.BlockSpec(memory_space=pltpu.SMEM),
            whole,
            whole,
            pl.BlockSpec(memory_space=pltpu.HBM),
        ],
        out_specs=[whole] * pieces,
        scratch_shapes=[
            pltpu.VMEM((pieces, depth, 2 * half), jnp.bfloat16),
            pltpu.SemaphoreType.DMA((pieces,)),
        ],
        cost_estimate=pl.CostEstimate(
            flops=4 * rows * half * weight.shape[0],
            bytes_accessed=4 * half * weight.shape[0] + 2 * rows * weight.shape[0],
            transcendentals=0,
        ),
        compiler_params=pltpu.CompilerParams(vmem_limit_bytes=48 << 20),
        name="project_out",
    )(place, mine, other, weight)


def joined_kernel(place, first_ref, first_other_ref, second_ref, second_other_ref, out_ref):
    runs = first_ref.shape[1] // lane

    def write(even_ref, odd_ref):
        for run in range(runs):
            here = slice(run * lane, (run + 1) * lane)
            out_ref[:, 2 * run * lane : (2 * run + 1) * lane] = even_ref[:, here]
            out_ref[:, (2 * run + 1) * lane : (2 * run + 2) * lane] = odd_ref[:, here]

    @pl.when(place[0] == 0)
    def _():
        write(first_ref, first_other_ref)

    @pl.when(place[0] != 0)
    def _():
        write(second_other_ref, second_ref)


def joined(place, first, first_other, second, second_other):
    whole = pl.BlockSpec(memory_space=pltpu.VMEM)
    return pl.pallas_call(
        joined_kernel,
        out_shape=jax.ShapeDtypeStruct((first.shape[0], 2 * first.shape[1]), first.dtype),
        in_specs=[pl.BlockSpec(memory_space=pltpu.SMEM)] + [whole] * 4,
        out_specs=whole,
        name="joined",
    )(place, first, first_other, second, second_other)


def local(
    patches,
    merge_gain,
    merge_first,
    merge_second,
    text_embeds,
    positions,
    segments,
    norm_gain,
    query_weight,
    keyval_weight,
    out_weight,
):
    count = patches.shape[0]
    width = merge_gain.shape[0]
    blocks, rows_here, slice_width = text_embeds.shape
    seq_len = segments.shape[0]
    block_len = seq_len // blocks
    section_index = lax.axis_index("section")
    cycle_index = lax.axis_index("blk")
    model_index = lax.axis_index("mp")
    n_mp = lax.axis_size("mp")
    n_blk = lax.axis_size("blk")
    first_core = section_index == 0
    head_size = keyval_weight.shape[4]
    rows = blocks * rows_here
    layers = 2

    query_own = query_weight[0]
    keyval_own = keyval_weight[0].reshape(keyval_weight.shape[1], 2 * head_size)
    out_own = out_weight[0]
    heads_half = query_own.shape[1] // 2
    weight_half = query_own.shape[0] // 2

    def packed(core):
        keep_rows = slice(core * weight_half, (core + 1) * weight_half)
        query_rows, keyval_rows = query_own[keep_rows], keyval_own[keep_rows]
        out_rows = out_own[:, keep_rows].T
        halves = (core, 1 - core)
        parts = [keyval_rows[:, half * head_size : (half + 1) * head_size] for half in halves]
        parts += [query_rows[:, half * heads_half : (half + 1) * heads_half] for half in halves]
        parts += [out_rows[:, half * heads_half : (half + 1) * heads_half] for half in halves]
        return jnp.concatenate(parts, axis=1)

    for_first, for_second = packed(0), packed(1)
    weight_keep = jnp.where(first_core, for_first, for_second)
    weight_other = swapped(jnp.where(first_core, for_second, for_first))
    keyval_width = 2 * head_size
    weight_full = []
    for home in range(layers):
        mine = jnp.where(section_index == home, weight_keep, weight_other)
        weight_full.append(lax.all_gather(mine, "blk", axis=0, tiled=True))
    gain_half = norm_gain[0].reshape(-1, 2, lane)
    gain_keep = jnp.where(first_core, gain_half[:, 0], gain_half[:, 1])
    gain_send = jnp.where(first_core, gain_half[:, 1], gain_half[:, 0])
    gain_other = swapped(gain_send)
    gain_layers = [
        jnp.where(first_core, gain_keep, gain_other).reshape(n_mp, 1, -1),
        jnp.where(first_core, gain_other, gain_keep).reshape(n_mp, 1, -1),
    ]

    inner = merger_inner(patches, merge_gain, merge_first)
    place = jnp.stack([section_index, cycle_index, model_index]).astype(jnp.int32)
    own, *terms = merger_outer(place, inner, swapped(inner), merge_second, n_mp)
    total = own.astype(jnp.float32)
    for part in [moved(terms[by - 1], "mp", by) for by in (2, 1, 3)]:
        total = total + part.astype(jnp.float32)
    merged_terms = lax.all_to_all(
        total.astype(jnp.bfloat16).reshape(n_blk, -1, total.shape[1]), "blk", 0, 0, tiled=True
    )

    row_where = (
        jnp.arange(blocks)[:, None] * block_len
        + cycle_index * rows_here
        + jnp.arange(rows_here)[None, :]
    ).reshape(-1)
    starts = jnp.stack([jnp.sum(segments < 1), jnp.sum(segments < 2)])
    scalars = jnp.concatenate([starts, jnp.stack([cycle_index, section_index])]).astype(jnp.int32)
    is_visual = (positions[None, :] == row_where[:, None]).astype(jnp.bfloat16)
    has_visual = jnp.max(is_visual, axis=1, keepdims=True)
    text_rows = my_half(text_embeds.reshape(rows, slice_width), 1, section_index)
    cosine, sine = rope_tables(row_where, head_size)
    keyval_cosine = jnp.where(first_core, jnp.concatenate([cosine, cosine], axis=1), 1.0)
    keyval_sine = jnp.where(first_core, jnp.concatenate([-sine, sine], axis=1), 0.0)
    early = (scalars, is_visual, has_visual, text_rows, cosine, sine, keyval_cosine, keyval_sine)
    merged_terms, early = lax.optimization_barrier((merged_terms, early))
    scalars, is_visual, has_visual, text_rows, cosine, sine, keyval_cosine, keyval_sine = early
    merged_mine = jnp.sum(merged_terms.astype(jnp.float32), axis=0).astype(jnp.bfloat16)
    merged = spread(merged_mine).reshape(n_blk * merged_mine.shape[0], -1)
    picked = jnp.dot(is_visual, merged, preferred_element_type=jnp.float32).astype(jnp.bfloat16)
    state = jnp.where(has_visual > 0, picked, text_rows)


    results = []
    for layer_index in range(layers):
        parts = [state] + [moved(state, "mp", by) for by in (1, 2, 3)]
        gain = gain_layers[layer_index]
        weight = weight_full[layer_index]
        kept, sent = project_in(place, parts, gain, weight, 0, keyval_width, True)
        total = kept + swapped(sent)
        shrink = lax.rsqrt(total[:, head_size : head_size + 1] / (n_mp * slice_width) + epsilon)
        keyval = total[:, :head_size] * shrink
        half = head_size // 2
        turned = jnp.concatenate([keyval[:, half:], keyval[:, :half]], axis=1)
        keyval = (keyval * keyval_cosine + turned * keyval_sine).astype(jnp.bfloat16)
        keyval, parts = lax.optimization_barrier((keyval, parts))
        kept, sent = project_in(place, parts, gain, weight, keyval_width, 2 * heads_half, False)
        query = ((kept + swapped(sent)) * shrink).reshape(rows, -1, head_size)
        query = rotate(query, cosine[:, None, :], sine[:, None, :])
        query = query.astype(jnp.bfloat16).reshape(rows, heads_half)
        gathered = spread(keyval).reshape(n_blk, blocks, rows_here, head_size)
        attended = attention(scalars, query, gathered, swapped(gathered))
        attended_other = swapped(attended)
        own, *terms = project_out(place, attended, attended_other, weight)
        arrived = [moved(terms[by - 1], "mp", by) for by in (2, 1, 3)]
        total = state.astype(jnp.float32) + own.astype(jnp.float32)
        for part in arrived:
            total = total + part.astype(jnp.float32)
        state = total.astype(jnp.bfloat16)
        results.append(state)

    first_other = swapped(results[0])
    second_other = swapped(results[1])
    hidden = joined(place, results[0], first_other, results[1], second_other)
    return hidden.reshape(1, blocks, rows_here, slice_width)


def solution(mesh):
    return jax.shard_map(
        local,
        mesh=mesh,
        in_specs=(
            P("section", None),
            P(),
            P(None, ("blk", "mp")),
            P(("blk", "mp"), None),
            P(None, "blk", "mp"),
            P(),
            P(),
            P("section", None),
            P("section", "blk", "mp"),
            P("section", "blk", "mp", None, None),
            P("section", "mp", "blk"),
        ),
        out_specs=P("section", None, "blk", "mp"),
        check_vma=False,
    )
```

```python
import functools
import math

import jax
import jax.numpy as jnp
from jax import lax
from jax.experimental import pallas as pl
from jax.experimental.pallas import tpu as pltpu
from jax.sharding import PartitionSpec as P

epsilon = 1e-06
rope_base = 1000000.0
lane = 128


def moved(value, axis, by):
    size = lax.axis_size(axis)
    return lax.ppermute(value, axis, [(i, (i + by) % size) for i in range(size)])


def swapped(value):
    return lax.ppermute(value, "section", [(0, 1), (1, 0)])


def rope_tables(where_at, head_size):
    steps_half = jnp.arange(head_size // 2).astype(jnp.float32)
    inverse = jnp.exp(-jnp.log(rope_base) * 2.0 * steps_half / head_size)
    angles = where_at.astype(jnp.float32)[:, None] * inverse[None, :]
    return (jnp.cos(angles), jnp.sin(angles))


def rotate(values, cosine, sine):
    half = values.shape[-1] // 2
    first = values[..., :half]
    second = values[..., half:]
    return jnp.concatenate(
        [first * cosine - second * sine, second * cosine + first * sine], axis=-1
    )


def my_half(value, axis, section_index):
    shape = value.shape
    runs = shape[axis] // (2 * lane)
    split = value.reshape(shape[:axis] + (runs, 2, lane) + shape[axis + 1 :])
    index = [slice(None)] * split.ndim
    index[axis + 1] = 0
    even = split[tuple(index)]
    index[axis + 1] = 1
    odd = split[tuple(index)]
    picked = jnp.where(section_index == 0, even, odd)
    return picked.reshape(shape[:axis] + (runs * lane,) + shape[axis + 1 :])


def spread(value):
    size = lax.axis_size("blk")
    copies = jnp.broadcast_to(value[None], (size,) + value.shape)
    return lax.all_to_all(copies, "blk", 0, 0, tiled=True)


def attention_kernel(scalars, query_ref, mine_ref, other_ref, out_ref, *, chunk_runs):
    runs, blocks, run, head_size = mine_ref.shape
    heads = query_ref.shape[1] // head_size
    rows = heads * run
    chunk = chunk_runs * run
    per_block = runs // chunk_runs
    block_len = runs * run
    start_one, start_two, cycle, section = scalars[0], scalars[1], scalars[2], scalars[3]
    factor = 1.0 / head_size**0.5 * math.log2(math.e)

    def stripes(key_ref, value_ref):
        def stripe(block, carry):
            row_from = pl.multiple_of(block * run, run)
            first = block * block_len + cycle * run
            here = query_ref[pl.ds(row_from, run), :]
            stacked = jnp.concatenate(
                [here[:, h * head_size : (h + 1) * head_size] for h in range(heads)], axis=0
            )
            row_at = lax.broadcasted_iota(jnp.int32, (rows, 1), 0) % run + first
            row_start = jnp.where(
                row_at >= start_two, start_two, jnp.where(row_at >= start_one, start_one, 0)
            )
            stripe_start = jnp.where(
                first >= start_two, start_two, jnp.where(first >= start_one, start_one, 0)
            )

            def step(index, state):
                top, total, mixed = state
                in_block = index // per_block
                from_run = (index % per_block) * chunk_runs
                key = key_ref[pl.ds(from_run, chunk_runs), in_block].reshape(chunk, head_size)
                value = value_ref[pl.ds(from_run, chunk_runs), in_block].reshape(chunk, head_size)
                scores = lax.dot_general(
                    stacked, key, (((1,), (1,)), ((), ())), preferred_element_type=jnp.float32
                )
                key_at = lax.broadcasted_iota(jnp.int32, (1, chunk), 1) + index * chunk
                allowed = (key_at <= row_at) & (key_at >= row_start)
                scores = jnp.where(allowed, scores * factor, -1e30)
                new_top = jnp.maximum(top, jnp.max(scores, axis=1, keepdims=True))
                fade = jnp.exp2(top - new_top)
                weights = jnp.exp2(scores - new_top)
                total = total * fade + jnp.sum(weights, axis=1, keepdims=True)
                mixed = mixed * fade + jnp.dot(
                    weights.astype(jnp.bfloat16), value, preferred_element_type=jnp.float32
                )
                return new_top, total, mixed

            state = (
                jnp.full((rows, 1), -1e30, jnp.float32),
                jnp.zeros((rows, 1), jnp.float32),
                jnp.zeros((rows, head_size), jnp.float32),
            )
            _, total, mixed = lax.fori_loop(
                stripe_start // chunk, (first + run - 1) // chunk + 1, step, state
            )
            result = (mixed / total).astype(out_ref.dtype)
            for h in range(heads):
                out_ref[pl.ds(row_from, run), h * head_size : (h + 1) * head_size] = result[
                    h * run : (h + 1) * run
                ]
            return carry

        lax.fori_loop(0, blocks, stripe, 0)

    @pl.when(section == 0)
    def _():
        stripes(mine_ref, other_ref)

    @pl.when(section != 0)
    def _():
        stripes(other_ref, mine_ref)


def attention(scalars, query, mine, other):
    whole = pl.BlockSpec(memory_space=pltpu.VMEM)
    return pl.pallas_call(
        functools.partial(attention_kernel, chunk_runs=mine.shape[0]),
        out_shape=jax.ShapeDtypeStruct(query.shape, query.dtype),
        in_specs=[pl.BlockSpec(memory_space=pltpu.SMEM), whole, whole, whole],
        out_specs=whole,
        cost_estimate=pl.CostEstimate(
            flops=4 * query.size * mine.size // query.shape[1] // 4,
            bytes_accessed=2 * (2 * query.size + 2 * mine.size),
            transcendentals=0,
        ),
        compiler_params=pltpu.CompilerParams(vmem_limit_bytes=16 << 20),
        name="attention",
    )(scalars, query, mine, other)


def merger_kernel(patches_ref, gain_ref, weight_ref, out_ref):
    width = gain_ref.shape[1]
    total = jnp.zeros(out_ref.shape, jnp.float32)
    for at in range(0, patches_ref.shape[1], width):
        piece = patches_ref[:, at : at + width].astype(jnp.float32)
        centered = piece - jnp.mean(piece, axis=1, keepdims=True)
        variance = jnp.mean(centered * centered, axis=1, keepdims=True)
        normed = (centered * lax.rsqrt(variance + epsilon) * gain_ref[...]).astype(jnp.bfloat16)
        total = total + jnp.dot(
            normed, weight_ref[at : at + width, :], preferred_element_type=jnp.float32
        )
    out_ref[...] = (0.5 * total * (1.0 + lax.erf(total * math.sqrt(0.5)))).astype(out_ref.dtype)


def merger_inner(patches, merge_gain, merge_first):
    whole = pl.BlockSpec(memory_space=pltpu.VMEM)
    rows, units = patches.shape[0], merge_first.shape[1]
    return pl.pallas_call(
        merger_kernel,
        out_shape=jax.ShapeDtypeStruct((rows, units), jnp.bfloat16),
        in_specs=[whole, whole, whole],
        out_specs=whole,
        cost_estimate=pl.CostEstimate(
            flops=2 * rows * merge_first.size,
            bytes_accessed=2 * (patches.size + merge_first.size),
            transcendentals=0,
        ),
        compiler_params=pltpu.CompilerParams(vmem_limit_bytes=12 << 20),
        name="merger_inner",
    )(patches, merge_gain.reshape(1, -1), merge_first)


def merger_outer_kernel(place, mine_ref, other_ref, weight_ref, *out_refs):
    section = place[0]
    tokens = mine_ref.shape[0]
    runs = out_refs[0].shape[1] // lane
    for by, out_ref in enumerate(out_refs):
        piece = (place[2] + by) % len(out_refs)
        weight = jnp.concatenate(
            [
                weight_ref[
                    :, pl.ds(pl.multiple_of((2 * (piece * runs + run) + section) * lane, lane), lane)
                ]
                for run in range(runs)
            ],
            axis=1,
        )
        for inner_ref, core in ((mine_ref, section), (other_ref, 1 - section)):
            result = jnp.dot(inner_ref[...], weight, preferred_element_type=jnp.float32)
            at = pl.multiple_of(core * tokens, tokens)
            out_ref[pl.ds(at, tokens), :] = result.astype(out_ref.dtype)


def merger_outer(place, mine, other, merge_second, n_mp):
    whole = pl.BlockSpec(memory_space=pltpu.VMEM)
    shape = jax.ShapeDtypeStruct(
        (2 * mine.shape[0], merge_second.shape[1] // 2 // n_mp), jnp.bfloat16
    )
    return pl.pallas_call(
        merger_outer_kernel,
        out_shape=[shape] * n_mp,
        in_specs=[pl.BlockSpec(memory_space=pltpu.SMEM), whole, whole, whole],
        out_specs=[whole] * n_mp,
        compiler_params=pltpu.CompilerParams(vmem_limit_bytes=12 << 20),
        name="merger_outer",
    )(place, mine, other, merge_second)


def project_in_kernel(
    place,
    own_ref,
    from_one,
    from_two,
    from_three,
    gain_ref,
    weight_hbm,
    kept_ref,
    sent_ref,
    rows_ref,
    weight_ref,
    sums_ref,
    semaphores,
    *,
    at,
):
    pieces, _, depth = gain_ref.shape
    half = weight_ref.shape[1] // 2
    copies = []
    for piece in range(pieces):
        deep = pl.ds(piece * depth, depth)
        copies.append(
            pltpu.make_async_copy(
                weight_hbm.at[deep, pl.ds(at, 2 * half)], weight_ref.at[deep], semaphores.at[piece]
            )
        )
        copies[-1].start()
    squares = jnp.zeros((own_ref.shape[0], 1), jnp.float32)
    for by, part_ref in enumerate((own_ref, from_one, from_two, from_three)):
        source = (place[2] + pieces - by) % pieces
        part = part_ref[...].astype(jnp.float32)
        if kept_ref.shape[1] > half:
            squares = squares + jnp.sum(part * part, axis=1, keepdims=True)
        rows_ref[source] = (part * gain_ref[source]).astype(jnp.bfloat16)
    if kept_ref.shape[1] > half:
        squares = jnp.broadcast_to(squares, (squares.shape[0], lane))
        kept_ref[:, half:] = squares
        sent_ref[:, half:] = squares
    for piece in range(pieces):
        copies[piece].wait()
        result = jnp.dot(
            rows_ref[piece],
            weight_ref[piece * depth : (piece + 1) * depth, :],
            preferred_element_type=jnp.float32,
        )
        if piece > 0:
            result = result + sums_ref[...]
        if piece < pieces - 1:
            sums_ref[...] = result
    kept_ref[:, :half] = result[:, :half]
    sent_ref[:, :half] = result[:, half:]


def project_in(place, parts, gain, weight, at, width, with_squares):
    rows, depth = parts[0].shape
    spare = lane if with_squares else 0
    out = jax.ShapeDtypeStruct((rows, width // 2 + spare), jnp.float32)
    whole = pl.BlockSpec(memory_space=pltpu.VMEM)
    return pl.pallas_call(
        functools.partial(project_in_kernel, at=at),
        out_shape=(out, out),
        in_specs=[pl.BlockSpec(memory_space=pltpu.SMEM)]
        + [whole] * 5
        + [pl.BlockSpec(memory_space=pltpu.HBM)],
        out_specs=(whole, whole),
        scratch_shapes=[
            pltpu.VMEM((len(parts), rows, depth), jnp.bfloat16),
            pltpu.VMEM((weight.shape[0], width), jnp.bfloat16),
            pltpu.VMEM((rows, width), jnp.float32),
            pltpu.SemaphoreType.DMA((len(parts),)),
        ],
        cost_estimate=pl.CostEstimate(
            flops=2 * rows * weight.shape[0] * width,
            bytes_accessed=2 * weight.shape[0] * width + 8 * rows * out.shape[1],
            transcendentals=0,
        ),
        compiler_params=pltpu.CompilerParams(vmem_limit_bytes=48 << 20),
        name="project_kv" if with_squares else "project_q",
    )(place, *parts, gain, weight)


def project_out_kernel(
    place, mine_ref, other_ref, weight_hbm, own_ref, one_ref, two_ref, three_ref, weight_ref, semaphores
):
    half = mine_ref.shape[1]
    depth = own_ref.shape[1]
    over_last = (((1,), (1,)), ((), ()))
    outs = (own_ref, one_ref, two_ref, three_ref)
    copies = []
    for by in range(len(outs)):
        source = (place[2] + by) % len(outs)
        copies.append(
            pltpu.make_async_copy(
                weight_hbm.at[
                    pl.ds(source * depth, depth), pl.ds(weight_hbm.shape[1] - 2 * half, 2 * half)
                ],
                weight_ref.at[by],
                semaphores.at[by],
            )
        )
        copies[-1].start()
    for by, out_ref in enumerate(outs):
        copies[by].wait()
        result = lax.dot_general(
            mine_ref[...], weight_ref[by, :, :half], over_last, preferred_element_type=jnp.float32
        ) + lax.dot_general(
            other_ref[...], weight_ref[by, :, half:], over_last, preferred_element_type=jnp.float32
        )
        out_ref[...] = result.astype(out_ref.dtype)


def project_out(place, mine, other, weight):
    rows, half = mine.shape
    pieces = lax.axis_size("mp")
    depth = weight.shape[0] // pieces
    shape = jax.ShapeDtypeStruct((rows, depth), jnp.bfloat16)
    whole = pl.BlockSpec(memory_space=pltpu.VMEM)
    return pl.pallas_call(
        project_out_kernel,
        out_shape=[shape] * pieces,
        in_specs=[
            pl.BlockSpec(memory_space=pltpu.SMEM),
            whole,
            whole,
            pl.BlockSpec(memory_space=pltpu.HBM),
        ],
        out_specs=[whole] * pieces,
        scratch_shapes=[
            pltpu.VMEM((pieces, depth, 2 * half), jnp.bfloat16),
            pltpu.SemaphoreType.DMA((pieces,)),
        ],
        cost_estimate=pl.CostEstimate(
            flops=4 * rows * half * weight.shape[0],
            bytes_accessed=4 * half * weight.shape[0] + 2 * rows * weight.shape[0],
            transcendentals=0,
        ),
        compiler_params=pltpu.CompilerParams(vmem_limit_bytes=48 << 20),
        name="project_out",
    )(place, mine, other, weight)


def joined_kernel(place, first_ref, first_other_ref, second_ref, second_other_ref, out_ref):
    runs = first_ref.shape[1] // lane

    def write(even_ref, odd_ref):
        for run in range(runs):
            here = slice(run * lane, (run + 1) * lane)
            out_ref[:, 2 * run * lane : (2 * run + 1) * lane] = even_ref[:, here]
            out_ref[:, (2 * run + 1) * lane : (2 * run + 2) * lane] = odd_ref[:, here]

    @pl.when(place[0] == 0)
    def _():
        write(first_ref, first_other_ref)

    @pl.when(place[0] != 0)
    def _():
        write(second_other_ref, second_ref)


def joined(place, first, first_other, second, second_other):
    whole = pl.BlockSpec(memory_space=pltpu.VMEM)
    return pl.pallas_call(
        joined_kernel,
        out_shape=jax.ShapeDtypeStruct((first.shape[0], 2 * first.shape[1]), first.dtype),
        in_specs=[pl.BlockSpec(memory_space=pltpu.SMEM)] + [whole] * 4,
        out_specs=whole,
        compiler_params=pltpu.CompilerParams(vmem_limit_bytes=8 << 20),
        name="joined",
    )(place, first, first_other, second, second_other)


def local(
    patches,
    merge_gain,
    merge_first,
    merge_second,
    text_embeds,
    positions,
    segments,
    norm_gain,
    query_weight,
    keyval_weight,
    out_weight,
):
    count = patches.shape[0]
    width = merge_gain.shape[0]
    blocks, rows_here, slice_width = text_embeds.shape
    seq_len = segments.shape[0]
    block_len = seq_len // blocks
    section_index = lax.axis_index("section")
    cycle_index = lax.axis_index("blk")
    model_index = lax.axis_index("mp")
    n_mp = lax.axis_size("mp")
    n_blk = lax.axis_size("blk")
    first_core = section_index == 0
    head_size = keyval_weight.shape[4]
    rows = blocks * rows_here
    layers = 2

    query_own = query_weight[0]
    keyval_own = keyval_weight[0].reshape(keyval_weight.shape[1], 2 * head_size)
    out_own = out_weight[0]
    heads_half = query_own.shape[1] // 2
    weight_half = query_own.shape[0] // 2

    def packed(core):
        keep_rows = slice(core * weight_half, (core + 1) * weight_half)
        query_rows, keyval_rows = query_own[keep_rows], keyval_own[keep_rows]
        out_rows = out_own[:, keep_rows].T
        halves = (core, 1 - core)
        parts = [keyval_rows[:, half * head_size : (half + 1) * head_size] for half in halves]
        parts += [query_rows[:, half * heads_half : (half + 1) * heads_half] for half in halves]
        parts += [out_rows[:, half * heads_half : (half + 1) * heads_half] for half in halves]
        return jnp.concatenate(parts, axis=1)

    for_first, for_second = packed(0), packed(1)
    weight_keep = jnp.where(first_core, for_first, for_second)
    weight_other = swapped(jnp.where(first_core, for_second, for_first))
    keyval_width = 2 * head_size
    weight_full = []
    for home in range(layers):
        mine = jnp.where(section_index == home, weight_keep, weight_other)
        weight_full.append(lax.all_gather(mine, "blk", axis=0, tiled=True))
    gain_half = norm_gain[0].reshape(-1, 2, lane)
    gain_keep = jnp.where(first_core, gain_half[:, 0], gain_half[:, 1])
    gain_send = jnp.where(first_core, gain_half[:, 1], gain_half[:, 0])
    gain_other = swapped(gain_send)
    gain_layers = [
        jnp.where(first_core, gain_keep, gain_other).reshape(n_mp, 1, -1),
        jnp.where(first_core, gain_other, gain_keep).reshape(n_mp, 1, -1),
    ]

    inner = merger_inner(patches, merge_gain, merge_first)
    place = jnp.stack([section_index, cycle_index, model_index]).astype(jnp.int32)
    own, *terms = merger_outer(place, inner, swapped(inner), merge_second, n_mp)
    total = own.astype(jnp.float32)
    for part in [moved(terms[by - 1], "mp", by) for by in (2, 1, 3)]:
        total = total + part.astype(jnp.float32)
    merged_terms = lax.all_to_all(
        total.astype(jnp.bfloat16).reshape(n_blk, -1, total.shape[1]), "blk", 0, 0, tiled=True
    )

    row_where = (
        jnp.arange(blocks)[:, None] * block_len
        + cycle_index * rows_here
        + jnp.arange(rows_here)[None, :]
    ).reshape(-1)
    starts = jnp.stack([jnp.sum(segments < 1), jnp.sum(segments < 2)])
    scalars = jnp.concatenate([starts, jnp.stack([cycle_index, section_index])]).astype(jnp.int32)
    is_visual = (positions[None, :] == row_where[:, None]).astype(jnp.bfloat16)
    has_visual = jnp.max(is_visual, axis=1, keepdims=True)
    text_rows = my_half(text_embeds.reshape(rows, slice_width), 1, section_index)
    cosine, sine = rope_tables(row_where, head_size)
    keyval_cosine = jnp.where(first_core, jnp.concatenate([cosine, cosine], axis=1), 1.0)
    keyval_sine = jnp.where(first_core, jnp.concatenate([-sine, sine], axis=1), 0.0)
    early = (scalars, is_visual, has_visual, text_rows, cosine, sine, keyval_cosine, keyval_sine)
    merged_terms, early = lax.optimization_barrier((merged_terms, early))
    scalars, is_visual, has_visual, text_rows, cosine, sine, keyval_cosine, keyval_sine = early
    merged_mine = jnp.sum(merged_terms.astype(jnp.float32), axis=0).astype(jnp.bfloat16)
    merged = spread(merged_mine).reshape(n_blk * merged_mine.shape[0], -1)
    picked = jnp.dot(is_visual, merged, preferred_element_type=jnp.float32).astype(jnp.bfloat16)
    state = jnp.where(has_visual > 0, picked, text_rows)


    results = []
    for layer_index in range(layers):
        parts = [state] + [moved(state, "mp", by) for by in (1, 2, 3)]
        gain = gain_layers[layer_index]
        weight = weight_full[layer_index]
        kept, sent = project_in(place, parts, gain, weight, 0, keyval_width, True)
        total = kept + swapped(sent)
        shrink = lax.rsqrt(total[:, head_size : head_size + 1] / (n_mp * slice_width) + epsilon)
        keyval = total[:, :head_size] * shrink
        half = head_size // 2
        turned = jnp.concatenate([keyval[:, half:], keyval[:, :half]], axis=1)
        keyval = (keyval * keyval_cosine + turned * keyval_sine).astype(jnp.bfloat16)
        keyval, parts = lax.optimization_barrier((keyval, parts))
        kept, sent = project_in(place, parts, gain, weight, keyval_width, 2 * heads_half, False)
        query = ((kept + swapped(sent)) * shrink).reshape(rows, -1, head_size)
        query = rotate(query, cosine[:, None, :], sine[:, None, :])
        query = query.astype(jnp.bfloat16).reshape(rows, heads_half)
        gathered = spread(keyval).reshape(n_blk, blocks, rows_here, head_size)
        attended = attention(scalars, query, gathered, swapped(gathered))
        attended_other = swapped(attended)
        own, *terms = project_out(place, attended, attended_other, weight)
        arrived = [moved(terms[by - 1], "mp", by) for by in (2, 1, 3)]
        total = state.astype(jnp.float32) + own.astype(jnp.float32)
        for part in arrived:
            total = total + part.astype(jnp.float32)
        state = total.astype(jnp.bfloat16)
        results.append(state)

    first_other = swapped(results[0])
    second_other = swapped(results[1])
    hidden = joined(place, results[0], first_other, results[1], second_other)
    return hidden.reshape(1, blocks, rows_here, slice_width)


def solution(mesh):
    return jax.shard_map(
        local,
        mesh=mesh,
        in_specs=(
            P("section", None),
            P(),
            P(None, ("blk", "mp")),
            P(("blk", "mp"), None),
            P(None, "blk", "mp"),
            P(),
            P(),
            P("section", None),
            P("section", "blk", "mp"),
            P("section", "blk", "mp", None, None),
            P("section", "mp", "blk"),
        ),
        out_specs=P("section", None, "blk", "mp"),
        check_vma=False,
    )
```

```python
import functools
import math

import jax
import jax.numpy as jnp
from jax import lax
from jax.experimental import pallas as pl
from jax.experimental.pallas import tpu as pltpu
from jax.sharding import PartitionSpec as P

epsilon = 1e-06
rope_base = 1000000.0
lane = 128


def moved(value, axis, by):
    size = lax.axis_size(axis)
    return lax.ppermute(value, axis, [(i, (i + by) % size) for i in range(size)])


def swapped(value):
    return lax.ppermute(value, "section", [(0, 1), (1, 0)])


def rope_tables(where_at, head_size):
    steps_half = jnp.arange(head_size // 2).astype(jnp.float32)
    inverse = jnp.exp(-jnp.log(rope_base) * 2.0 * steps_half / head_size)
    angles = where_at.astype(jnp.float32)[:, None] * inverse[None, :]
    return (jnp.cos(angles), jnp.sin(angles))


def my_half(value, axis, section_index):
    shape = value.shape
    runs = shape[axis] // (2 * lane)
    split = value.reshape(shape[:axis] + (runs, 2, lane) + shape[axis + 1 :])
    index = [slice(None)] * split.ndim
    index[axis + 1] = 0
    even = split[tuple(index)]
    index[axis + 1] = 1
    odd = split[tuple(index)]
    picked = jnp.where(section_index == 0, even, odd)
    return picked.reshape(shape[:axis] + (runs * lane,) + shape[axis + 1 :])


def spread(value):
    size = lax.axis_size("blk")
    copies = jnp.broadcast_to(value[None], (size,) + value.shape)
    return lax.all_to_all(copies, "blk", 0, 0, tiled=True)


def attention_kernel(scalars, query_ref, mine_ref, other_ref, out_ref, *, chunk_runs):
    runs, blocks, run, head_size = mine_ref.shape
    heads = query_ref.shape[1] // head_size
    rows = heads * run
    chunk = chunk_runs * run
    per_block = runs // chunk_runs
    block_len = runs * run
    start_one, start_two, cycle, section = scalars[0], scalars[1], scalars[2], scalars[3]
    factor = 1.0 / head_size**0.5 * math.log2(math.e)

    def stripes(key_ref, value_ref):
        def stripe(block, carry):
            row_from = pl.multiple_of(block * run, run)
            first = block * block_len + cycle * run
            here = query_ref[pl.ds(row_from, run), :]
            stacked = jnp.concatenate(
                [here[:, h * head_size : (h + 1) * head_size] for h in range(heads)], axis=0
            )
            row_at = lax.broadcasted_iota(jnp.int32, (rows, 1), 0) % run + first
            row_start = jnp.where(
                row_at >= start_two, start_two, jnp.where(row_at >= start_one, start_one, 0)
            )
            stripe_start = jnp.where(
                first >= start_two, start_two, jnp.where(first >= start_one, start_one, 0)
            )

            def step(index, state):
                top, total, mixed = state
                in_block = index // per_block
                from_run = (index % per_block) * chunk_runs
                key = key_ref[pl.ds(from_run, chunk_runs), in_block].reshape(chunk, head_size)
                value = value_ref[pl.ds(from_run, chunk_runs), in_block].reshape(chunk, head_size)
                scores = lax.dot_general(
                    stacked, key, (((1,), (1,)), ((), ())), preferred_element_type=jnp.float32
                )
                key_at = lax.broadcasted_iota(jnp.int32, (1, chunk), 1) + index * chunk
                allowed = (key_at <= row_at) & (key_at >= row_start)
                scores = jnp.where(allowed, scores * factor, -1e30)
                new_top = jnp.maximum(top, jnp.max(scores, axis=1, keepdims=True))
                fade = jnp.exp2(top - new_top)
                weights = jnp.exp2(scores - new_top)
                total = total * fade + jnp.sum(weights, axis=1, keepdims=True)
                mixed = mixed * fade + jnp.dot(
                    weights.astype(jnp.bfloat16), value, preferred_element_type=jnp.float32
                )
                return new_top, total, mixed

            state = (
                jnp.full((rows, 1), -1e30, jnp.float32),
                jnp.zeros((rows, 1), jnp.float32),
                jnp.zeros((rows, head_size), jnp.float32),
            )
            _, total, mixed = lax.fori_loop(
                stripe_start // chunk, (first + run - 1) // chunk + 1, step, state
            )
            result = (mixed / total).astype(out_ref.dtype)
            for h in range(heads):
                out_ref[pl.ds(row_from, run), h * head_size : (h + 1) * head_size] = result[
                    h * run : (h + 1) * run
                ]
            return carry

        lax.fori_loop(0, blocks, stripe, 0)

    @pl.when(section == 0)
    def _():
        stripes(mine_ref, other_ref)

    @pl.when(section != 0)
    def _():
        stripes(other_ref, mine_ref)


def attention(scalars, query, mine, other):
    whole = pl.BlockSpec(memory_space=pltpu.VMEM)
    return pl.pallas_call(
        functools.partial(attention_kernel, chunk_runs=mine.shape[0]),
        out_shape=jax.ShapeDtypeStruct(query.shape, query.dtype),
        in_specs=[pl.BlockSpec(memory_space=pltpu.SMEM), whole, whole, whole],
        out_specs=whole,
        cost_estimate=pl.CostEstimate(
            flops=4 * query.size * mine.size // query.shape[1] // 4,
            bytes_accessed=2 * (2 * query.size + 2 * mine.size),
            transcendentals=0,
        ),
        compiler_params=pltpu.CompilerParams(vmem_limit_bytes=16 << 20),
        name="attention",
    )(scalars, query, mine, other)


def merger_kernel(patches_ref, gain_ref, weight_ref, out_ref):
    width = gain_ref.shape[1]
    total = jnp.zeros(out_ref.shape, jnp.float32)
    for at in range(0, patches_ref.shape[1], width):
        piece = patches_ref[:, at : at + width].astype(jnp.float32)
        centered = piece - jnp.mean(piece, axis=1, keepdims=True)
        variance = jnp.mean(centered * centered, axis=1, keepdims=True)
        normed = (centered * lax.rsqrt(variance + epsilon) * gain_ref[...]).astype(jnp.bfloat16)
        total = total + jnp.dot(
            normed, weight_ref[at : at + width, :], preferred_element_type=jnp.float32
        )
    out_ref[...] = (0.5 * total * (1.0 + lax.erf(total * math.sqrt(0.5)))).astype(out_ref.dtype)


def merger_inner(patches, merge_gain, merge_first):
    whole = pl.BlockSpec(memory_space=pltpu.VMEM)
    rows, units = patches.shape[0], merge_first.shape[1]
    return pl.pallas_call(
        merger_kernel,
        out_shape=jax.ShapeDtypeStruct((rows, units), jnp.bfloat16),
        in_specs=[whole, whole, whole],
        out_specs=whole,
        cost_estimate=pl.CostEstimate(
            flops=2 * rows * merge_first.size,
            bytes_accessed=2 * (patches.size + merge_first.size),
            transcendentals=0,
        ),
        compiler_params=pltpu.CompilerParams(vmem_limit_bytes=12 << 20),
        name="merger_inner",
    )(patches, merge_gain.reshape(1, -1), merge_first)


def merger_outer_kernel(place, mine_ref, other_ref, weight_ref, *out_refs):
    section = place[0]
    tokens = mine_ref.shape[0]
    runs = out_refs[0].shape[1] // lane
    for by, out_ref in enumerate(out_refs):
        piece = (place[2] + by) % len(out_refs)
        weight = jnp.concatenate(
            [
                weight_ref[
                    :, pl.ds(pl.multiple_of((2 * (piece * runs + run) + section) * lane, lane), lane)
                ]
                for run in range(runs)
            ],
            axis=1,
        )
        for inner_ref, core in ((mine_ref, section), (other_ref, 1 - section)):
            result = jnp.dot(inner_ref[...], weight, preferred_element_type=jnp.float32)
            at = pl.multiple_of(core * tokens, tokens)
            out_ref[pl.ds(at, tokens), :] = result.astype(out_ref.dtype)


def merger_outer(place, mine, other, merge_second, n_mp):
    whole = pl.BlockSpec(memory_space=pltpu.VMEM)
    shape = jax.ShapeDtypeStruct(
        (2 * mine.shape[0], merge_second.shape[1] // 2 // n_mp), jnp.bfloat16
    )
    return pl.pallas_call(
        merger_outer_kernel,
        out_shape=[shape] * n_mp,
        in_specs=[pl.BlockSpec(memory_space=pltpu.SMEM), whole, whole, whole],
        out_specs=[whole] * n_mp,
        compiler_params=pltpu.CompilerParams(vmem_limit_bytes=12 << 20),
        name="merger_outer",
    )(place, mine, other, merge_second)


def project_in_kernel(
    place,
    own_ref,
    from_one,
    from_two,
    from_three,
    gain_ref,
    weight_hbm,
    kept_ref,
    sent_ref,
    *rest,
    at,
):
    later_ref = rest[0] if len(rest) > 4 else None
    rows_ref, weight_ref, sums_ref, semaphores = rest[-4:]
    pieces, _, depth = gain_ref.shape
    half = weight_ref.shape[1] // 2
    copies = []
    for piece in range(pieces):
        deep = pl.ds(piece * depth, depth)
        copies.append(
            pltpu.make_async_copy(
                weight_hbm.at[deep, pl.ds(at, 2 * half)], weight_ref.at[deep], semaphores.at[piece]
            )
        )
        copies[-1].start()
    if later_ref is not None:
        for by in range(pieces):
            source = (place[2] + by) % pieces
            copies.append(
                pltpu.make_async_copy(
                    weight_hbm.at[
                        pl.ds(source * depth, depth), pl.ds(at + 2 * half, later_ref.shape[2])
                    ],
                    later_ref.at[by],
                    semaphores.at[pieces + by],
                )
            )
            copies[-1].start()
    squares = jnp.zeros((own_ref.shape[0], 1), jnp.float32)
    for by, part_ref in enumerate((own_ref, from_one, from_two, from_three)):
        source = (place[2] + pieces - by) % pieces
        part = part_ref[...].astype(jnp.float32)
        if kept_ref.shape[1] > half:
            squares = squares + jnp.sum(part * part, axis=1, keepdims=True)
        rows_ref[source] = (part * gain_ref[source]).astype(jnp.bfloat16)
    if kept_ref.shape[1] > half:
        squares = jnp.broadcast_to(squares, (squares.shape[0], lane))
        kept_ref[:, half:] = squares
        sent_ref[:, half:] = squares
    for piece in range(pieces):
        copies[piece].wait()
        result = jnp.dot(
            rows_ref[piece],
            weight_ref[piece * depth : (piece + 1) * depth, :],
            preferred_element_type=jnp.float32,
        )
        if piece > 0:
            result = result + sums_ref[...]
        if piece < pieces - 1:
            sums_ref[...] = result
    kept_ref[:, :half] = result[:, :half]
    sent_ref[:, :half] = result[:, half:]
    for copy in copies[pieces:]:
        copy.wait()


def project_in(place, parts, gain, weight, at, width, with_squares):
    rows, depth = parts[0].shape
    spare = lane if with_squares else 0
    out = jax.ShapeDtypeStruct((rows, width // 2 + spare), jnp.float32)
    outs = [out, out]
    if not with_squares:
        later = weight.shape[1] - at - width
        outs.append(jax.ShapeDtypeStruct((len(parts), depth, later), weight.dtype))
    whole = pl.BlockSpec(memory_space=pltpu.VMEM)
    return pl.pallas_call(
        functools.partial(project_in_kernel, at=at),
        out_shape=outs,
        in_specs=[pl.BlockSpec(memory_space=pltpu.SMEM)]
        + [whole] * 5
        + [pl.BlockSpec(memory_space=pltpu.HBM)],
        out_specs=[whole] * len(outs),
        scratch_shapes=[
            pltpu.VMEM((len(parts), rows, depth), jnp.bfloat16),
            pltpu.VMEM((weight.shape[0], width), jnp.bfloat16),
            pltpu.VMEM((rows, width), jnp.float32),
            pltpu.SemaphoreType.DMA((2 * len(parts),)),
        ],
        cost_estimate=pl.CostEstimate(
            flops=2 * rows * weight.shape[0] * width,
            bytes_accessed=2 * weight.shape[0] * width + 8 * rows * out.shape[1],
            transcendentals=0,
        ),
        compiler_params=pltpu.CompilerParams(vmem_limit_bytes=48 << 20),
        name="project_kv" if with_squares else "project_q",
    )(place, *parts, gain, weight)


def keyval_rotate_kernel(kept_ref, arrived_ref, cosine_ref, sine_ref, out_ref, shrink_ref, *, features):
    total = kept_ref[...] + arrived_ref[...]
    shrink = lax.rsqrt(total[:, lane:] / features + epsilon)
    shrink_ref[...] = shrink
    values = total[:, :lane] * shrink
    turned = pltpu.roll(values, lane // 2, 1)
    result = (values * cosine_ref[...] + turned * sine_ref[...]).astype(out_ref.dtype)
    for copy in range(out_ref.shape[0]):
        out_ref[copy] = result


def keyval_rotate(kept, arrived, cosine, sine, copies, features):
    whole = pl.BlockSpec(memory_space=pltpu.VMEM)
    rows = kept.shape[0]
    return pl.pallas_call(
        functools.partial(keyval_rotate_kernel, features=features),
        out_shape=(
            jax.ShapeDtypeStruct((copies, rows, lane), jnp.bfloat16),
            jax.ShapeDtypeStruct((rows, lane), jnp.float32),
        ),
        in_specs=[whole] * 4,
        out_specs=(whole, whole),
        compiler_params=pltpu.CompilerParams(vmem_limit_bytes=8 << 20),
        name="keyval_rotate",
    )(kept, arrived, cosine, sine)


def query_rotate_kernel(kept_ref, arrived_ref, shrink_ref, cosine_ref, sine_ref, out_ref):
    for at in range(0, out_ref.shape[1], lane):
        head = slice(at, at + lane)
        values = (kept_ref[:, head] + arrived_ref[:, head]) * shrink_ref[...]
        turned = pltpu.roll(values, lane // 2, 1)
        out_ref[:, head] = (values * cosine_ref[...] + turned * sine_ref[...]).astype(out_ref.dtype)


def query_rotate(kept, arrived, shrink, cosine, sine):
    whole = pl.BlockSpec(memory_space=pltpu.VMEM)
    return pl.pallas_call(
        query_rotate_kernel,
        out_shape=jax.ShapeDtypeStruct(kept.shape, jnp.bfloat16),
        in_specs=[whole] * 5,
        out_specs=whole,
        cost_estimate=pl.CostEstimate(flops=0, bytes_accessed=12 * kept.size * 8, transcendentals=0),
        compiler_params=pltpu.CompilerParams(vmem_limit_bytes=8 << 20),
        name="query_rotate",
    )(kept, arrived, shrink, cosine, sine)


def project_out_kernel(mine_ref, other_ref, weight_ref, *outs):
    half = mine_ref.shape[1]
    over_last = (((1,), (1,)), ((), ()))
    for by, out_ref in enumerate(outs):
        result = lax.dot_general(
            mine_ref[...], weight_ref[by, :, :half], over_last, preferred_element_type=jnp.float32
        ) + lax.dot_general(
            other_ref[...], weight_ref[by, :, half:], over_last, preferred_element_type=jnp.float32
        )
        out_ref[...] = result.astype(out_ref.dtype)


def project_out(mine, other, weight):
    rows, half = mine.shape
    pieces, depth, _ = weight.shape
    shape = jax.ShapeDtypeStruct((rows, depth), jnp.bfloat16)
    whole = pl.BlockSpec(memory_space=pltpu.VMEM)
    return pl.pallas_call(
        project_out_kernel,
        out_shape=[shape] * pieces,
        in_specs=[whole] * 3,
        out_specs=[whole] * pieces,
        cost_estimate=pl.CostEstimate(
            flops=2 * rows * weight.size,
            bytes_accessed=2 * weight.size + 2 * rows * depth * pieces,
            transcendentals=0,
        ),
        compiler_params=pltpu.CompilerParams(vmem_limit_bytes=48 << 20),
        name="project_out",
    )(mine, other, weight)


def joined_kernel(place, first_ref, first_other_ref, second_ref, second_other_ref, out_ref):
    runs = first_ref.shape[1] // lane

    def write(even_ref, odd_ref):
        for run in range(runs):
            here = slice(run * lane, (run + 1) * lane)
            out_ref[:, 2 * run * lane : (2 * run + 1) * lane] = even_ref[:, here]
            out_ref[:, (2 * run + 1) * lane : (2 * run + 2) * lane] = odd_ref[:, here]

    @pl.when(place[0] == 0)
    def _():
        write(first_ref, first_other_ref)

    @pl.when(place[0] != 0)
    def _():
        write(second_other_ref, second_ref)


def joined(place, first, first_other, second, second_other):
    whole = pl.BlockSpec(memory_space=pltpu.VMEM)
    return pl.pallas_call(
        joined_kernel,
        out_shape=jax.ShapeDtypeStruct((first.shape[0], 2 * first.shape[1]), first.dtype),
        in_specs=[pl.BlockSpec(memory_space=pltpu.SMEM)] + [whole] * 4,
        out_specs=whole,
        compiler_params=pltpu.CompilerParams(vmem_limit_bytes=8 << 20),
        name="joined",
    )(place, first, first_other, second, second_other)


def local(
    patches,
    merge_gain,
    merge_first,
    merge_second,
    text_embeds,
    positions,
    segments,
    norm_gain,
    query_weight,
    keyval_weight,
    out_weight,
):
    count = patches.shape[0]
    width = merge_gain.shape[0]
    blocks, rows_here, slice_width = text_embeds.shape
    seq_len = segments.shape[0]
    block_len = seq_len // blocks
    section_index = lax.axis_index("section")
    cycle_index = lax.axis_index("blk")
    model_index = lax.axis_index("mp")
    n_mp = lax.axis_size("mp")
    n_blk = lax.axis_size("blk")
    first_core = section_index == 0
    head_size = keyval_weight.shape[4]
    rows = blocks * rows_here
    layers = 2

    query_own = query_weight[0]
    keyval_own = keyval_weight[0].reshape(keyval_weight.shape[1], 2 * head_size)
    out_own = out_weight[0]
    heads_half = query_own.shape[1] // 2
    weight_half = query_own.shape[0] // 2

    def packed(core):
        keep_rows = slice(core * weight_half, (core + 1) * weight_half)
        query_rows, keyval_rows = query_own[keep_rows], keyval_own[keep_rows]
        out_rows = out_own[:, keep_rows].T
        halves = (core, 1 - core)
        parts = [keyval_rows[:, half * head_size : (half + 1) * head_size] for half in halves]
        parts += [query_rows[:, half * heads_half : (half + 1) * heads_half] for half in halves]
        parts += [out_rows[:, half * heads_half : (half + 1) * heads_half] for half in halves]
        return jnp.concatenate(parts, axis=1)

    for_first, for_second = packed(0), packed(1)
    weight_keep = jnp.where(first_core, for_first, for_second)
    weight_other = swapped(jnp.where(first_core, for_second, for_first))
    keyval_width = 2 * head_size
    weight_full = []
    for home in range(layers):
        mine = jnp.where(section_index == home, weight_keep, weight_other)
        weight_full.append(lax.all_gather(mine, "blk", axis=0, tiled=True))
    gain_half = norm_gain[0].reshape(-1, 2, lane)
    gain_keep = jnp.where(first_core, gain_half[:, 0], gain_half[:, 1])
    gain_send = jnp.where(first_core, gain_half[:, 1], gain_half[:, 0])
    gain_other = swapped(gain_send)
    gain_layers = [
        jnp.where(first_core, gain_keep, gain_other).reshape(n_mp, 1, -1),
        jnp.where(first_core, gain_other, gain_keep).reshape(n_mp, 1, -1),
    ]

    inner = merger_inner(patches, merge_gain, merge_first)
    place = jnp.stack([section_index, cycle_index, model_index]).astype(jnp.int32)
    own, *terms = merger_outer(place, inner, swapped(inner), merge_second, n_mp)
    total = own.astype(jnp.float32)
    for part in [moved(terms[by - 1], "mp", by) for by in (2, 1, 3)]:
        total = total + part.astype(jnp.float32)
    merged_terms = lax.all_to_all(
        total.astype(jnp.bfloat16).reshape(n_blk, -1, total.shape[1]), "blk", 0, 0, tiled=True
    )

    row_where = (
        jnp.arange(blocks)[:, None] * block_len
        + cycle_index * rows_here
        + jnp.arange(rows_here)[None, :]
    ).reshape(-1)
    starts = jnp.stack([jnp.sum(segments < 1), jnp.sum(segments < 2)])
    scalars = jnp.concatenate([starts, jnp.stack([cycle_index, section_index])]).astype(jnp.int32)
    is_visual = (positions[None, :] == row_where[:, None]).astype(jnp.bfloat16)
    has_visual = jnp.max(is_visual, axis=1, keepdims=True)
    text_rows = my_half(text_embeds.reshape(rows, slice_width), 1, section_index)
    cosine, sine = rope_tables(row_where, head_size)
    cosine = jnp.concatenate([cosine, cosine], axis=1)
    sine = jnp.concatenate([-sine, sine], axis=1)
    keyval_cosine = jnp.where(first_core, cosine, 1.0)
    keyval_sine = jnp.where(first_core, sine, 0.0)
    early = (scalars, is_visual, has_visual, text_rows, cosine, sine, keyval_cosine, keyval_sine)
    merged_terms, early = lax.optimization_barrier((merged_terms, early))
    scalars, is_visual, has_visual, text_rows, cosine, sine, keyval_cosine, keyval_sine = early
    merged_mine = jnp.sum(merged_terms.astype(jnp.float32), axis=0).astype(jnp.bfloat16)
    merged = spread(merged_mine).reshape(n_blk * merged_mine.shape[0], -1)
    picked = jnp.dot(is_visual, merged, preferred_element_type=jnp.float32).astype(jnp.bfloat16)
    state = jnp.where(has_visual > 0, picked, text_rows)


    results = []
    for layer_index in range(layers):
        parts = [state] + [moved(state, "mp", by) for by in (1, 2, 3)]
        gain = gain_layers[layer_index]
        weight = weight_full[layer_index]
        kept, sent = project_in(place, parts, gain, weight, 0, keyval_width, True)
        keyval_copies, shrink = keyval_rotate(
            kept, swapped(sent), keyval_cosine, keyval_sine, n_blk, n_mp * slice_width
        )
        keyval_copies, parts = lax.optimization_barrier((keyval_copies, parts))
        kept, sent, out_weight_here = project_in(
            place, parts, gain, weight, keyval_width, 2 * heads_half, False
        )
        gathered = lax.all_to_all(keyval_copies, "blk", 0, 0, tiled=True)
        gathered, kept, arrived = lax.optimization_barrier((gathered, kept, swapped(sent)))
        query = query_rotate(kept, arrived, shrink, cosine, sine)
        gathered = gathered.reshape(n_blk, blocks, rows_here, head_size)
        attended = attention(scalars, query, gathered, swapped(gathered))
        attended_other = swapped(attended)
        own, *terms = project_out(attended, attended_other, out_weight_here)
        arrived = [moved(terms[by - 1], "mp", by) for by in (2, 1, 3)]
        total = state.astype(jnp.float32) + own.astype(jnp.float32)
        for part in arrived:
            total = total + part.astype(jnp.float32)
        state = total.astype(jnp.bfloat16)
        results.append(state)

    first_other = swapped(results[0])
    second_other = swapped(results[1])
    hidden = joined(place, results[0], first_other, results[1], second_other)
    return hidden.reshape(1, blocks, rows_here, slice_width)


def solution(mesh):
    return jax.shard_map(
        local,
        mesh=mesh,
        in_specs=(
            P("section", None),
            P(),
            P(None, ("blk", "mp")),
            P(("blk", "mp"), None),
            P(None, "blk", "mp"),
            P(),
            P(),
            P("section", None),
            P("section", "blk", "mp"),
            P("section", "blk", "mp", None, None),
            P("section", "mp", "blk"),
        ),
        out_specs=P("section", None, "blk", "mp"),
        check_vma=False,
    )
```

```python
import functools
import math

import jax
import jax.numpy as jnp
from jax import lax
from jax.experimental import pallas as pl
from jax.experimental.pallas import tpu as pltpu
from jax.sharding import PartitionSpec as P

epsilon = 1e-06
rope_base = 1000000.0
lane = 128


def moved(value, axis, by):
    size = lax.axis_size(axis)
    return lax.ppermute(value, axis, [(i, (i + by) % size) for i in range(size)])


def swapped(value):
    return lax.ppermute(value, "section", [(0, 1), (1, 0)])


def rope_tables(where_at, head_size):
    steps_half = jnp.arange(head_size // 2).astype(jnp.float32)
    inverse = jnp.exp(-jnp.log(rope_base) * 2.0 * steps_half / head_size)
    angles = where_at.astype(jnp.float32)[:, None] * inverse[None, :]
    return (jnp.cos(angles), jnp.sin(angles))


def my_half(value, axis, section_index):
    shape = value.shape
    runs = shape[axis] // (2 * lane)
    split = value.reshape(shape[:axis] + (runs, 2, lane) + shape[axis + 1 :])
    index = [slice(None)] * split.ndim
    index[axis + 1] = 0
    even = split[tuple(index)]
    index[axis + 1] = 1
    odd = split[tuple(index)]
    picked = jnp.where(section_index == 0, even, odd)
    return picked.reshape(shape[:axis] + (runs * lane,) + shape[axis + 1 :])


def spread(value):
    size = lax.axis_size("blk")
    copies = jnp.broadcast_to(value[None], (size,) + value.shape)
    return lax.all_to_all(copies, "blk", 0, 0, tiled=True)


def attention_kernel(scalars, query_ref, mine_ref, other_ref, out_ref, *, chunk_runs, blocks_from):
    runs, _, run, head_size = mine_ref.shape
    blocks = out_ref.shape[0] // run
    heads = query_ref.shape[1] // head_size
    rows = heads * run
    chunk = chunk_runs * run
    per_block = runs // chunk_runs
    block_len = runs * run
    start_one, start_two, cycle, section = scalars[0], scalars[1], scalars[2], scalars[3]
    factor = 1.0 / head_size**0.5 * math.log2(math.e)

    def stripes(key_ref, value_ref):
        def stripe(at, carry):
            block = blocks_from + at
            row_from = pl.multiple_of(at * run, run)
            first = block * block_len + cycle * run
            here = query_ref[pl.ds(pl.multiple_of(block * run, run), run), :]
            stacked = jnp.concatenate(
                [here[:, h * head_size : (h + 1) * head_size] for h in range(heads)], axis=0
            )
            row_at = lax.broadcasted_iota(jnp.int32, (rows, 1), 0) % run + first
            row_start = jnp.where(
                row_at >= start_two, start_two, jnp.where(row_at >= start_one, start_one, 0)
            )
            stripe_start = jnp.where(
                first >= start_two, start_two, jnp.where(first >= start_one, start_one, 0)
            )

            def step(index, state):
                top, total, mixed = state
                in_block = index // per_block
                from_run = (index % per_block) * chunk_runs
                key = key_ref[pl.ds(from_run, chunk_runs), in_block].reshape(chunk, head_size)
                value = value_ref[pl.ds(from_run, chunk_runs), in_block].reshape(chunk, head_size)
                scores = lax.dot_general(
                    stacked, key, (((1,), (1,)), ((), ())), preferred_element_type=jnp.float32
                )
                key_at = lax.broadcasted_iota(jnp.int32, (1, chunk), 1) + index * chunk
                allowed = (key_at <= row_at) & (key_at >= row_start)
                scores = jnp.where(allowed, scores * factor, -1e30)
                new_top = jnp.maximum(top, jnp.max(scores, axis=1, keepdims=True))
                fade = jnp.exp2(top - new_top)
                weights = jnp.exp2(scores - new_top)
                total = total * fade + jnp.sum(weights, axis=1, keepdims=True)
                mixed = mixed * fade + jnp.dot(
                    weights.astype(jnp.bfloat16), value, preferred_element_type=jnp.float32
                )
                return new_top, total, mixed

            state = (
                jnp.full((rows, 1), -1e30, jnp.float32),
                jnp.zeros((rows, 1), jnp.float32),
                jnp.zeros((rows, head_size), jnp.float32),
            )
            _, total, mixed = lax.fori_loop(
                stripe_start // chunk, (first + run - 1) // chunk + 1, step, state
            )
            result = (mixed / total).astype(out_ref.dtype)
            for h in range(heads):
                out_ref[pl.ds(row_from, run), h * head_size : (h + 1) * head_size] = result[
                    h * run : (h + 1) * run
                ]
            return carry

        lax.fori_loop(0, blocks, stripe, 0)

    @pl.when(section == 0)
    def _():
        stripes(mine_ref, other_ref)

    @pl.when(section != 0)
    def _():
        stripes(other_ref, mine_ref)


def attention(scalars, query, mine, other, blocks_from, blocks):
    whole = pl.BlockSpec(memory_space=pltpu.VMEM)
    rows = blocks * mine.shape[2]
    return pl.pallas_call(
        functools.partial(
            attention_kernel, chunk_runs=mine.shape[0], blocks_from=blocks_from
        ),
        out_shape=jax.ShapeDtypeStruct((rows, query.shape[1]), query.dtype),
        in_specs=[pl.BlockSpec(memory_space=pltpu.SMEM), whole, whole, whole],
        out_specs=whole,
        cost_estimate=pl.CostEstimate(
            flops=rows * query.shape[1] * mine.size // mine.shape[3],
            bytes_accessed=2 * (2 * rows * query.shape[1] + 2 * mine.size),
            transcendentals=0,
        ),
        compiler_params=pltpu.CompilerParams(vmem_limit_bytes=16 << 20),
        name="attention",
    )(scalars, query, mine, other)


def merger_kernel(patches_ref, gain_ref, weight_ref, out_ref):
    width = gain_ref.shape[1]
    total = jnp.zeros(out_ref.shape, jnp.float32)
    for at in range(0, patches_ref.shape[1], width):
        piece = patches_ref[:, at : at + width].astype(jnp.float32)
        centered = piece - jnp.mean(piece, axis=1, keepdims=True)
        variance = jnp.mean(centered * centered, axis=1, keepdims=True)
        normed = (centered * lax.rsqrt(variance + epsilon) * gain_ref[...]).astype(jnp.bfloat16)
        total = total + jnp.dot(
            normed, weight_ref[at : at + width, :], preferred_element_type=jnp.float32
        )
    out_ref[...] = (0.5 * total * (1.0 + lax.erf(total * math.sqrt(0.5)))).astype(out_ref.dtype)


def merger_inner(patches, merge_gain, merge_first):
    whole = pl.BlockSpec(memory_space=pltpu.VMEM)
    rows, units = patches.shape[0], merge_first.shape[1]
    return pl.pallas_call(
        merger_kernel,
        out_shape=jax.ShapeDtypeStruct((rows, units), jnp.bfloat16),
        in_specs=[whole, whole, whole],
        out_specs=whole,
        cost_estimate=pl.CostEstimate(
            flops=2 * rows * merge_first.size,
            bytes_accessed=2 * (patches.size + merge_first.size),
            transcendentals=0,
        ),
        compiler_params=pltpu.CompilerParams(vmem_limit_bytes=12 << 20),
        name="merger_inner",
    )(patches, merge_gain.reshape(1, -1), merge_first)


def merger_outer_kernel(place, mine_ref, other_ref, weight_ref, *out_refs):
    section = place[0]
    tokens = mine_ref.shape[0]
    runs = out_refs[0].shape[1] // lane
    for by, out_ref in enumerate(out_refs):
        piece = (place[2] + by) % len(out_refs)
        weight = jnp.concatenate(
            [
                weight_ref[
                    :, pl.ds(pl.multiple_of((2 * (piece * runs + run) + section) * lane, lane), lane)
                ]
                for run in range(runs)
            ],
            axis=1,
        )
        for inner_ref, core in ((mine_ref, section), (other_ref, 1 - section)):
            result = jnp.dot(inner_ref[...], weight, preferred_element_type=jnp.float32)
            at = pl.multiple_of(core * tokens, tokens)
            out_ref[pl.ds(at, tokens), :] = result.astype(out_ref.dtype)


def merger_outer(place, mine, other, merge_second, n_mp):
    whole = pl.BlockSpec(memory_space=pltpu.VMEM)
    shape = jax.ShapeDtypeStruct(
        (2 * mine.shape[0], merge_second.shape[1] // 2 // n_mp), jnp.bfloat16
    )
    return pl.pallas_call(
        merger_outer_kernel,
        out_shape=[shape] * n_mp,
        in_specs=[pl.BlockSpec(memory_space=pltpu.SMEM), whole, whole, whole],
        out_specs=[whole] * n_mp,
        compiler_params=pltpu.CompilerParams(vmem_limit_bytes=12 << 20),
        name="merger_outer",
    )(place, mine, other, merge_second)


def project_in_kernel(
    place,
    own_ref,
    from_one,
    from_two,
    from_three,
    gain_ref,
    weight_hbm,
    kept_ref,
    sent_ref,
    *rest,
    at,
):
    later_ref = rest[0] if len(rest) > 4 else None
    rows_ref, weight_ref, sums_ref, semaphores = rest[-4:]
    pieces, _, depth = gain_ref.shape
    half = weight_ref.shape[1] // 2
    copies = []
    for piece in range(pieces):
        deep = pl.ds(piece * depth, depth)
        copies.append(
            pltpu.make_async_copy(
                weight_hbm.at[deep, pl.ds(at, 2 * half)], weight_ref.at[deep], semaphores.at[piece]
            )
        )
        copies[-1].start()
    if later_ref is not None:
        for by in range(pieces):
            source = (place[2] + by) % pieces
            copies.append(
                pltpu.make_async_copy(
                    weight_hbm.at[
                        pl.ds(source * depth, depth), pl.ds(at + 2 * half, later_ref.shape[2])
                    ],
                    later_ref.at[by],
                    semaphores.at[pieces + by],
                )
            )
            copies[-1].start()
    squares = jnp.zeros((own_ref.shape[0], 1), jnp.float32)
    for by, part_ref in enumerate((own_ref, from_one, from_two, from_three)):
        source = (place[2] + pieces - by) % pieces
        part = part_ref[...].astype(jnp.float32)
        if kept_ref.shape[1] > half:
            squares = squares + jnp.sum(part * part, axis=1, keepdims=True)
        rows_ref[source] = (part * gain_ref[source]).astype(jnp.bfloat16)
    if kept_ref.shape[1] > half:
        squares = jnp.broadcast_to(squares, (squares.shape[0], lane))
        kept_ref[:, half:] = squares
        sent_ref[:, half:] = squares
    for piece in range(pieces):
        copies[piece].wait()
        result = jnp.dot(
            rows_ref[piece],
            weight_ref[piece * depth : (piece + 1) * depth, :],
            preferred_element_type=jnp.float32,
        )
        if piece > 0:
            result = result + sums_ref[...]
        if piece < pieces - 1:
            sums_ref[...] = result
    kept_ref[:, :half] = result[:, :half]
    sent_ref[:, :half] = result[:, half:]
    for copy in copies[pieces:]:
        copy.wait()


def project_in(place, parts, gain, weight, at, width, with_squares):
    rows, depth = parts[0].shape
    spare = lane if with_squares else 0
    out = jax.ShapeDtypeStruct((rows, width // 2 + spare), jnp.float32)
    outs = [out, out]
    if not with_squares:
        later = weight.shape[1] - at - width
        outs.append(jax.ShapeDtypeStruct((len(parts), depth, later), weight.dtype))
    whole = pl.BlockSpec(memory_space=pltpu.VMEM)
    return pl.pallas_call(
        functools.partial(project_in_kernel, at=at),
        out_shape=outs,
        in_specs=[pl.BlockSpec(memory_space=pltpu.SMEM)]
        + [whole] * 5
        + [pl.BlockSpec(memory_space=pltpu.HBM)],
        out_specs=[whole] * len(outs),
        scratch_shapes=[
            pltpu.VMEM((len(parts), rows, depth), jnp.bfloat16),
            pltpu.VMEM((weight.shape[0], width), jnp.bfloat16),
            pltpu.VMEM((rows, width), jnp.float32),
            pltpu.SemaphoreType.DMA((2 * len(parts),)),
        ],
        cost_estimate=pl.CostEstimate(
            flops=2 * rows * weight.shape[0] * width,
            bytes_accessed=2 * weight.shape[0] * width + 8 * rows * out.shape[1],
            transcendentals=0,
        ),
        compiler_params=pltpu.CompilerParams(vmem_limit_bytes=48 << 20),
        name="project_kv" if with_squares else "project_q",
    )(place, *parts, gain, weight)


def keyval_rotate_kernel(
    kept_ref, arrived_ref, cosine_ref, sine_ref, out_hbm, shrink_ref, result_ref, semaphores, *, features
):
    total = kept_ref[...] + arrived_ref[...]
    shrink = lax.rsqrt(total[:, lane:] / features + epsilon)
    shrink_ref[...] = shrink
    values = total[:, :lane] * shrink
    turned = pltpu.roll(values, lane // 2, 1)
    result_ref[...] = (values * cosine_ref[...] + turned * sine_ref[...]).astype(result_ref.dtype)
    copies = [
        pltpu.make_async_copy(result_ref, out_hbm.at[index], semaphores.at[index])
        for index in range(out_hbm.shape[0])
    ]
    for copy in copies:
        copy.start()
    for copy in copies:
        copy.wait()


def keyval_rotate(kept, arrived, cosine, sine, copies, features):
    whole = pl.BlockSpec(memory_space=pltpu.VMEM)
    rows = kept.shape[0]
    return pl.pallas_call(
        functools.partial(keyval_rotate_kernel, features=features),
        out_shape=(
            jax.ShapeDtypeStruct((copies, rows, lane), jnp.bfloat16),
            jax.ShapeDtypeStruct((rows, lane), jnp.float32),
        ),
        in_specs=[whole] * 4,
        out_specs=(pl.BlockSpec(memory_space=pltpu.HBM), whole),
        scratch_shapes=[
            pltpu.VMEM((rows, lane), jnp.bfloat16),
            pltpu.SemaphoreType.DMA((copies,)),
        ],
        compiler_params=pltpu.CompilerParams(vmem_limit_bytes=8 << 20),
        name="keyval_rotate",
    )(kept, arrived, cosine, sine)


def query_rotate_kernel(kept_ref, arrived_ref, shrink_ref, cosine_ref, sine_ref, out_ref):
    for at in range(0, out_ref.shape[1], lane):
        head = slice(at, at + lane)
        values = (kept_ref[:, head] + arrived_ref[:, head]) * shrink_ref[...]
        turned = pltpu.roll(values, lane // 2, 1)
        out_ref[:, head] = (values * cosine_ref[...] + turned * sine_ref[...]).astype(out_ref.dtype)


def query_rotate(kept, arrived, shrink, cosine, sine):
    whole = pl.BlockSpec(memory_space=pltpu.VMEM)
    return pl.pallas_call(
        query_rotate_kernel,
        out_shape=jax.ShapeDtypeStruct(kept.shape, jnp.bfloat16),
        in_specs=[whole] * 5,
        out_specs=whole,
        cost_estimate=pl.CostEstimate(flops=0, bytes_accessed=12 * kept.size * 8, transcendentals=0),
        compiler_params=pltpu.CompilerParams(vmem_limit_bytes=8 << 20),
        name="query_rotate",
    )(kept, arrived, shrink, cosine, sine)


def project_out_kernel(mine_ref, other_ref, weight_ref, *outs):
    half = mine_ref.shape[1]
    over_last = (((1,), (1,)), ((), ()))
    for by, out_ref in enumerate(outs):
        result = lax.dot_general(
            mine_ref[...], weight_ref[by, :, :half], over_last, preferred_element_type=jnp.float32
        ) + lax.dot_general(
            other_ref[...], weight_ref[by, :, half:], over_last, preferred_element_type=jnp.float32
        )
        out_ref[...] = result.astype(out_ref.dtype)


def project_out(mine, other, weight):
    rows, half = mine.shape
    pieces, depth, _ = weight.shape
    shape = jax.ShapeDtypeStruct((rows, depth), jnp.bfloat16)
    whole = pl.BlockSpec(memory_space=pltpu.VMEM)
    return pl.pallas_call(
        project_out_kernel,
        out_shape=[shape] * pieces,
        in_specs=[whole] * 3,
        out_specs=[whole] * pieces,
        cost_estimate=pl.CostEstimate(
            flops=2 * rows * weight.size,
            bytes_accessed=2 * weight.size + 2 * rows * depth * pieces,
            transcendentals=0,
        ),
        compiler_params=pltpu.CompilerParams(vmem_limit_bytes=48 << 20),
        name="project_out",
    )(mine, other, weight)


def joined_kernel(place, first_ref, first_other_ref, *refs):
    *seconds, out_ref = refs
    half = len(seconds) // 2
    runs = first_ref.shape[1] // lane

    def write(even_ref, odd_ref, at):
        here = slice(at, at + even_ref.shape[0])
        for run in range(runs):
            columns = slice(run * lane, (run + 1) * lane)
            out_ref[here, 2 * run * lane : (2 * run + 1) * lane] = even_ref[:, columns]
            out_ref[here, (2 * run + 1) * lane : (2 * run + 2) * lane] = odd_ref[:, columns]

    @pl.when(place[0] == 0)
    def _():
        write(first_ref, first_other_ref, 0)

    @pl.when(place[0] != 0)
    def _():
        for part in range(half):
            write(seconds[half + part], seconds[part], part * seconds[part].shape[0])


def joined(place, first, first_other, second, second_other):
    whole = pl.BlockSpec(memory_space=pltpu.VMEM)
    return pl.pallas_call(
        joined_kernel,
        out_shape=jax.ShapeDtypeStruct((first.shape[0], 2 * first.shape[1]), first.dtype),
        in_specs=[pl.BlockSpec(memory_space=pltpu.SMEM)] + [whole] * (2 + 2 * len(second)),
        out_specs=whole,
        compiler_params=pltpu.CompilerParams(vmem_limit_bytes=8 << 20),
        name="joined",
    )(place, first, first_other, *second, *second_other)


def local(
    patches,
    merge_gain,
    merge_first,
    merge_second,
    text_embeds,
    positions,
    segments,
    norm_gain,
    query_weight,
    keyval_weight,
    out_weight,
):
    count = patches.shape[0]
    width = merge_gain.shape[0]
    blocks, rows_here, slice_width = text_embeds.shape
    seq_len = segments.shape[0]
    block_len = seq_len // blocks
    section_index = lax.axis_index("section")
    cycle_index = lax.axis_index("blk")
    model_index = lax.axis_index("mp")
    n_mp = lax.axis_size("mp")
    n_blk = lax.axis_size("blk")
    first_core = section_index == 0
    head_size = keyval_weight.shape[4]
    rows = blocks * rows_here
    layers = 2

    query_own = query_weight[0]
    keyval_own = keyval_weight[0].reshape(keyval_weight.shape[1], 2 * head_size)
    out_own = out_weight[0]
    heads_half = query_own.shape[1] // 2
    weight_half = query_own.shape[0] // 2

    def packed(core):
        keep_rows = slice(core * weight_half, (core + 1) * weight_half)
        query_rows, keyval_rows = query_own[keep_rows], keyval_own[keep_rows]
        out_rows = out_own[:, keep_rows].T
        halves = (core, 1 - core)
        parts = [keyval_rows[:, half * head_size : (half + 1) * head_size] for half in halves]
        parts += [query_rows[:, half * heads_half : (half + 1) * heads_half] for half in halves]
        parts += [out_rows[:, half * heads_half : (half + 1) * heads_half] for half in halves]
        return jnp.concatenate(parts, axis=1)

    for_first, for_second = packed(0), packed(1)
    weight_keep = jnp.where(first_core, for_first, for_second)
    weight_other = swapped(jnp.where(first_core, for_second, for_first))
    keyval_width = 2 * head_size
    weight_full = []
    for home in range(layers):
        mine = jnp.where(section_index == home, weight_keep, weight_other)
        weight_full.append(lax.all_gather(mine, "blk", axis=0, tiled=True))
    gain_half = norm_gain[0].reshape(-1, 2, lane)
    gain_keep = jnp.where(first_core, gain_half[:, 0], gain_half[:, 1])
    gain_send = jnp.where(first_core, gain_half[:, 1], gain_half[:, 0])
    gain_other = swapped(gain_send)
    gain_layers = [
        jnp.where(first_core, gain_keep, gain_other).reshape(n_mp, 1, -1),
        jnp.where(first_core, gain_other, gain_keep).reshape(n_mp, 1, -1),
    ]

    inner = merger_inner(patches, merge_gain, merge_first)
    place = jnp.stack([section_index, cycle_index, model_index]).astype(jnp.int32)
    own, *terms = merger_outer(place, inner, swapped(inner), merge_second, n_mp)
    total = own.astype(jnp.float32)
    for part in [moved(terms[by - 1], "mp", by) for by in (2, 1, 3)]:
        total = total + part.astype(jnp.float32)
    merged_terms = lax.all_to_all(
        total.astype(jnp.bfloat16).reshape(n_blk, -1, total.shape[1]), "blk", 0, 0, tiled=True
    )

    row_where = (
        jnp.arange(blocks)[:, None] * block_len
        + cycle_index * rows_here
        + jnp.arange(rows_here)[None, :]
    ).reshape(-1)
    starts = jnp.stack([jnp.sum(segments < 1), jnp.sum(segments < 2)])
    scalars = jnp.concatenate([starts, jnp.stack([cycle_index, section_index])]).astype(jnp.int32)
    is_visual = (positions[None, :] == row_where[:, None]).astype(jnp.bfloat16)
    has_visual = jnp.max(is_visual, axis=1, keepdims=True)
    text_rows = my_half(text_embeds.reshape(rows, slice_width), 1, section_index)
    cosine, sine = rope_tables(row_where, head_size)
    cosine = jnp.concatenate([cosine, cosine], axis=1)
    sine = jnp.concatenate([-sine, sine], axis=1)
    keyval_cosine = jnp.where(first_core, cosine, 1.0)
    keyval_sine = jnp.where(first_core, sine, 0.0)
    early = (scalars, is_visual, has_visual, text_rows, cosine, sine, keyval_cosine, keyval_sine)
    merged_terms, early = lax.optimization_barrier((merged_terms, early))
    scalars, is_visual, has_visual, text_rows, cosine, sine, keyval_cosine, keyval_sine = early
    merged_mine = jnp.sum(merged_terms.astype(jnp.float32), axis=0).astype(jnp.bfloat16)
    merged = spread(merged_mine).reshape(n_blk * merged_mine.shape[0], -1)
    picked = jnp.dot(is_visual, merged, preferred_element_type=jnp.float32).astype(jnp.bfloat16)
    state = jnp.where(has_visual > 0, picked, text_rows)


    results = []
    for layer_index in range(layers):
        parts = [state] + [moved(state, "mp", by) for by in (1, 2, 3)]
        gain = gain_layers[layer_index]
        weight = weight_full[layer_index]
        kept, sent = project_in(place, parts, gain, weight, 0, keyval_width, True)
        keyval_copies, shrink = keyval_rotate(
            kept, swapped(sent), keyval_cosine, keyval_sine, n_blk, n_mp * slice_width
        )
        keyval_copies, parts = lax.optimization_barrier((keyval_copies, parts))
        kept, sent, out_weight_here = project_in(
            place, parts, gain, weight, keyval_width, 2 * heads_half, False
        )
        gathered = lax.all_to_all(keyval_copies, "blk", 0, 0, tiled=True)
        gathered, kept, arrived = lax.optimization_barrier((gathered, kept, swapped(sent)))
        query = query_rotate(kept, arrived, shrink, cosine, sine)
        gathered = gathered.reshape(n_blk, blocks, rows_here, head_size)
        gathered_other = swapped(gathered)
        parts_of = 1 if layer_index + 1 < layers else 2
        here = blocks // parts_of
        states = []
        for part_index in range(parts_of):
            attended = attention(
                scalars, query, gathered, gathered_other, part_index * here, here
            )
            own, *terms = project_out(attended, swapped(attended), out_weight_here)
            arrived = [moved(terms[by - 1], "mp", by) for by in (2, 1, 3)]
            size = here * rows_here
            total = state[part_index * size : (part_index + 1) * size].astype(jnp.float32)
            total = total + own.astype(jnp.float32)
            for part in arrived:
                total = total + part.astype(jnp.float32)
            states.append(total.astype(jnp.bfloat16))
        state = states[0] if parts_of == 1 else states
        results.append(state)

    first_other = swapped(results[0])
    second = results[1]
    second_other = [swapped(part) for part in second]
    hidden = joined(place, results[0], first_other, second, second_other)
    return hidden.reshape(1, blocks, rows_here, slice_width)


def solution(mesh):
    return jax.shard_map(
        local,
        mesh=mesh,
        in_specs=(
            P("section", None),
            P(),
            P(None, ("blk", "mp")),
            P(("blk", "mp"), None),
            P(None, "blk", "mp"),
            P(),
            P(),
            P("section", None),
            P("section", "blk", "mp"),
            P("section", "blk", "mp", None, None),
            P("section", "mp", "blk"),
        ),
        out_specs=P("section", None, "blk", "mp"),
        check_vma=False,
    )
```

```python
import functools
import math

import jax
import jax.numpy as jnp
from jax import lax
from jax.experimental import pallas as pl
from jax.experimental.pallas import tpu as pltpu
from jax.sharding import PartitionSpec as P

epsilon = 1e-06
rope_base = 1000000.0
lane = 128


def moved(value, axis, by):
    size = lax.axis_size(axis)
    return lax.ppermute(value, axis, [(i, (i + by) % size) for i in range(size)])


def swapped(value):
    return lax.ppermute(value, "section", [(0, 1), (1, 0)])


def rope_tables(where_at, head_size):
    steps_half = jnp.arange(head_size // 2).astype(jnp.float32)
    inverse = jnp.exp(-jnp.log(rope_base) * 2.0 * steps_half / head_size)
    angles = where_at.astype(jnp.float32)[:, None] * inverse[None, :]
    return (jnp.cos(angles), jnp.sin(angles))


def my_half(value, axis, section_index):
    shape = value.shape
    runs = shape[axis] // (2 * lane)
    split = value.reshape(shape[:axis] + (runs, 2, lane) + shape[axis + 1 :])
    index = [slice(None)] * split.ndim
    index[axis + 1] = 0
    even = split[tuple(index)]
    index[axis + 1] = 1
    odd = split[tuple(index)]
    picked = jnp.where(section_index == 0, even, odd)
    return picked.reshape(shape[:axis] + (runs * lane,) + shape[axis + 1 :])


def spread(value):
    size = lax.axis_size("blk")
    copies = jnp.broadcast_to(value[None], (size,) + value.shape)
    return lax.all_to_all(copies, "blk", 0, 0, tiled=True)


def attention_kernel(scalars, query_ref, mine_ref, other_ref, out_ref, *, chunk_runs):
    runs, blocks, run, head_size = mine_ref.shape
    heads = query_ref.shape[1] // head_size
    rows = heads * run
    chunk = chunk_runs * run
    per_block = runs // chunk_runs
    block_len = runs * run
    start_one, start_two, cycle, section = scalars[0], scalars[1], scalars[2], scalars[3]
    factor = 1.0 / head_size**0.5 * math.log2(math.e)

    def stripes(key_ref, value_ref):
        def stripe(block, carry):
            row_from = pl.multiple_of(block * run, run)
            first = block * block_len + cycle * run
            here = query_ref[pl.ds(row_from, run), :]
            stacked = jnp.concatenate(
                [here[:, h * head_size : (h + 1) * head_size] for h in range(heads)], axis=0
            )
            row_at = lax.broadcasted_iota(jnp.int32, (rows, 1), 0) % run + first
            row_start = jnp.where(
                row_at >= start_two, start_two, jnp.where(row_at >= start_one, start_one, 0)
            )
            stripe_start = jnp.where(
                first >= start_two, start_two, jnp.where(first >= start_one, start_one, 0)
            )

            def step(index, state):
                top, total, mixed = state
                in_block = index // per_block
                from_run = (index % per_block) * chunk_runs
                key = key_ref[pl.ds(from_run, chunk_runs), in_block].reshape(chunk, head_size)
                value = value_ref[pl.ds(from_run, chunk_runs), in_block].reshape(chunk, head_size)
                scores = lax.dot_general(
                    stacked, key, (((1,), (1,)), ((), ())), preferred_element_type=jnp.float32
                )
                key_at = lax.broadcasted_iota(jnp.int32, (1, chunk), 1) + index * chunk
                allowed = (key_at <= row_at) & (key_at >= row_start)
                scores = jnp.where(allowed, scores * factor, -1e30)
                new_top = jnp.maximum(top, jnp.max(scores, axis=1, keepdims=True))
                fade = jnp.exp2(top - new_top)
                weights = jnp.exp2(scores - new_top)
                total = total * fade + jnp.sum(weights, axis=1, keepdims=True)
                mixed = mixed * fade + jnp.dot(
                    weights.astype(jnp.bfloat16), value, preferred_element_type=jnp.float32
                )
                return new_top, total, mixed

            state = (
                jnp.full((rows, 1), -1e30, jnp.float32),
                jnp.zeros((rows, 1), jnp.float32),
                jnp.zeros((rows, head_size), jnp.float32),
            )
            _, total, mixed = lax.fori_loop(
                stripe_start // chunk, (first + run - 1) // chunk + 1, step, state
            )
            result = (mixed / total).astype(out_ref.dtype)
            for h in range(heads):
                out_ref[pl.ds(row_from, run), h * head_size : (h + 1) * head_size] = result[
                    h * run : (h + 1) * run
                ]
            return carry

        lax.fori_loop(0, blocks, stripe, 0)

    @pl.when(section == 0)
    def _():
        stripes(mine_ref, other_ref)

    @pl.when(section != 0)
    def _():
        stripes(other_ref, mine_ref)


def attention(scalars, query, mine, other):
    whole = pl.BlockSpec(memory_space=pltpu.VMEM)
    return pl.pallas_call(
        functools.partial(attention_kernel, chunk_runs=mine.shape[0]),
        out_shape=jax.ShapeDtypeStruct(query.shape, query.dtype),
        in_specs=[pl.BlockSpec(memory_space=pltpu.SMEM), whole, whole, whole],
        out_specs=whole,
        cost_estimate=pl.CostEstimate(
            flops=4 * query.size * mine.size // query.shape[1] // 4,
            bytes_accessed=2 * (2 * query.size + 2 * mine.size),
            transcendentals=0,
        ),
        compiler_params=pltpu.CompilerParams(vmem_limit_bytes=16 << 20),
        name="attention",
    )(scalars, query, mine, other)


def weight_packed_kernel(place, query_ref, keyval_ref, out_weight_ref, keep_ref, send_ref):
    rows = keep_ref.shape[0]
    heads, head = query_ref.shape[1] // 2, keyval_ref.shape[1] // 2

    def write(ref, core):
        here = slice(core * rows, (core + 1) * rows)
        turned = out_weight_ref[:, here].T
        at = 0
        for source, width in ((keyval_ref[here, :], head), (query_ref[here, :], heads), (turned, heads)):
            for half in (core, 1 - core):
                ref[:, at : at + width] = source[:, half * width : (half + 1) * width]
                at += width

    for core in range(2):

        @pl.when(place[0] == core)
        def _():
            write(keep_ref, core)
            write(send_ref, 1 - core)


def weight_packed(place, query, keyval, out_weight):
    whole = pl.BlockSpec(memory_space=pltpu.VMEM)
    shard = jax.ShapeDtypeStruct(
        (query.shape[0] // 2, query.shape[1] + keyval.shape[1] + out_weight.shape[0]), query.dtype
    )
    return pl.pallas_call(
        weight_packed_kernel,
        out_shape=(shard, shard),
        in_specs=[pl.BlockSpec(memory_space=pltpu.SMEM)] + [whole] * 3,
        out_specs=(whole, whole),
        compiler_params=pltpu.CompilerParams(vmem_limit_bytes=12 << 20),
        name="weight_packed",
    )(place, query, keyval, out_weight)


def weight_picked_kernel(place, keep_ref, other_ref, out_ref, *, home):
    @pl.when(place[0] == home)
    def _():
        out_ref[...] = keep_ref[...]

    @pl.when(place[0] != home)
    def _():
        out_ref[...] = other_ref[...]


def weight_picked(place, keep, other, home):
    whole = pl.BlockSpec(memory_space=pltpu.VMEM)
    return pl.pallas_call(
        functools.partial(weight_picked_kernel, home=home),
        out_shape=jax.ShapeDtypeStruct(keep.shape, keep.dtype),
        in_specs=[pl.BlockSpec(memory_space=pltpu.SMEM), whole, whole],
        out_specs=whole,
        compiler_params=pltpu.CompilerParams(vmem_limit_bytes=8 << 20),
        name="weight_picked",
    )(place, keep, other)


def merger_kernel(patches_ref, gain_ref, weight_ref, out_ref):
    width = gain_ref.shape[1]
    total = jnp.zeros(out_ref.shape, jnp.float32)
    for at in range(0, patches_ref.shape[1], width):
        piece = patches_ref[:, at : at + width].astype(jnp.float32)
        centered = piece - jnp.mean(piece, axis=1, keepdims=True)
        variance = jnp.mean(centered * centered, axis=1, keepdims=True)
        normed = (centered * lax.rsqrt(variance + epsilon) * gain_ref[...]).astype(jnp.bfloat16)
        total = total + jnp.dot(
            normed, weight_ref[at : at + width, :], preferred_element_type=jnp.float32
        )
    out_ref[...] = (0.5 * total * (1.0 + lax.erf(total * math.sqrt(0.5)))).astype(out_ref.dtype)


def merger_inner(patches, merge_gain, merge_first):
    whole = pl.BlockSpec(memory_space=pltpu.VMEM)
    rows, units = patches.shape[0], merge_first.shape[1]
    return pl.pallas_call(
        merger_kernel,
        out_shape=jax.ShapeDtypeStruct((rows, units), jnp.bfloat16),
        in_specs=[whole, whole, whole],
        out_specs=whole,
        cost_estimate=pl.CostEstimate(
            flops=2 * rows * merge_first.size,
            bytes_accessed=2 * (patches.size + merge_first.size),
            transcendentals=0,
        ),
        compiler_params=pltpu.CompilerParams(vmem_limit_bytes=12 << 20),
        name="merger_inner",
    )(patches, merge_gain.reshape(1, -1), merge_first)


def merger_outer_kernel(place, mine_ref, other_ref, weight_ref, *out_refs):
    section = place[0]
    tokens = mine_ref.shape[0]
    runs = out_refs[0].shape[1] // lane
    for by, out_ref in enumerate(out_refs):
        piece = (place[2] + by) % len(out_refs)
        weight = jnp.concatenate(
            [
                weight_ref[
                    :, pl.ds(pl.multiple_of((2 * (piece * runs + run) + section) * lane, lane), lane)
                ]
                for run in range(runs)
            ],
            axis=1,
        )
        for inner_ref, core in ((mine_ref, section), (other_ref, 1 - section)):
            result = jnp.dot(inner_ref[...], weight, preferred_element_type=jnp.float32)
            at = pl.multiple_of(core * tokens, tokens)
            out_ref[pl.ds(at, tokens), :] = result.astype(out_ref.dtype)


def merger_outer(place, mine, other, merge_second, n_mp):
    whole = pl.BlockSpec(memory_space=pltpu.VMEM)
    shape = jax.ShapeDtypeStruct(
        (2 * mine.shape[0], merge_second.shape[1] // 2 // n_mp), jnp.bfloat16
    )
    return pl.pallas_call(
        merger_outer_kernel,
        out_shape=[shape] * n_mp,
        in_specs=[pl.BlockSpec(memory_space=pltpu.SMEM), whole, whole, whole],
        out_specs=[whole] * n_mp,
        compiler_params=pltpu.CompilerParams(vmem_limit_bytes=12 << 20),
        name="merger_outer",
    )(place, mine, other, merge_second)


def project_in_kernel(
    place,
    own_ref,
    from_one,
    from_two,
    from_three,
    gain_ref,
    weight_hbm,
    kept_ref,
    sent_ref,
    *rest,
    at,
):
    later_ref = rest[0] if len(rest) > 4 else None
    rows_ref, weight_ref, sums_ref, semaphores = rest[-4:]
    pieces, _, depth = gain_ref.shape
    half = weight_ref.shape[1] // 2
    copies = []
    for piece in range(pieces):
        deep = pl.ds(piece * depth, depth)
        copies.append(
            pltpu.make_async_copy(
                weight_hbm.at[deep, pl.ds(at, 2 * half)], weight_ref.at[deep], semaphores.at[piece]
            )
        )
        copies[-1].start()
    if later_ref is not None:
        for by in range(pieces):
            source = (place[2] + by) % pieces
            copies.append(
                pltpu.make_async_copy(
                    weight_hbm.at[
                        pl.ds(source * depth, depth), pl.ds(at + 2 * half, later_ref.shape[2])
                    ],
                    later_ref.at[by],
                    semaphores.at[pieces + by],
                )
            )
            copies[-1].start()
    squares = jnp.zeros((own_ref.shape[0], 1), jnp.float32)
    for by, part_ref in enumerate((own_ref, from_one, from_two, from_three)):
        source = (place[2] + pieces - by) % pieces
        part = part_ref[...].astype(jnp.float32)
        if kept_ref.shape[1] > half:
            squares = squares + jnp.sum(part * part, axis=1, keepdims=True)
        rows_ref[source] = (part * gain_ref[source]).astype(jnp.bfloat16)
    if kept_ref.shape[1] > half:
        squares = jnp.broadcast_to(squares, (squares.shape[0], lane))
        kept_ref[:, half:] = squares
        sent_ref[:, half:] = squares
    for piece in range(pieces):
        copies[piece].wait()
        result = jnp.dot(
            rows_ref[piece],
            weight_ref[piece * depth : (piece + 1) * depth, :],
            preferred_element_type=jnp.float32,
        )
        if piece > 0:
            result = result + sums_ref[...]
        if piece < pieces - 1:
            sums_ref[...] = result
    kept_ref[:, :half] = result[:, :half]
    sent_ref[:, :half] = result[:, half:]
    for copy in copies[pieces:]:
        copy.wait()


def project_in(place, parts, gain, weight, at, width, with_squares):
    rows, depth = parts[0].shape
    spare = lane if with_squares else 0
    out = jax.ShapeDtypeStruct((rows, width // 2 + spare), jnp.float32)
    outs = [out, out]
    if not with_squares:
        later = weight.shape[1] - at - width
        outs.append(jax.ShapeDtypeStruct((len(parts), depth, later), weight.dtype))
    whole = pl.BlockSpec(memory_space=pltpu.VMEM)
    return pl.pallas_call(
        functools.partial(project_in_kernel, at=at),
        out_shape=outs,
        in_specs=[pl.BlockSpec(memory_space=pltpu.SMEM)]
        + [whole] * 5
        + [pl.BlockSpec(memory_space=pltpu.HBM)],
        out_specs=[whole] * len(outs),
        scratch_shapes=[
            pltpu.VMEM((len(parts), rows, depth), jnp.bfloat16),
            pltpu.VMEM((weight.shape[0], width), jnp.bfloat16),
            pltpu.VMEM((rows, width), jnp.float32),
            pltpu.SemaphoreType.DMA((2 * len(parts),)),
        ],
        cost_estimate=pl.CostEstimate(
            flops=2 * rows * weight.shape[0] * width,
            bytes_accessed=2 * weight.shape[0] * width + 8 * rows * out.shape[1],
            transcendentals=0,
        ),
        compiler_params=pltpu.CompilerParams(vmem_limit_bytes=48 << 20),
        name="project_kv" if with_squares else "project_q",
    )(place, *parts, gain, weight)


def keyval_rotate_kernel(kept_ref, arrived_ref, cosine_ref, sine_ref, out_ref, shrink_ref, *, features):
    total = kept_ref[...] + arrived_ref[...]
    shrink = lax.rsqrt(total[:, lane:] / features + epsilon)
    shrink_ref[...] = shrink
    values = total[:, :lane] * shrink
    turned = pltpu.roll(values, lane // 2, 1)
    result = (values * cosine_ref[...] + turned * sine_ref[...]).astype(out_ref.dtype)
    for copy in range(out_ref.shape[0]):
        out_ref[copy] = result


def keyval_rotate(kept, arrived, cosine, sine, copies, features):
    whole = pl.BlockSpec(memory_space=pltpu.VMEM)
    rows = kept.shape[0]
    return pl.pallas_call(
        functools.partial(keyval_rotate_kernel, features=features),
        out_shape=(
            jax.ShapeDtypeStruct((copies, rows, lane), jnp.bfloat16),
            jax.ShapeDtypeStruct((rows, lane), jnp.float32),
        ),
        in_specs=[whole] * 4,
        out_specs=(whole, whole),
        compiler_params=pltpu.CompilerParams(vmem_limit_bytes=8 << 20),
        name="keyval_rotate",
    )(kept, arrived, cosine, sine)


def query_rotate_kernel(kept_ref, arrived_ref, shrink_ref, cosine_ref, sine_ref, out_ref):
    for at in range(0, out_ref.shape[1], lane):
        head = slice(at, at + lane)
        values = (kept_ref[:, head] + arrived_ref[:, head]) * shrink_ref[...]
        turned = pltpu.roll(values, lane // 2, 1)
        out_ref[:, head] = (values * cosine_ref[...] + turned * sine_ref[...]).astype(out_ref.dtype)


def query_rotate(kept, arrived, shrink, cosine, sine):
    whole = pl.BlockSpec(memory_space=pltpu.VMEM)
    return pl.pallas_call(
        query_rotate_kernel,
        out_shape=jax.ShapeDtypeStruct(kept.shape, jnp.bfloat16),
        in_specs=[whole] * 5,
        out_specs=whole,
        cost_estimate=pl.CostEstimate(flops=0, bytes_accessed=12 * kept.size * 8, transcendentals=0),
        compiler_params=pltpu.CompilerParams(vmem_limit_bytes=8 << 20),
        name="query_rotate",
    )(kept, arrived, shrink, cosine, sine)


def project_out_kernel(mine_ref, other_ref, weight_ref, *outs):
    half = mine_ref.shape[1]
    over_last = (((1,), (1,)), ((), ()))
    for by, out_ref in enumerate(outs):
        result = lax.dot_general(
            mine_ref[...], weight_ref[by, :, :half], over_last, preferred_element_type=jnp.float32
        ) + lax.dot_general(
            other_ref[...], weight_ref[by, :, half:], over_last, preferred_element_type=jnp.float32
        )
        out_ref[...] = result.astype(out_ref.dtype)


def project_out(mine, other, weight):
    rows, half = mine.shape
    pieces, depth, _ = weight.shape
    shape = jax.ShapeDtypeStruct((rows, depth), jnp.bfloat16)
    whole = pl.BlockSpec(memory_space=pltpu.VMEM)
    return pl.pallas_call(
        project_out_kernel,
        out_shape=[shape] * pieces,
        in_specs=[whole] * 3,
        out_specs=[whole] * pieces,
        cost_estimate=pl.CostEstimate(
            flops=2 * rows * weight.size,
            bytes_accessed=2 * weight.size + 2 * rows * depth * pieces,
            transcendentals=0,
        ),
        compiler_params=pltpu.CompilerParams(vmem_limit_bytes=48 << 20),
        name="project_out",
    )(mine, other, weight)


def joined_kernel(place, first_ref, first_other_ref, second_ref, second_other_ref, out_ref):
    runs = first_ref.shape[1] // lane

    def write(even_ref, odd_ref):
        for run in range(runs):
            here = slice(run * lane, (run + 1) * lane)
            out_ref[:, 2 * run * lane : (2 * run + 1) * lane] = even_ref[:, here]
            out_ref[:, (2 * run + 1) * lane : (2 * run + 2) * lane] = odd_ref[:, here]

    @pl.when(place[0] == 0)
    def _():
        write(first_ref, first_other_ref)

    @pl.when(place[0] != 0)
    def _():
        write(second_other_ref, second_ref)


def joined(place, first, first_other, second, second_other):
    whole = pl.BlockSpec(memory_space=pltpu.VMEM)
    return pl.pallas_call(
        joined_kernel,
        out_shape=jax.ShapeDtypeStruct((first.shape[0], 2 * first.shape[1]), first.dtype),
        in_specs=[pl.BlockSpec(memory_space=pltpu.SMEM)] + [whole] * 4,
        out_specs=whole,
        compiler_params=pltpu.CompilerParams(vmem_limit_bytes=8 << 20),
        name="joined",
    )(place, first, first_other, second, second_other)


def local(
    patches,
    merge_gain,
    merge_first,
    merge_second,
    text_embeds,
    positions,
    segments,
    norm_gain,
    query_weight,
    keyval_weight,
    out_weight,
):
    count = patches.shape[0]
    width = merge_gain.shape[0]
    blocks, rows_here, slice_width = text_embeds.shape
    seq_len = segments.shape[0]
    block_len = seq_len // blocks
    section_index = lax.axis_index("section")
    cycle_index = lax.axis_index("blk")
    model_index = lax.axis_index("mp")
    n_mp = lax.axis_size("mp")
    n_blk = lax.axis_size("blk")
    first_core = section_index == 0
    head_size = keyval_weight.shape[4]
    rows = blocks * rows_here
    layers = 2

    query_own = query_weight[0]
    keyval_own = keyval_weight[0].reshape(keyval_weight.shape[1], 2 * head_size)
    out_own = out_weight[0]
    heads_half = query_own.shape[1] // 2

    place = jnp.stack([section_index, cycle_index, model_index]).astype(jnp.int32)
    weight_keep, weight_send = weight_packed(place, query_own, keyval_own, out_own)
    weight_other = swapped(weight_send)
    keyval_width = 2 * head_size
    weight_full = []
    for home in range(layers):
        mine = weight_picked(place, weight_keep, weight_other, home)
        weight_full.append(lax.all_gather(mine, "blk", axis=0, tiled=True))
    gain_half = norm_gain[0].reshape(-1, 2, lane)
    gain_keep = jnp.where(first_core, gain_half[:, 0], gain_half[:, 1])
    gain_send = jnp.where(first_core, gain_half[:, 1], gain_half[:, 0])
    gain_other = swapped(gain_send)
    gain_layers = [
        jnp.where(first_core, gain_keep, gain_other).reshape(n_mp, 1, -1),
        jnp.where(first_core, gain_other, gain_keep).reshape(n_mp, 1, -1),
    ]

    inner = merger_inner(patches, merge_gain, merge_first)
    own, *terms = merger_outer(place, inner, swapped(inner), merge_second, n_mp)
    total = own.astype(jnp.float32)
    for part in [moved(terms[by - 1], "mp", by) for by in (2, 1, 3)]:
        total = total + part.astype(jnp.float32)
    merged_terms = lax.all_to_all(
        total.astype(jnp.bfloat16).reshape(n_blk, -1, total.shape[1]), "blk", 0, 0, tiled=True
    )

    row_where = (
        jnp.arange(blocks)[:, None] * block_len
        + cycle_index * rows_here
        + jnp.arange(rows_here)[None, :]
    ).reshape(-1)
    starts = jnp.stack([jnp.sum(segments < 1), jnp.sum(segments < 2)])
    scalars = jnp.concatenate([starts, jnp.stack([cycle_index, section_index])]).astype(jnp.int32)
    is_visual = (positions[None, :] == row_where[:, None]).astype(jnp.bfloat16)
    has_visual = jnp.max(is_visual, axis=1, keepdims=True)
    text_rows = my_half(text_embeds.reshape(rows, slice_width), 1, section_index)
    cosine, sine = rope_tables(row_where, head_size)
    cosine = jnp.concatenate([cosine, cosine], axis=1)
    sine = jnp.concatenate([-sine, sine], axis=1)
    keyval_cosine = jnp.where(first_core, cosine, 1.0)
    keyval_sine = jnp.where(first_core, sine, 0.0)
    early = (scalars, is_visual, has_visual, text_rows, cosine, sine, keyval_cosine, keyval_sine)
    merged_terms, early = lax.optimization_barrier((merged_terms, early))
    scalars, is_visual, has_visual, text_rows, cosine, sine, keyval_cosine, keyval_sine = early
    merged_mine = jnp.sum(merged_terms.astype(jnp.float32), axis=0).astype(jnp.bfloat16)
    merged = spread(merged_mine).reshape(n_blk * merged_mine.shape[0], -1)
    picked = jnp.dot(is_visual, merged, preferred_element_type=jnp.float32).astype(jnp.bfloat16)
    state = jnp.where(has_visual > 0, picked, text_rows)


    results = []
    for layer_index in range(layers):
        parts = [state] + [moved(state, "mp", by) for by in (1, 2, 3)]
        gain = gain_layers[layer_index]
        weight = weight_full[layer_index]
        kept, sent = project_in(place, parts, gain, weight, 0, keyval_width, True)
        keyval_copies, shrink = keyval_rotate(
            kept, swapped(sent), keyval_cosine, keyval_sine, n_blk, n_mp * slice_width
        )
        keyval_copies, parts = lax.optimization_barrier((keyval_copies, parts))
        kept, sent, out_weight_here = project_in(
            place, parts, gain, weight, keyval_width, 2 * heads_half, False
        )
        gathered = lax.all_to_all(keyval_copies, "blk", 0, 0, tiled=True)
        gathered, kept, arrived = lax.optimization_barrier((gathered, kept, swapped(sent)))
        query = query_rotate(kept, arrived, shrink, cosine, sine)
        gathered = gathered.reshape(n_blk, blocks, rows_here, head_size)
        attended = attention(scalars, query, gathered, swapped(gathered))
        attended_other = swapped(attended)
        own, *terms = project_out(attended, attended_other, out_weight_here)
        arrived = [moved(terms[by - 1], "mp", by) for by in (2, 1, 3)]
        total = state.astype(jnp.float32) + own.astype(jnp.float32)
        for part in arrived:
            total = total + part.astype(jnp.float32)
        state = total.astype(jnp.bfloat16)
        results.append(state)

    first_other = swapped(results[0])
    second_other = swapped(results[1])
    hidden = joined(place, results[0], first_other, results[1], second_other)
    return hidden.reshape(1, blocks, rows_here, slice_width)


def solution(mesh):
    return jax.shard_map(
        local,
        mesh=mesh,
        in_specs=(
            P("section", None),
            P(),
            P(None, ("blk", "mp")),
            P(("blk", "mp"), None),
            P(None, "blk", "mp"),
            P(),
            P(),
            P("section", None),
            P("section", "blk", "mp"),
            P("section", "blk", "mp", None, None),
            P("section", "mp", "blk"),
        ),
        out_specs=P("section", None, "blk", "mp"),
        check_vma=False,
    )
```

```python
import functools
import math

import jax
import jax.numpy as jnp
from jax import lax
from jax.experimental import pallas as pl
from jax.experimental.pallas import tpu as pltpu
from jax.sharding import PartitionSpec as P

epsilon = 1e-06
rope_base = 1000000.0
lane = 128


def moved(value, axis, by):
    size = lax.axis_size(axis)
    return lax.ppermute(value, axis, [(i, (i + by) % size) for i in range(size)])


def swapped(value):
    return lax.ppermute(value, "section", [(0, 1), (1, 0)])


def rope_tables(where_at, head_size):
    steps_half = jnp.arange(head_size // 2).astype(jnp.float32)
    inverse = jnp.exp(-jnp.log(rope_base) * 2.0 * steps_half / head_size)
    angles = where_at.astype(jnp.float32)[:, None] * inverse[None, :]
    return (jnp.cos(angles), jnp.sin(angles))


def my_half(value, axis, section_index):
    shape = value.shape
    runs = shape[axis] // (2 * lane)
    split = value.reshape(shape[:axis] + (runs, 2, lane) + shape[axis + 1 :])
    index = [slice(None)] * split.ndim
    index[axis + 1] = 0
    even = split[tuple(index)]
    index[axis + 1] = 1
    odd = split[tuple(index)]
    picked = jnp.where(section_index == 0, even, odd)
    return picked.reshape(shape[:axis] + (runs * lane,) + shape[axis + 1 :])


def spread(value):
    size = lax.axis_size("blk")
    copies = jnp.broadcast_to(value[None], (size,) + value.shape)
    return lax.all_to_all(copies, "blk", 0, 0, tiled=True)


def attention_kernel(scalars, query_ref, mine_ref, other_ref, out_ref, *, chunk_runs):
    runs, blocks, run, head_size = mine_ref.shape
    heads = query_ref.shape[1] // head_size
    rows = heads * run
    chunk = chunk_runs * run
    per_block = runs // chunk_runs
    block_len = runs * run
    start_one, start_two, cycle, section = scalars[0], scalars[1], scalars[2], scalars[3]
    factor = 1.0 / head_size**0.5 * math.log2(math.e)

    def stripes(key_ref, value_ref):
        def stripe(block, carry):
            row_from = pl.multiple_of(block * run, run)
            first = block * block_len + cycle * run
            here = query_ref[pl.ds(row_from, run), :]
            stacked = jnp.concatenate(
                [here[:, h * head_size : (h + 1) * head_size] for h in range(heads)], axis=0
            )
            row_at = lax.broadcasted_iota(jnp.int32, (rows, 1), 0) % run + first
            row_start = jnp.where(
                row_at >= start_two, start_two, jnp.where(row_at >= start_one, start_one, 0)
            )
            stripe_start = jnp.where(
                first >= start_two, start_two, jnp.where(first >= start_one, start_one, 0)
            )

            def step(index, state):
                top, total, mixed = state
                in_block = index // per_block
                from_run = (index % per_block) * chunk_runs
                key = key_ref[pl.ds(from_run, chunk_runs), in_block].reshape(chunk, head_size)
                value = value_ref[pl.ds(from_run, chunk_runs), in_block].reshape(chunk, head_size)
                scores = lax.dot_general(
                    stacked, key, (((1,), (1,)), ((), ())), preferred_element_type=jnp.float32
                )
                key_at = lax.broadcasted_iota(jnp.int32, (1, chunk), 1) + index * chunk
                allowed = (key_at <= row_at) & (key_at >= row_start)
                scores = jnp.where(allowed, scores * factor, -1e30)
                new_top = jnp.maximum(top, jnp.max(scores, axis=1, keepdims=True))
                fade = jnp.exp2(top - new_top)
                weights = jnp.exp2(scores - new_top)
                total = total * fade + jnp.sum(weights, axis=1, keepdims=True)
                mixed = mixed * fade + jnp.dot(
                    weights.astype(jnp.bfloat16), value, preferred_element_type=jnp.float32
                )
                return new_top, total, mixed

            state = (
                jnp.full((rows, 1), -1e30, jnp.float32),
                jnp.zeros((rows, 1), jnp.float32),
                jnp.zeros((rows, head_size), jnp.float32),
            )
            _, total, mixed = lax.fori_loop(
                stripe_start // chunk, (first + run - 1) // chunk + 1, step, state
            )
            result = (mixed / total).astype(out_ref.dtype)
            for h in range(heads):
                out_ref[pl.ds(row_from, run), h * head_size : (h + 1) * head_size] = result[
                    h * run : (h + 1) * run
                ]
            return carry

        lax.fori_loop(0, blocks, stripe, 0)

    @pl.when(section == 0)
    def _():
        stripes(mine_ref, other_ref)

    @pl.when(section != 0)
    def _():
        stripes(other_ref, mine_ref)


def attention(scalars, query, mine, other):
    whole = pl.BlockSpec(memory_space=pltpu.VMEM)
    return pl.pallas_call(
        functools.partial(attention_kernel, chunk_runs=mine.shape[0]),
        out_shape=jax.ShapeDtypeStruct(query.shape, query.dtype),
        in_specs=[pl.BlockSpec(memory_space=pltpu.SMEM), whole, whole, whole],
        out_specs=whole,
        cost_estimate=pl.CostEstimate(
            flops=4 * query.size * mine.size // query.shape[1] // 4,
            bytes_accessed=2 * (2 * query.size + 2 * mine.size),
            transcendentals=0,
        ),
        compiler_params=pltpu.CompilerParams(vmem_limit_bytes=16 << 20),
        name="attention",
    )(scalars, query, mine, other)


def merger_kernel(patches_ref, gain_ref, weight_ref, out_ref):
    width = gain_ref.shape[1]
    total = jnp.zeros(out_ref.shape, jnp.float32)
    for at in range(0, patches_ref.shape[1], width):
        piece = patches_ref[:, at : at + width].astype(jnp.float32)
        centered = piece - jnp.mean(piece, axis=1, keepdims=True)
        variance = jnp.mean(centered * centered, axis=1, keepdims=True)
        normed = (centered * lax.rsqrt(variance + epsilon) * gain_ref[...]).astype(jnp.bfloat16)
        total = total + jnp.dot(
            normed, weight_ref[at : at + width, :], preferred_element_type=jnp.float32
        )
    out_ref[...] = (0.5 * total * (1.0 + lax.erf(total * math.sqrt(0.5)))).astype(out_ref.dtype)


def merger_inner(patches, merge_gain, merge_first):
    whole = pl.BlockSpec(memory_space=pltpu.VMEM)
    rows, units = patches.shape[0], merge_first.shape[1]
    return pl.pallas_call(
        merger_kernel,
        out_shape=jax.ShapeDtypeStruct((rows, units), jnp.bfloat16),
        in_specs=[whole, whole, whole],
        out_specs=whole,
        cost_estimate=pl.CostEstimate(
            flops=2 * rows * merge_first.size,
            bytes_accessed=2 * (patches.size + merge_first.size),
            transcendentals=0,
        ),
        compiler_params=pltpu.CompilerParams(vmem_limit_bytes=12 << 20),
        name="merger_inner",
    )(patches, merge_gain.reshape(1, -1), merge_first)


def merger_outer_kernel(place, mine_ref, other_ref, weight_ref, *out_refs):
    section = place[0]
    tokens = mine_ref.shape[0]
    runs = out_refs[0].shape[1] // lane
    for by, out_ref in enumerate(out_refs):
        piece = (place[2] + by) % len(out_refs)
        weight = jnp.concatenate(
            [
                weight_ref[
                    :, pl.ds(pl.multiple_of((2 * (piece * runs + run) + section) * lane, lane), lane)
                ]
                for run in range(runs)
            ],
            axis=1,
        )
        for inner_ref, core in ((mine_ref, section), (other_ref, 1 - section)):
            result = jnp.dot(inner_ref[...], weight, preferred_element_type=jnp.float32)
            at = pl.multiple_of(core * tokens, tokens)
            out_ref[pl.ds(at, tokens), :] = result.astype(out_ref.dtype)


def merger_outer(place, mine, other, merge_second, n_mp):
    whole = pl.BlockSpec(memory_space=pltpu.VMEM)
    shape = jax.ShapeDtypeStruct(
        (2 * mine.shape[0], merge_second.shape[1] // 2 // n_mp), jnp.bfloat16
    )
    return pl.pallas_call(
        merger_outer_kernel,
        out_shape=[shape] * n_mp,
        in_specs=[pl.BlockSpec(memory_space=pltpu.SMEM), whole, whole, whole],
        out_specs=[whole] * n_mp,
        compiler_params=pltpu.CompilerParams(vmem_limit_bytes=12 << 20),
        name="merger_outer",
    )(place, mine, other, merge_second)


def project_in_kernel(
    place,
    own_ref,
    from_one,
    from_two,
    from_three,
    gain_ref,
    weight_hbm,
    kept_ref,
    sent_ref,
    *rest,
    at,
):
    later_ref = rest[0] if len(rest) > 4 else None
    rows_ref, weight_ref, sums_ref, semaphores = rest[-4:]
    pieces, _, depth = gain_ref.shape
    half = weight_ref.shape[1] // 2
    copies = []
    for piece in range(pieces):
        deep = pl.ds(piece * depth, depth)
        copies.append(
            pltpu.make_async_copy(
                weight_hbm.at[deep, pl.ds(at, 2 * half)], weight_ref.at[deep], semaphores.at[piece]
            )
        )
        copies[-1].start()
    if later_ref is not None:
        for by in range(pieces):
            source = (place[2] + by) % pieces
            copies.append(
                pltpu.make_async_copy(
                    weight_hbm.at[
                        pl.ds(source * depth, depth), pl.ds(at + 2 * half, later_ref.shape[2])
                    ],
                    later_ref.at[by],
                    semaphores.at[pieces + by],
                )
            )
            copies[-1].start()
    squares = jnp.zeros((own_ref.shape[0], 1), jnp.float32)
    for by, part_ref in enumerate((own_ref, from_one, from_two, from_three)):
        source = (place[2] + pieces - by) % pieces
        part = part_ref[...].astype(jnp.float32)
        if kept_ref.shape[1] > half:
            squares = squares + jnp.sum(part * part, axis=1, keepdims=True)
        rows_ref[source] = (part * gain_ref[source]).astype(jnp.bfloat16)
    if kept_ref.shape[1] > half:
        squares = jnp.broadcast_to(squares, (squares.shape[0], lane))
        kept_ref[:, half:] = squares
        sent_ref[:, half:] = squares
    for piece in range(pieces):
        copies[piece].wait()
        result = jnp.dot(
            rows_ref[piece],
            weight_ref[piece * depth : (piece + 1) * depth, :],
            preferred_element_type=jnp.float32,
        )
        if piece > 0:
            result = result + sums_ref[...]
        if piece < pieces - 1:
            sums_ref[...] = result
    kept_ref[:, :half] = result[:, :half]
    sent_ref[:, :half] = result[:, half:]
    for copy in copies[pieces:]:
        copy.wait()


def project_in(place, parts, gain, weight, at, width, with_squares):
    rows, depth = parts[0].shape
    spare = lane if with_squares else 0
    out = jax.ShapeDtypeStruct((rows, width // 2 + spare), jnp.float32)
    outs = [out, out]
    if not with_squares:
        later = weight.shape[1] - at - width
        outs.append(jax.ShapeDtypeStruct((len(parts), depth, later), weight.dtype))
    whole = pl.BlockSpec(memory_space=pltpu.VMEM)
    return pl.pallas_call(
        functools.partial(project_in_kernel, at=at),
        out_shape=outs,
        in_specs=[pl.BlockSpec(memory_space=pltpu.SMEM)]
        + [whole] * 5
        + [pl.BlockSpec(memory_space=pltpu.HBM)],
        out_specs=[whole] * len(outs),
        scratch_shapes=[
            pltpu.VMEM((len(parts), rows, depth), jnp.bfloat16),
            pltpu.VMEM((weight.shape[0], width), jnp.bfloat16),
            pltpu.VMEM((rows, width), jnp.float32),
            pltpu.SemaphoreType.DMA((2 * len(parts),)),
        ],
        cost_estimate=pl.CostEstimate(
            flops=2 * rows * weight.shape[0] * width,
            bytes_accessed=2 * weight.shape[0] * width + 8 * rows * out.shape[1],
            transcendentals=0,
        ),
        compiler_params=pltpu.CompilerParams(vmem_limit_bytes=48 << 20),
        name="project_kv" if with_squares else "project_q",
    )(place, *parts, gain, weight)


def keyval_rotate_kernel(kept_ref, arrived_ref, cosine_ref, sine_ref, out_ref, shrink_ref, *, features):
    total = kept_ref[...] + arrived_ref[...]
    shrink = lax.rsqrt(total[:, lane:] / features + epsilon)
    shrink_ref[...] = shrink
    values = total[:, :lane] * shrink
    turned = pltpu.roll(values, lane // 2, 1)
    result = (values * cosine_ref[...] + turned * sine_ref[...]).astype(out_ref.dtype)
    for copy in range(out_ref.shape[0]):
        out_ref[copy] = result


def keyval_rotate(kept, arrived, cosine, sine, copies, features):
    whole = pl.BlockSpec(memory_space=pltpu.VMEM)
    rows = kept.shape[0]
    return pl.pallas_call(
        functools.partial(keyval_rotate_kernel, features=features),
        out_shape=(
            jax.ShapeDtypeStruct((copies, rows, lane), jnp.bfloat16),
            jax.ShapeDtypeStruct((rows, lane), jnp.float32),
        ),
        in_specs=[whole] * 4,
        out_specs=(whole, whole),
        compiler_params=pltpu.CompilerParams(vmem_limit_bytes=8 << 20),
        name="keyval_rotate",
    )(kept, arrived, cosine, sine)


def query_rotate_kernel(kept_ref, arrived_ref, shrink_ref, cosine_ref, sine_ref, out_ref):
    for at in range(0, out_ref.shape[1], lane):
        head = slice(at, at + lane)
        values = (kept_ref[:, head] + arrived_ref[:, head]) * shrink_ref[...]
        turned = pltpu.roll(values, lane // 2, 1)
        out_ref[:, head] = (values * cosine_ref[...] + turned * sine_ref[...]).astype(out_ref.dtype)


def query_rotate(kept, arrived, shrink, cosine, sine):
    whole = pl.BlockSpec(memory_space=pltpu.VMEM)
    return pl.pallas_call(
        query_rotate_kernel,
        out_shape=jax.ShapeDtypeStruct(kept.shape, jnp.bfloat16),
        in_specs=[whole] * 5,
        out_specs=whole,
        cost_estimate=pl.CostEstimate(flops=0, bytes_accessed=12 * kept.size * 8, transcendentals=0),
        compiler_params=pltpu.CompilerParams(vmem_limit_bytes=8 << 20),
        name="query_rotate",
    )(kept, arrived, shrink, cosine, sine)


def project_out_kernel(mine_ref, other_ref, weight_ref, *outs):
    half = mine_ref.shape[1]
    over_last = (((1,), (1,)), ((), ()))
    for by, out_ref in enumerate(outs):
        result = lax.dot_general(
            mine_ref[...], weight_ref[by, :, :half], over_last, preferred_element_type=jnp.float32
        ) + lax.dot_general(
            other_ref[...], weight_ref[by, :, half:], over_last, preferred_element_type=jnp.float32
        )
        out_ref[...] = result.astype(out_ref.dtype)


def project_out(mine, other, weight):
    rows, half = mine.shape
    pieces, depth, _ = weight.shape
    shape = jax.ShapeDtypeStruct((rows, depth), jnp.bfloat16)
    whole = pl.BlockSpec(memory_space=pltpu.VMEM)
    return pl.pallas_call(
        project_out_kernel,
        out_shape=[shape] * pieces,
        in_specs=[whole] * 3,
        out_specs=[whole] * pieces,
        cost_estimate=pl.CostEstimate(
            flops=2 * rows * weight.size,
            bytes_accessed=2 * weight.size + 2 * rows * depth * pieces,
            transcendentals=0,
        ),
        compiler_params=pltpu.CompilerParams(vmem_limit_bytes=48 << 20),
        name="project_out",
    )(mine, other, weight)


def joined_kernel(place, first_ref, first_other_ref, second_ref, second_other_ref, out_ref):
    runs = first_ref.shape[1] // lane

    def write(even_ref, odd_ref):
        for run in range(runs):
            here = slice(run * lane, (run + 1) * lane)
            out_ref[:, 2 * run * lane : (2 * run + 1) * lane] = even_ref[:, here]
            out_ref[:, (2 * run + 1) * lane : (2 * run + 2) * lane] = odd_ref[:, here]

    @pl.when(place[0] == 0)
    def _():
        write(first_ref, first_other_ref)

    @pl.when(place[0] != 0)
    def _():
        write(second_other_ref, second_ref)


def joined(place, first, first_other, second, second_other):
    whole = pl.BlockSpec(memory_space=pltpu.VMEM)
    return pl.pallas_call(
        joined_kernel,
        out_shape=jax.ShapeDtypeStruct((first.shape[0], 2 * first.shape[1]), first.dtype),
        in_specs=[pl.BlockSpec(memory_space=pltpu.SMEM)] + [whole] * 4,
        out_specs=whole,
        compiler_params=pltpu.CompilerParams(vmem_limit_bytes=8 << 20),
        name="joined",
    )(place, first, first_other, second, second_other)


def local(
    patches,
    merge_gain,
    merge_first,
    merge_second,
    text_embeds,
    positions,
    segments,
    norm_gain,
    query_weight,
    keyval_weight,
    out_weight,
):
    count = patches.shape[0]
    width = merge_gain.shape[0]
    blocks, rows_here, slice_width = text_embeds.shape
    seq_len = segments.shape[0]
    block_len = seq_len // blocks
    section_index = lax.axis_index("section")
    cycle_index = lax.axis_index("blk")
    model_index = lax.axis_index("mp")
    n_mp = lax.axis_size("mp")
    n_blk = lax.axis_size("blk")
    first_core = section_index == 0
    head_size = keyval_weight.shape[4]
    rows = blocks * rows_here
    layers = 2

    query_own = query_weight[0]
    keyval_own = keyval_weight[0].reshape(keyval_weight.shape[1], 2 * head_size)
    out_own = out_weight[0]
    heads_half = query_own.shape[1] // 2
    weight_half = query_own.shape[0] // 2

    def packed(core):
        keep_rows = slice(core * weight_half, (core + 1) * weight_half)
        query_rows, keyval_rows = query_own[keep_rows], keyval_own[keep_rows]
        out_rows = out_own[:, keep_rows].T
        halves = (core, 1 - core)
        parts = [keyval_rows[:, half * head_size : (half + 1) * head_size] for half in halves]
        parts += [query_rows[:, half * heads_half : (half + 1) * heads_half] for half in halves]
        parts += [out_rows[:, half * heads_half : (half + 1) * heads_half] for half in halves]
        return jnp.concatenate(parts, axis=1)

    for_first, for_second = packed(0), packed(1)
    weight_keep = jnp.where(first_core, for_first, for_second)
    weight_other = swapped(jnp.where(first_core, for_second, for_first))
    keyval_width = 2 * head_size
    inner = merger_inner(patches, merge_gain, merge_first)
    weight_full = []
    for home in range(layers):
        if home > 0:
            inner, weight_keep, weight_other = lax.optimization_barrier(
                (inner, weight_keep, weight_other)
            )
        mine = jnp.where(section_index == home, weight_keep, weight_other)
        weight_full.append(lax.all_gather(mine, "blk", axis=0, tiled=True))
    gain_half = norm_gain[0].reshape(-1, 2, lane)
    gain_keep = jnp.where(first_core, gain_half[:, 0], gain_half[:, 1])
    gain_send = jnp.where(first_core, gain_half[:, 1], gain_half[:, 0])
    gain_other = swapped(gain_send)
    gain_layers = [
        jnp.where(first_core, gain_keep, gain_other).reshape(n_mp, 1, -1),
        jnp.where(first_core, gain_other, gain_keep).reshape(n_mp, 1, -1),
    ]

    place = jnp.stack([section_index, cycle_index, model_index]).astype(jnp.int32)
    own, *terms = merger_outer(place, inner, swapped(inner), merge_second, n_mp)
    total = own.astype(jnp.float32)
    for part in [moved(terms[by - 1], "mp", by) for by in (2, 1, 3)]:
        total = total + part.astype(jnp.float32)
    merged_terms = lax.all_to_all(
        total.astype(jnp.bfloat16).reshape(n_blk, -1, total.shape[1]), "blk", 0, 0, tiled=True
    )

    row_where = (
        jnp.arange(blocks)[:, None] * block_len
        + cycle_index * rows_here
        + jnp.arange(rows_here)[None, :]
    ).reshape(-1)
    starts = jnp.stack([jnp.sum(segments < 1), jnp.sum(segments < 2)])
    scalars = jnp.concatenate([starts, jnp.stack([cycle_index, section_index])]).astype(jnp.int32)
    is_visual = (positions[None, :] == row_where[:, None]).astype(jnp.bfloat16)
    has_visual = jnp.max(is_visual, axis=1, keepdims=True)
    text_rows = my_half(text_embeds.reshape(rows, slice_width), 1, section_index)
    cosine, sine = rope_tables(row_where, head_size)
    cosine = jnp.concatenate([cosine, cosine], axis=1)
    sine = jnp.concatenate([-sine, sine], axis=1)
    keyval_cosine = jnp.where(first_core, cosine, 1.0)
    keyval_sine = jnp.where(first_core, sine, 0.0)
    early = (scalars, is_visual, has_visual, text_rows, cosine, sine, keyval_cosine, keyval_sine)
    merged_terms, early = lax.optimization_barrier((merged_terms, early))
    scalars, is_visual, has_visual, text_rows, cosine, sine, keyval_cosine, keyval_sine = early
    merged_mine = jnp.sum(merged_terms.astype(jnp.float32), axis=0).astype(jnp.bfloat16)
    merged = spread(merged_mine).reshape(n_blk * merged_mine.shape[0], -1)
    picked = jnp.dot(is_visual, merged, preferred_element_type=jnp.float32).astype(jnp.bfloat16)
    state = jnp.where(has_visual > 0, picked, text_rows)


    results = []
    for layer_index in range(layers):
        parts = [state] + [moved(state, "mp", by) for by in (1, 2, 3)]
        gain = gain_layers[layer_index]
        weight = weight_full[layer_index]
        kept, sent = project_in(place, parts, gain, weight, 0, keyval_width, True)
        keyval_copies, shrink = keyval_rotate(
            kept, swapped(sent), keyval_cosine, keyval_sine, n_blk, n_mp * slice_width
        )
        keyval_copies, parts = lax.optimization_barrier((keyval_copies, parts))
        kept, sent, out_weight_here = project_in(
            place, parts, gain, weight, keyval_width, 2 * heads_half, False
        )
        gathered = lax.all_to_all(keyval_copies, "blk", 0, 0, tiled=True)
        gathered, kept, arrived = lax.optimization_barrier((gathered, kept, swapped(sent)))
        query = query_rotate(kept, arrived, shrink, cosine, sine)
        gathered = gathered.reshape(n_blk, blocks, rows_here, head_size)
        attended = attention(scalars, query, gathered, swapped(gathered))
        attended_other = swapped(attended)
        own, *terms = project_out(attended, attended_other, out_weight_here)
        arrived = [moved(terms[by - 1], "mp", by) for by in (2, 1, 3)]
        total = state.astype(jnp.float32) + own.astype(jnp.float32)
        for part in arrived:
            total = total + part.astype(jnp.float32)
        state = total.astype(jnp.bfloat16)
        results.append(state)

    first_other = swapped(results[0])
    second_other = swapped(results[1])
    hidden = joined(place, results[0], first_other, results[1], second_other)
    return hidden.reshape(1, blocks, rows_here, slice_width)


def solution(mesh):
    return jax.shard_map(
        local,
        mesh=mesh,
        in_specs=(
            P("section", None),
            P(),
            P(None, ("blk", "mp")),
            P(("blk", "mp"), None),
            P(None, "blk", "mp"),
            P(),
            P(),
            P("section", None),
            P("section", "blk", "mp"),
            P("section", "blk", "mp", None, None),
            P("section", "mp", "blk"),
        ),
        out_specs=P("section", None, "blk", "mp"),
        check_vma=False,
    )
```
